32 devices in a mesh: dp: 4 (over y, x), seq: 8 (over z, core).
Axes of the slice: x: 2, y: 2, z: 4, core: 2. Of those that a mesh axis runs over, the one named last changes fastest.
Arguments:
- inputs: bfloat16 [2, 4, 1024, 768], P(None, 'dp', 'seq'), may hold values from -6 to 6
- segments: int32 [2, 4, 1024], P(None, 'dp'), may hold values from 0 to 2, never falling along the last dimension, each value on 1 to 512 neighbouring positions
- w_query: float32 [768, 768], P(('dp', 'seq')), may hold values from -0.21875 to 0.21875
- b_query: float32 [768], P(('dp', 'seq')), may hold values from -3 to 3
- w_key: float32 [768, 768], P(('dp', 'seq')), may hold values from -0.21875 to 0.21875
- w_value: float32 [768, 768], P(('dp', 'seq')), may hold values from -0.21875 to 0.21875
- b_value: float32 [768], P(('dp', 'seq')), may hold values from -0.3125 to 0.3125
- w_output: float32 [768, 768], P(('dp', 'seq')), may hold values from -1.75 to 1.75
- b_output: float32 [768], P(('dp', 'seq')), may hold values from -1.75 to 1.75
- gain_first: float32 [768], P(('dp', 'seq')), may hold values from 0.5 to 1.5
- shift_first: float32 [768], P(('dp', 'seq')), may hold values from -1.75 to 1.75
- w_inner: float32 [768, 3072], P(('dp', 'seq')), may hold values from -0.21875 to 0.21875
- b_inner: float32 [3072], P(('dp', 'seq')), may hold values from -1.75 to 1.75
- w_outer: float32 [3072, 768], P(('dp', 'seq')), may hold values from -0.109375 to 0.109375
- b_outer: float32 [768], P(('dp', 'seq')), may hold values from -1.75 to 1.75
- gain_second: float32 [768], P(('dp', 'seq')), may hold values from 0.5 to 1.5
- shift_second: float32 [768], P(('dp', 'seq')), may hold values from -1.75 to 1.75
- cotangent: bfloat16 [2, 4, 1024, 768], P(None, 'dp', 'seq'), may hold values from -6 to 6
Outputs:
- outputs: bfloat16 [2, 4, 1024, 768], P(None, 'dp', 'seq')
- grad_inputs: bfloat16 [2, 4, 1024, 768], P(None, 'dp', 'seq')
- grad_w_query: float32 [768, 768], P(('dp', 'seq'))
- grad_b_query: float32 [768], P(('dp', 'seq'))
- grad_w_key: float32 [768, 768], P(('dp', 'seq'))
- grad_w_value: float32 [768, 768], P(('dp', 'seq'))
- grad_b_value: float32 [768], P(('dp', 'seq'))
- grad_w_output: float32 [768, 768], P(('dp', 'seq'))
- grad_b_output: float32 [768], P(('dp', 'seq'))
- grad_gain_first: float32 [768], P(('dp', 'seq'))
- grad_shift_first: float32 [768], P(('dp', 'seq'))
- grad_w_inner: float32 [768, 3072], P(('dp', 'seq'))
- grad_b_inner: float32 [3072], P(('dp', 'seq'))
- grad_w_outer: float32 [3072, 768], P(('dp', 'seq'))
- grad_b_outer: float32 [768], P(('dp', 'seq'))
- grad_gain_second: float32 [768], P(('dp', 'seq'))
- grad_shift_second: float32 [768], P(('dp', 'seq'))
The draws below stay inside these ranges and needn't reach their ends.
Inputs may be any that keep to these rules, and one draw needn't show every extreme that they name: `segments`: segment numbers never fall along a sequence; a document has 1 to 512 tokens and one has exactly 512.
All inputs are finite; a program needn't handle non-finite values.
Results may differ from the reference program's by a relative error of at most 0.017.
Values may be sent and summed in bfloat16 or wider, within the bound.
No kernel may reach another device: no remote copies, remote signals or barrier semaphores. Data moves between devices by JAX's collectives and lax.ppermute only.
A program may use at most 256 MiB of HBM per device.

```python
import math
import jax
import jax.numpy as jnp
import numpy as np
from jax import lax

D = 768
HEADS = 12
HEAD_DIM = 64
FF = 3072
MB = 2
SEQS = 4
LENGTH = 1024
DOCS = 3
DOC_MOST = 512


def steps_of(stream_key, extent, shards, smallest, high):
    level = 1.0
    for dim, blocks in shards:
        heights = jax.random.uniform(jax.random.fold_in(jax.random.fold_in(stream_key, 6), dim), (blocks,), jnp.float32, smallest / len(shards), high / len(shards))
        level = level * jnp.repeat(jnp.exp(heights), extent[dim] // blocks).reshape((-1,) + (1,) * (len(extent) - 1 - dim))
    return level


def profile(amount, total, limit, slope):
    weights = [(1 << 20) // math.isqrt(grade ** slope) + 1 for grade in range(2, amount + 1)]
    rest, holding = total - limit - (amount - 1), [1] * (amount - 1)
    while rest > 0:
        candidates = [i for i in range(amount - 1) if holding[i] < limit]
        mass, left = sum([weights[i] for i in candidates]), rest
        for i in candidates:
            more = min(limit - holding[i], max(1, left * weights[i] // mass), rest)
            holding[i] = holding[i] + more
            rest = rest - more
    return np.array([limit] + holding)


def ragged_sizes(stream_key, amount, total, bound, skew):
    if amount == 2:
        one = jax.random.randint(stream_key, (), max(1, total - bound), min(bound, total - 1) + 1)
        return jnp.stack([one, total - one])
    tallies = jnp.asarray(profile(amount, total, bound, skew), jnp.int32)
    twos = (amount - 1) // 2
    source_of, sink = tallies[1:1 + 2 * twos:2], tallies[2:2 + 2 * twos:2]
    margin = jnp.minimum(source_of - 1, bound - sink)
    shifted = jax.random.randint(jax.random.fold_in(stream_key, 1), (twos,), 0, 1 << 20) % (margin + 1)
    tallies = tallies.at[1:1 + 2 * twos:2].set(source_of - shifted).at[2:2 + 2 * twos:2].set(sink + shifted)
    return tallies[jax.random.permutation(jax.random.fold_in(stream_key, 2), amount)]


def normal_values(key, dims, deviation, bound, cuts=(), dtype=jnp.bfloat16):
    level = steps_of(key, dims, cuts, -0.22, 0.18) if cuts else 1.0
    values = jax.random.normal(key, dims, jnp.float32) * deviation * level
    return jnp.minimum(jnp.maximum(values, -bound), bound).astype(dtype)


def setup_inputs(seed: int = 0) -> dict:
    seeds = jax.random.split(jax.random.key(seed), 19)
    return {
        "inputs": normal_values(seeds[0], (MB, SEQS, LENGTH, D), 1.0, 6.0, ((1, 4), (2, 8))),
        "segments": jax.vmap(lambda own: jnp.searchsorted(jnp.cumsum(ragged_sizes(own, DOCS, LENGTH, DOC_MOST, 1)), jnp.arange(LENGTH), side="right"))(jax.random.split(seeds[1], MB * SEQS)).reshape((MB, SEQS, LENGTH)).astype(jnp.int32),
        "w_query": normal_values(seeds[2], (D, D), D ** -0.5, 0.21875, ((0, 32),), jnp.float32),
        "b_query": normal_values(seeds[3], (D,), 0.5, 3.0, ((0, 32),), jnp.float32),
        "w_key": normal_values(seeds[4], (D, D), D ** -0.5, 0.21875, ((0, 32),), jnp.float32),
        "w_value": normal_values(seeds[5], (D, D), D ** -0.5, 0.21875, ((0, 32),), jnp.float32),
        "b_value": normal_values(seeds[6], (D,), 0.05, 0.3125, ((0, 32),), jnp.float32),
        "w_output": normal_values(seeds[7], (D, D), (D // 64) ** -0.5, 1.75, ((0, 32),), jnp.float32),
        "b_output": normal_values(seeds[8], (D,), 0.3, 1.75, ((0, 32),), jnp.float32),
        "gain_first": jnp.clip(1.0 + 0.1 * jax.random.normal(seeds[9], (D,), jnp.float32), 0.5, 1.5),
        "shift_first": normal_values(seeds[10], (D,), 0.3, 1.75, ((0, 32),), jnp.float32),
        "w_inner": normal_values(seeds[11], (D, FF), D ** -0.5, 0.21875, ((0, 32),), jnp.float32),
        "b_inner": normal_values(seeds[12], (FF,), 0.3, 1.75, ((0, 32),), jnp.float32),
        "w_outer": normal_values(seeds[13], (FF, D), FF ** -0.5, 0.109375, ((0, 32),), jnp.float32),
        "b_outer": normal_values(seeds[14], (D,), 0.3, 1.75, ((0, 32),), jnp.float32),
        "gain_second": jnp.clip(1.0 + 0.1 * jax.random.normal(seeds[15], (D,), jnp.float32), 0.5, 1.5),
        "shift_second": normal_values(seeds[16], (D,), 0.3, 1.75, ((0, 32),), jnp.float32),
        "cotangent": normal_values(seeds[17], (MB, SEQS, LENGTH, D), 1.0, 6.0, ((1, 4), (2, 8))),
    }


@jax.custom_vjp
def low(v):
    return lax.optimization_barrier(v.astype(jnp.bfloat16)).astype(jnp.float32)

@jax.custom_vjp
def low_back(v):
    return v

def low_keep(v):
    return (low(v), None)

def low_pass(kept, grad):
    return (grad,)

def back_keep(v):
    return (v, None)

def back_low(kept, grad):
    return (low(grad),)
low.defvjp(low_keep, low_pass)
low_back.defvjp(back_keep, back_low)

def matmul(left, right):
    return jnp.dot(left, right, precision=lax.Precision.HIGHEST, preferred_element_type=jnp.float32)

def layer_norm(z, gain, shift):
    mean = lax.optimization_barrier(jnp.mean(z, axis=-1, keepdims=True))
    centered = z - mean
    rstd = lax.rsqrt(lax.optimization_barrier(jnp.mean(centered * centered, axis=-1, keepdims=True)) + 1e-05)
    return centered * rstd * gain + shift

def attention(queries, keys, values, seg_row):
    length = queries.shape[0]
    q_block = math.gcd(length, 512)
    blocks = length // q_block
    q_split = queries.reshape(blocks, q_block, HEADS, HEAD_DIM)
    seg_split = seg_row.reshape(blocks, q_block)
    keys_h = keys.reshape(length, HEADS, HEAD_DIM)
    values_h = values.reshape(length, HEADS, HEAD_DIM)

    def one_block(pair):
        q_part, seg_part = pair
        scores = jnp.einsum('qhd,khd->hqk', q_part, keys_h, precision=lax.Precision.HIGHEST) * 0.125
        scores = low_back(scores)
        same = (seg_part[:, None] == seg_row[None, :])[None]
        scores = jnp.where(same, scores, -1e+30)
        top = lax.optimization_barrier(jnp.max(scores, axis=-1, keepdims=True))
        lse = top + jnp.log(lax.optimization_barrier(jnp.sum(jnp.exp(scores - top), axis=-1, keepdims=True)))
        probs = low(jnp.exp(scores - lse))
        mixed = jnp.einsum('hqk,khd->qhd', probs, values_h, precision=lax.Precision.HIGHEST)
        return mixed.reshape(q_block, HEADS * HEAD_DIM)
    return lax.map(jax.checkpoint(one_block), (q_split, seg_split)).reshape(length, HEADS * HEAD_DIM)

def one_sequence(params, tokens, seg_row):
    wq, bq, wk, wv, bv, wo, bo, g1, s1, w1, b1, w2, b2, g2, s2 = params
    queries = low(low_back(matmul(tokens, wq) + bq))
    keys = low(low_back(matmul(tokens, wk)))
    values = low(low_back(matmul(tokens, wv) + bv))
    mixed = low(low_back(attention(queries, keys, values, seg_row)))
    branch = low_back(matmul(mixed, wo) + bo)
    hidden = layer_norm(tokens + branch, g1, s1)
    inner = low_back(matmul(low(hidden), w1) + b1)
    active = low(jax.nn.gelu(inner, approximate=False))
    outer = low_back(matmul(active, w2) + b2)
    return layer_norm(hidden + outer, g2, s2)

def reference(inputs, segments, w_query, b_query, w_key, w_value, b_value, w_output, b_output, gain_first, shift_first, w_inner, b_inner, w_outer, b_outer, gain_second, shift_second, cotangent):
    shape = inputs.shape
    params = (w_query, b_query, w_key, w_value, b_value, w_output, b_output, gain_first, shift_first, w_inner, b_inner, w_outer, b_outer, gain_second, shift_second)
    flat_in = inputs.astype(jnp.float32).reshape(shape[0] * shape[1], shape[2], shape[3])
    flat_seg = segments.reshape(shape[0] * shape[1], shape[2])
    flat_cot = cotangent.astype(jnp.float32).reshape(flat_in.shape)

    def forward(weights, tokens):
        rounded = tuple((low(item) for item in weights))

        def per_sequence(pair):
            return one_sequence(rounded, pair[0], pair[1])
        return lax.map(jax.checkpoint(per_sequence), (tokens, flat_seg))
    result, pull = jax.vjp(forward, params, flat_in)
    grads, grad_tokens = pull(flat_cot)
    return (result.astype(jnp.bfloat16).reshape(shape), grad_tokens.astype(jnp.bfloat16).reshape(shape), grads[0], grads[1], grads[2], grads[3], grads[4], grads[5], grads[6], grads[7], grads[8], grads[9], grads[10], grads[11], grads[12], grads[13], grads[14])
```

```python
import math

import jax
import jax.numpy as jnp
from jax import lax
from jax.experimental import pallas as pl
from jax.experimental.pallas import tpu as pltpu
from jax.sharding import PartitionSpec as P

HEADS = 12
HEAD_DIM = 64


def narrow(masters):
    return tuple((item.astype(jnp.bfloat16) for item in masters))


def fetch_forward(masters):
    lowered = narrow(masters)
    return (
        lax.all_gather(lowered[0], ("dp", "seq"), axis=0, tiled=True),
        lax.all_gather(lowered[1], ("dp", "seq"), axis=0, tiled=True),
        lax.all_gather(lowered[2], ("dp", "seq"), axis=0, tiled=True),
        lax.all_gather(lowered[3], ("dp", "seq"), axis=0, tiled=True),
        lax.all_gather(lowered[4], ("dp", "seq"), axis=0, tiled=True),
        lax.all_gather(lowered[5], ("dp", "seq"), axis=0, tiled=True),
        lax.all_gather(lowered[6], ("dp", "seq"), axis=0, tiled=True),
        lax.all_gather(lowered[7], ("dp", "seq"), axis=0, tiled=True),
        lax.all_gather(lowered[8], ("dp", "seq"), axis=0, tiled=True),
        lax.all_gather(lowered[9], ("dp", "seq"), axis=0, tiled=True),
        lax.all_gather(lowered[10], ("dp", "seq"), axis=0, tiled=True),
        lax.all_gather(lowered[11], ("dp", "seq"), axis=0, tiled=True),
        lax.all_gather(lowered[12], ("dp", "seq"), axis=0, tiled=True),
        lax.all_gather(lowered[13], ("dp", "seq"), axis=0, tiled=True),
        lax.all_gather(lowered[14], ("dp", "seq"), axis=0, tiled=True),
    )


def fetch_backward(masters):
    lowered = narrow(masters)
    return (
        lax.all_gather(lowered[0], ("dp", "seq"), axis=0, tiled=True),
        lax.all_gather(lowered[1], ("dp", "seq"), axis=0, tiled=True),
        lax.all_gather(lowered[2], ("dp", "seq"), axis=0, tiled=True),
        lax.all_gather(lowered[3], ("dp", "seq"), axis=0, tiled=True),
        lax.all_gather(lowered[4], ("dp", "seq"), axis=0, tiled=True),
        lax.all_gather(lowered[5], ("dp", "seq"), axis=0, tiled=True),
        lax.all_gather(lowered[6], ("dp", "seq"), axis=0, tiled=True),
        lax.all_gather(lowered[7], ("dp", "seq"), axis=0, tiled=True),
        lax.all_gather(lowered[8], ("dp", "seq"), axis=0, tiled=True),
        lax.all_gather(lowered[9], ("dp", "seq"), axis=0, tiled=True),
        lax.all_gather(lowered[10], ("dp", "seq"), axis=0, tiled=True),
        lax.all_gather(lowered[11], ("dp", "seq"), axis=0, tiled=True),
        lax.all_gather(lowered[12], ("dp", "seq"), axis=0, tiled=True),
        lax.all_gather(lowered[13], ("dp", "seq"), axis=0, tiled=True),
        lax.all_gather(lowered[14], ("dp", "seq"), axis=0, tiled=True),
    )


def sum_owners(terms):
    return (
        lax.psum_scatter(terms[0], ("dp", "seq"), scatter_dimension=0, tiled=True),
        lax.psum_scatter(terms[1], ("dp", "seq"), scatter_dimension=0, tiled=True),
        lax.psum_scatter(terms[2], ("dp", "seq"), scatter_dimension=0, tiled=True),
        lax.psum_scatter(terms[3], ("dp", "seq"), scatter_dimension=0, tiled=True),
        lax.psum_scatter(terms[4], ("dp", "seq"), scatter_dimension=0, tiled=True),
        lax.psum_scatter(terms[5], ("dp", "seq"), scatter_dimension=0, tiled=True),
        lax.psum_scatter(terms[6], ("dp", "seq"), scatter_dimension=0, tiled=True),
        lax.psum_scatter(terms[7], ("dp", "seq"), scatter_dimension=0, tiled=True),
        lax.psum_scatter(terms[8], ("dp", "seq"), scatter_dimension=0, tiled=True),
        lax.psum_scatter(terms[9], ("dp", "seq"), scatter_dimension=0, tiled=True),
        lax.psum_scatter(terms[10], ("dp", "seq"), scatter_dimension=0, tiled=True),
        lax.psum_scatter(terms[11], ("dp", "seq"), scatter_dimension=0, tiled=True),
        lax.psum_scatter(terms[12], ("dp", "seq"), scatter_dimension=0, tiled=True),
        lax.psum_scatter(terms[13], ("dp", "seq"), scatter_dimension=0, tiled=True),
        lax.psum_scatter(terms[14], ("dp", "seq"), scatter_dimension=0, tiled=True),
    )


def layer_norm(z, gain, shift):
    mean = jnp.mean(z, axis=-1, keepdims=True)
    centered = z - mean
    rstd = lax.rsqrt(jnp.mean(centered * centered, axis=-1, keepdims=True) + 1e-05)
    normed = centered * rstd
    return (normed * gain + shift, normed, rstd)


def norm_back(grad, normed, rstd, gain):
    scaled = grad * gain
    inner = (
        scaled
        - jnp.mean(scaled, axis=-1, keepdims=True)
        - normed * jnp.mean(scaled * normed, axis=-1, keepdims=True)
    )
    return (rstd * inner, jnp.sum(grad * normed, axis=0), jnp.sum(grad, axis=0))


def gelu_exact(value):
    return jax.nn.gelu(value, approximate=False)


def key_blocks(keys_all, values_all, seg_row):
    length = keys_all.shape[0]
    width = math.gcd(length, 1024)
    count = length // width
    keys_split = keys_all.reshape(count, width, HEADS, HEAD_DIM)
    values_split = values_all.reshape(count, width, HEADS, HEAD_DIM)
    return (keys_split, values_split, seg_row.reshape(count, width))


def block_scores(queries, keys, query_seg, key_seg):
    scores = jnp.einsum("qhd,khd->hqk", queries, keys, preferred_element_type=jnp.float32) * 0.125
    same = (query_seg[:, None] == key_seg[None, :])[None]
    return jnp.where(same, scores, -1e30)


def attend(queries, keys_all, values_all, seg_row, query_seg):
    rows = queries.shape[0]
    query_h = queries.reshape(rows, HEADS, HEAD_DIM)
    keys_split, values_split, seg_split = key_blocks(keys_all, values_all, seg_row)

    def first_pass(carry, block):
        top, total = carry
        keys, key_seg = block
        scores = block_scores(query_h, keys, query_seg, key_seg)
        new_top = jnp.maximum(top, jnp.max(scores, axis=-1))
        total = total * jnp.exp(top - new_top) + jnp.sum(
            jnp.exp(scores - new_top[..., None]), axis=-1
        )
        return ((new_top, total), None)

    start = (jnp.full((HEADS, rows), -1e30, jnp.float32), jnp.zeros((HEADS, rows), jnp.float32))
    (top, total), _ = lax.scan(first_pass, start, (keys_split, seg_split))
    lse = top + jnp.log(total)

    def second_pass(acc, block):
        keys, values, key_seg = block
        scores = block_scores(query_h, keys, query_seg, key_seg)
        probs = jnp.exp(scores - lse[..., None]).astype(jnp.bfloat16)
        return (
            acc + jnp.einsum("hqk,khd->qhd", probs, values, preferred_element_type=jnp.float32),
            None,
        )

    mixed, _ = lax.scan(
        second_pass,
        jnp.zeros((rows, HEADS, HEAD_DIM), jnp.float32),
        (keys_split, values_split, seg_split),
    )
    return (lse, mixed.reshape(rows, HEADS * HEAD_DIM))


def attend_back(queries, grad_mixed, lse, delta, keys_all, values_all, seg_row, query_seg):
    rows = queries.shape[0]
    query_h = queries.reshape(rows, HEADS, HEAD_DIM)
    grad_h = grad_mixed.reshape(rows, HEADS, HEAD_DIM)
    keys_split, values_split, seg_split = key_blocks(keys_all, values_all, seg_row)

    def step(grad_query, block):
        keys, values, key_seg = block
        scores = block_scores(query_h, keys, query_seg, key_seg)
        probs = jnp.exp(scores - lse[..., None])
        grad_probs = jnp.einsum("qhd,khd->hqk", grad_h, values, preferred_element_type=jnp.float32)
        grad_scores = (probs * (grad_probs - delta[..., None])).astype(jnp.bfloat16)
        grad_query = grad_query + jnp.einsum(
            "hqk,khd->qhd", grad_scores, keys, preferred_element_type=jnp.float32
        )
        grad_keys = (
            jnp.einsum("hqk,qhd->khd", grad_scores, query_h, preferred_element_type=jnp.float32)
            * 0.125
        )
        grad_values = jnp.einsum(
            "hqk,qhd->khd", probs.astype(jnp.bfloat16), grad_h, preferred_element_type=jnp.float32
        )
        width = keys.shape[0]
        joined = jnp.concatenate(
            [
                grad_keys.reshape(width, HEADS * HEAD_DIM),
                grad_values.reshape(width, HEADS * HEAD_DIM),
            ],
            axis=-1,
        )
        return (grad_query, joined)

    grad_query, joined = lax.scan(
        step, jnp.zeros((rows, HEADS, HEAD_DIM), jnp.float32), (keys_split, values_split, seg_split)
    )
    grad_query = (grad_query * 0.125).reshape(rows, HEADS * HEAD_DIM)
    return (grad_query, joined.reshape(keys_all.shape[0], 2 * HEADS * HEAD_DIM))


def outer_sum(left, right):
    return jnp.einsum("tf,tg->fg", left, right, preferred_element_type=jnp.float32)


def times_transposed(left, weight):
    return jnp.einsum("tg,fg->tf", left, weight, preferred_element_type=jnp.float32)


def column_sum(value):
    return jnp.sum(value.astype(jnp.float32), axis=0)


def per_device(
    inputs,
    segments,
    w_query,
    b_query,
    w_key,
    w_value,
    b_value,
    w_output,
    b_output,
    gain_first,
    shift_first,
    w_inner,
    b_inner,
    w_outer,
    b_outer,
    gain_second,
    shift_second,
    cotangent,
):
    masters = (
        w_query,
        b_query,
        w_key,
        w_value,
        b_value,
        w_output,
        b_output,
        gain_first,
        shift_first,
        w_inner,
        b_inner,
        w_outer,
        b_outer,
        gain_second,
        shift_second,
    )
    rows = inputs.shape[2]
    offset = lax.axis_index("seq") * rows
    results = []
    grad_rows = []
    totals = None
    for micro in range(inputs.shape[0]):
        tokens = inputs[micro, 0]
        seg_row = segments[micro, 0]
        query_seg = lax.dynamic_slice_in_dim(seg_row, offset, rows)
        full = fetch_forward(masters)
        wq, bq, wk, wv, bv, wo, bo, g1, s1, w1, b1, w2, b2, g2, s2 = full
        g1f, s1f, g2f, s2f = (
            g1.astype(jnp.float32),
            s1.astype(jnp.float32),
            g2.astype(jnp.float32),
            s2.astype(jnp.float32),
        )
        queries = (
            jnp.dot(tokens, wq, preferred_element_type=jnp.float32) + bq.astype(jnp.float32)
        ).astype(jnp.bfloat16)
        keys = jnp.dot(tokens, wk, preferred_element_type=jnp.float32).astype(jnp.bfloat16)
        values = (
            jnp.dot(tokens, wv, preferred_element_type=jnp.float32) + bv.astype(jnp.float32)
        ).astype(jnp.bfloat16)
        keys_all, values_all = (
            lax.all_gather(keys, "seq", axis=0, tiled=True),
            lax.all_gather(values, "seq", axis=0, tiled=True),
        )
        lse, mixed = attend(queries, keys_all, values_all, seg_row, query_seg)
        mixed_low = mixed.astype(jnp.bfloat16)
        branch = jnp.dot(mixed_low, wo, preferred_element_type=jnp.float32) + bo.astype(jnp.float32)
        hidden, normed_first, rstd_first = layer_norm(tokens.astype(jnp.float32) + branch, g1f, s1f)
        hidden_low = hidden.astype(jnp.bfloat16)
        inner = jnp.dot(hidden_low, w1, preferred_element_type=jnp.float32) + b1.astype(jnp.float32)
        active, gelu_pull = jax.vjp(gelu_exact, inner)
        active_low = active.astype(jnp.bfloat16)
        outer = jnp.dot(active_low, w2, preferred_element_type=jnp.float32) + b2.astype(jnp.float32)
        result, normed_second, rstd_second = layer_norm(hidden + outer, g2f, s2f)
        results.append(result.astype(jnp.bfloat16))
        wq, bq, wk, wv, bv, wo, bo, g1, s1, w1, b1, w2, b2, g2, s2 = fetch_backward(masters)
        keys_all, values_all = (
            lax.all_gather(keys, "seq", axis=0, tiled=True),
            lax.all_gather(values, "seq", axis=0, tiled=True),
        )
        grad_out = cotangent[micro, 0].astype(jnp.float32)
        grad_z2, grad_g2, grad_s2 = norm_back(grad_out, normed_second, rstd_second, g2f)
        grad_outer = grad_z2.astype(jnp.bfloat16)
        grad_w2 = outer_sum(active_low, grad_outer)
        grad_b2 = column_sum(grad_outer)
        grad_active = times_transposed(grad_outer, w2)
        grad_inner = gelu_pull(grad_active)[0].astype(jnp.bfloat16)
        grad_w1 = outer_sum(hidden_low, grad_inner)
        grad_b1 = column_sum(grad_inner)
        grad_hidden = times_transposed(grad_inner, w1) + grad_z2
        grad_z1, grad_g1, grad_s1 = norm_back(grad_hidden, normed_first, rstd_first, g1f)
        grad_branch = grad_z1.astype(jnp.bfloat16)
        grad_wo = outer_sum(mixed_low, grad_branch)
        grad_bo = column_sum(grad_branch)
        grad_mixed = times_transposed(grad_branch, wo).astype(jnp.bfloat16)
        delta = jnp.sum(
            (grad_mixed.astype(jnp.float32) * mixed).reshape(rows, HEADS, HEAD_DIM), axis=-1
        ).T
        grad_query, joined = attend_back(
            queries, grad_mixed, lse, delta, keys_all, values_all, seg_row, query_seg
        )
        summed = lax.psum_scatter(
            joined.astype(jnp.bfloat16), "seq", scatter_dimension=0, tiled=True
        ).astype(jnp.float32)
        width = summed.shape[1] // 2
        grad_keys = summed[:, :width].astype(jnp.bfloat16)
        grad_values = summed[:, width:].astype(jnp.bfloat16)
        grad_query = grad_query.astype(jnp.bfloat16)
        grad_wq = outer_sum(tokens, grad_query)
        grad_wk = outer_sum(tokens, grad_keys)
        grad_wv = outer_sum(tokens, grad_values)
        grad_bq = column_sum(grad_query)
        grad_bv = column_sum(grad_values)
        grad_tokens = (
            times_transposed(grad_query, wq)
            + times_transposed(grad_keys, wk)
            + times_transposed(grad_values, wv)
            + grad_z1
        )
        grad_rows.append(grad_tokens.astype(jnp.bfloat16))
        terms = (
            grad_wq,
            grad_bq,
            grad_wk,
            grad_wv,
            grad_bv,
            grad_wo,
            grad_bo,
            grad_g1,
            grad_s1,
            grad_w1,
            grad_b1,
            grad_w2,
            grad_b2,
            grad_g2,
            grad_s2,
        )
        totals = terms if totals is None else tuple((old + new for old, new in zip(totals, terms)))
    owned = sum_owners(totals)
    outputs = jnp.stack(results)[:, None]
    grad_inputs = jnp.stack(grad_rows)[:, None]
    return (
        outputs,
        grad_inputs,
        owned[0],
        owned[1],
        owned[2],
        owned[3],
        owned[4],
        owned[5],
        owned[6],
        owned[7],
        owned[8],
        owned[9],
        owned[10],
        owned[11],
        owned[12],
        owned[13],
        owned[14],
    )


BOTH = ("dp", "seq")
CHIPS = 16
BAND = 128
F32 = jnp.float32
BF16 = jnp.bfloat16
IN_VMEM = pl.BlockSpec(memory_space=pltpu.VMEM)
IN_PLACE = pl.BlockSpec(memory_space=pl.ANY)


def pairs(dp_bits, seq_bits, keep=lambda dp, seq: True):
    return [
        (dp * 8 + seq, (dp ^ dp_bits) * 8 + (seq ^ seq_bits))
        for dp in range(4)
        for seq in range(8)
        if keep(dp, seq)
    ]


CORE, Z1, Z2, Z3 = pairs(0, 1), pairs(0, 2), pairs(0, 4), pairs(0, 6)
Z3_INNER = pairs(0, 6, lambda dp, seq: seq // 2 in (1, 2))
X, Y = pairs(1, 0), pairs(2, 0)


def send(value, route):
    return lax.ppermute(value, BOTH, route)


def after(value, *events):
    return lax.optimization_barrier((value, *events))[0]


def my_chip():
    return lax.axis_index("dp") * 4 + lax.axis_index("seq") // 2


def my_core():
    return lax.axis_index("seq") % 2


def dot_nn(a, b):
    return lax.dot_general(a, b, (((1,), (0,)), ((), ())), preferred_element_type=F32)


def dot_nt(a, b):
    return lax.dot_general(a, b, (((1,), (1,)), ((), ())), preferred_element_type=F32)


def dot_tn(a, b):
    return lax.dot_general(a, b, (((0,), (0,)), ((), ())), preferred_element_type=F32)


def call(body, outs, n_in, in_specs=None, out_specs=None, scratch=(), grid=None, cost=None):
    kwargs = {} if grid is None else {"grid": grid}
    return pl.pallas_call(
        body,
        out_shape=[jax.ShapeDtypeStruct(s, d) for s, d in outs],
        in_specs=in_specs or [IN_VMEM] * n_in,
        out_specs=out_specs or [IN_VMEM] * len(outs),
        scratch_shapes=list(scratch),
        cost_estimate=pl.CostEstimate(flops=cost[0], bytes_accessed=cost[1], transcendentals=0)
        if cost
        else None,
        **kwargs,
    )


def gather_z(block):
    parts = [block, send(block, Z1), send(block, Z2), send(block, Z3)]
    half = block.shape[1] // 2
    return (
        jnp.concatenate([p[:, :half] for p in parts], axis=0),
        jnp.concatenate([p[:, half:] for p in parts], axis=0),
    )


def gather_xy(first, second):
    first_x, second_y = send(first, X), send(second, Y)
    first_y, second_x = send(first, Y), send(second, X)
    return (
        (first, first_x, first_y, send(first_x, Y)),
        (second, second_x, second_y, send(second_y, X)),
    )


def placed(groups, rows, target, cols, sems, base):
    me = my_chip()
    half = groups[0].shape[1]
    copies = []
    for g in range(4):
        for z in range(4):
            at = pl.multiple_of(((g * 4 + z) ^ me) * rows, 16)
            copies.append(
                pltpu.make_async_copy(
                    groups[g].at[pl.ds(z * rows, rows), :],
                    target.at[pl.ds(at, rows), pl.ds(cols, half)],
                    sems.at[base + g * 4 + z],
                )
            )
    return copies


def project_kernel(*refs):
    xs, first, second = refs[0:8], refs[8:12], refs[12:16]
    bq_ref, bv_ref = refs[16:18]
    q_ref, k_ref, v_ref, w_ref, x_ref, sems = refs[18:]
    loads = [pltpu.make_async_copy(xs[s], x_ref.at[s], sems.at[32 + s]) for s in range(8)]
    loads += placed(first, 48, w_ref, 0, sems, 0) + placed(second, 48, w_ref, 768, sems, 16)
    for c in loads:
        c.start()
    for c in loads:
        c.wait()
    bq, bv = bq_ref[...], bv_ref[...]

    def queries(s, _):
        x = x_ref[s].reshape(2 * BAND, 768)
        q = (dot_nn(x, w_ref[:, 0:384]) + bq).astype(BF16) * jnp.asarray(0.125, BF16)
        q_ref[s] = q.reshape(2, BAND, 384)
        return 0

    lax.fori_loop(0, 2, queries, 0)

    def slot(s, _):
        x = x_ref[s].reshape(2 * BAND, 768)
        k_ref[s] = dot_nn(x, w_ref[:, 384:768]).astype(BF16).reshape(2, BAND, 384)
        v_ref[s] = (dot_nn(x, w_ref[:, 768:1152]) + bv).astype(BF16).reshape(2, BAND, 384)
        return 0

    lax.fori_loop(0, 8, slot, 0)


def attend_kernel(q_ref, k_ref, v_ref, kseg_ref, qseg_ref, mix_ref, low_ref, lse_ref):
    mask = jnp.where(kseg_ref[0] == qseg_ref[0], 0.0, -1e30)
    q = q_ref[:, 0].reshape(2 * BAND, 384)
    for h in range(6):
        cols = slice(64 * h, 64 * h + 64)
        k = k_ref[:, 0, :, cols].reshape(8 * BAND, 64)
        v = v_ref[:, 0, :, cols].reshape(8 * BAND, 64)
        s = dot_nt(k, q[:, cols]) + mask
        top = jnp.max(s, axis=0, keepdims=True)
        e = jnp.exp(s - top)
        total = jnp.sum(e, axis=0, keepdims=True)
        mixed = dot_tn(v, e.astype(BF16)) * (1.0 / total)
        mix_ref[0, cols] = mixed
        low_ref[0, cols] = mixed.astype(BF16)
        lse_ref[0, h : h + 1] = top + jnp.log(total)


def norm(z):
    mean = jnp.mean(z, axis=-1, keepdims=True)
    centered = z - mean
    rstd = lax.rsqrt(jnp.mean(centered * centered, axis=-1, keepdims=True) + 1e-05)
    return (centered * rstd, rstd)


def norm_grad(grad, normed, rstd, gain):
    scaled = grad * gain
    return rstd * (
        scaled
        - jnp.mean(scaled, axis=-1, keepdims=True)
        - normed * jnp.mean(scaled * normed, axis=-1, keepdims=True)
    )


def forward_kernel(*refs):
    x_ref, own_ref, other_ref, vec_ref, b1_ref = refs[0:5]
    wa, wb, va, vb = refs[5:9], refs[9:13], refs[13:17], refs[17:21]
    n1_ref, r1_ref, low_ref, act_ref, slope_ref, f_ref, w1_ref, w2_ref, tok_ref, sems = refs[21:]
    loads1 = placed(wa, 48, w1_ref, 0, sems, 0) + placed(wb, 48, w1_ref, 768, sems, 16)
    loads2 = placed(va, 96, w2_ref, 0, sems, 32) + placed(vb, 96, w2_ref, 384, sems, 48)
    tokens = pltpu.make_async_copy(x_ref.at[pl.ds(0, 2)], tok_ref, sems.at[64])
    for c in [tokens] + loads1 + loads2:
        c.start()
    tokens.wait()
    bo, g1, s1 = vec_ref[2:3], vec_ref[3:4], vec_ref[4:5]

    def rows(i, _):
        r = pl.ds(i * 128, 128)
        o = pl.ds((i ^ 2) * 128, 128)
        z = tok_ref[i // 2, i % 2].astype(F32) + (own_ref[r].astype(F32) + other_ref[o].astype(F32)) + bo
        n, rstd = norm(z)
        n1_ref[r] = n
        r1_ref[r] = rstd
        low_ref[r] = (n * g1 + s1).astype(BF16)
        return 0

    lax.fori_loop(0, 4, rows, 0)
    for c in loads1:
        c.wait()

    def inner(j, _):
        cols = pl.ds(pl.multiple_of(j * 256, 256), 256)
        u = dot_nn(low_ref[...], w1_ref[:, cols]) + b1_ref[:, cols]
        cdf = 0.5 * (1.0 + lax.erf(u * (1.0 / math.sqrt(2.0))))
        act_ref[:, cols] = (u * cdf).astype(BF16)
        slope = cdf + u * (jnp.exp(-0.5 * u * u) * (1.0 / math.sqrt(2.0 * math.pi)))
        slope_ref[:, cols] = slope.astype(BF16)
        return 0

    lax.fori_loop(0, 6, inner, 0)
    for c in loads2:
        c.wait()

    def outer(j, _):
        cols = pl.ds(pl.multiple_of(j * 256, 256), 256)
        f_ref[:, cols] = dot_nn(act_ref[...], w2_ref[:, cols]).astype(BF16)
        return 0

    lax.fori_loop(0, 3, outer, 0)


def middle_kernel(
    n1_ref, own_ref, other_ref, cot_ref, pcot_ref, vec_ref, slope_ref, w1_ref, w2_ref,
    out_ref, df_ref, dz_ref, du_ref, dh_ref, sums_ref, db1_ref,
):
    g1, s1, b2, g2, s2 = (vec_ref[i : i + 1] for i in (3, 4, 5, 6, 7))

    def rows(i, which):
        ref, base = which
        r, o = pl.ds(base + i * 128, 128), pl.ds(256 - base + i * 128, 128)
        z = n1_ref[r] * g1 + s1 + (own_ref[r].astype(F32) + other_ref[o].astype(F32)) + b2
        n, rstd = norm(z)
        grad = ref[pl.ds(i * 128, 128)].astype(F32)
        dz = norm_grad(grad, n, rstd, g2)
        dz_ref[r] = dz
        df_ref[r] = dz.astype(BF16)
        return (r, n, grad, dz)

    sums_ref[...] = jnp.zeros_like(sums_ref)

    def own_rows(i, _):
        r, n, grad, dz = rows(i, (cot_ref, 0))
        out_ref[r] = (n * g2 + s2).astype(BF16)
        sums_ref[0:1] += jnp.sum(grad * n, axis=0, keepdims=True)
        sums_ref[1:2] += jnp.sum(grad, axis=0, keepdims=True)
        sums_ref[2:3] += jnp.sum(dz.astype(BF16).astype(F32), axis=0, keepdims=True)
        return 0

    def other_rows(i, _):
        rows(i, (pcot_ref, 256))
        return 0

    lax.fori_loop(0, 2, own_rows, 0)
    lax.fori_loop(0, 2, other_rows, 0)

    def hidden(j, _):
        cols = pl.ds(pl.multiple_of(j * 256, 256), 256)
        du = (dot_nt(df_ref[...], w2_ref[cols, :]) * slope_ref[:, cols].astype(F32)).astype(BF16)
        du_ref[:, cols] = du
        db1_ref[:, cols] = jnp.sum(du.astype(F32), axis=0, keepdims=True)
        return 0

    lax.fori_loop(0, 6, hidden, 0)

    def back(j, _):
        cols = pl.ds(pl.multiple_of(j * 256, 256), 256)
        dh_ref[:, cols] = dot_nt(du_ref[...], w1_ref[cols, :]).astype(BF16)
        return 0

    lax.fori_loop(0, 3, back, 0)


def first_kernel(dz_ref, own_ref, other_ref, n1_ref, r1_ref, vec_ref, wo_ref, dz1_ref, do_ref, half_ref, da_ref, sums_ref):
    g1 = vec_ref[3:4]
    core = my_core()
    sums_ref[...] = jnp.zeros_like(sums_ref)

    def rows(i):
        r, o = pl.ds(i * 128, 128), pl.ds((i ^ 2) * 128, 128)
        grad = dz_ref[r] + (own_ref[r].astype(F32) + other_ref[o].astype(F32))
        n = n1_ref[r]
        dz = norm_grad(grad, n, r1_ref[r], g1)
        low = dz.astype(BF16)
        do_ref[r] = low
        half_ref[r] = jnp.where(core == 0, low[:, :384], low[:, 384:])
        return (r, n, grad, dz, low)

    def own_rows(i, _):
        r, n, grad, dz, low = rows(i)
        dz1_ref[r] = dz
        sums_ref[0:1] += jnp.sum(grad * n, axis=0, keepdims=True)
        sums_ref[1:2] += jnp.sum(grad, axis=0, keepdims=True)
        sums_ref[2:3] += jnp.sum(low.astype(F32), axis=0, keepdims=True)
        return 0

    def other_rows(i, _):
        rows(i)
        return 0

    lax.fori_loop(0, 2, own_rows, 0)
    lax.fori_loop(2, 4, other_rows, 0)
    for m in range(2):
        for c in range(2):
            part = do_ref[pl.ds((c * 2 + m) * BAND, BAND), :]
            da_ref[m, :, c * BAND : (c + 1) * BAND] = dot_nt(wo_ref[...], part).astype(BF16)


def attend_back_kernel(q_ref, k_ref, v_ref, mix_ref, da_ref, lse_ref, kseg_ref, qseg_ref, dq_ref, dk_ref, dv_ref):
    mask = jnp.where(kseg_ref[0] == qseg_ref[0], 0.0, -1e30)
    q = q_ref[:, 0].reshape(2 * BAND, 384)
    for pair in range(3):
        dks, dvs, dqs = [], [], []
        for h in (2 * pair, 2 * pair + 1):
            cols = slice(64 * h, 64 * h + 64)
            k = k_ref[:, 0, :, cols].reshape(8 * BAND, 64)
            v = v_ref[:, 0, :, cols].reshape(8 * BAND, 64)
            qh, da = q[:, cols], da_ref[0, cols]
            p = jnp.exp(dot_nt(k, qh) + mask - lse_ref[0, h : h + 1])
            delta = jnp.sum(da.astype(F32) * mix_ref[0, cols], axis=0, keepdims=True)
            ds = (p * (dot_nn(v, da) - delta)).astype(BF16)
            dvs.append(dot_nt(p.astype(BF16), da))
            dks.append(dot_nn(ds, qh))
            dqs.append(dot_tn(k, ds))
        both = slice(128 * pair, 128 * pair + 128)
        dk_ref[:, 0, :, both] = jnp.concatenate(dks, axis=1).astype(BF16).reshape(8, BAND, 128)
        dv_ref[:, 0, :, both] = jnp.concatenate(dvs, axis=1).astype(BF16).reshape(8, BAND, 128)
        dq = jnp.transpose(jnp.concatenate(dqs, axis=0) * 0.125)
        dq_ref[:, 0, :, both] = dq.astype(BF16).reshape(2, BAND, 128)


def token_grad_kernel(dq_ref, dk_ref, dv_ref, w_ref, own_ref, send_ref):
    z = pl.program_id(0)
    for c, ref in enumerate((own_ref, send_ref)):
        dk = dk_ref[c].reshape(2 * BAND, 384)
        dv = dv_ref[c].reshape(2 * BAND, 384)
        ref[0] = (dot_nt(dk, w_ref[:, 384:768]) + dot_nt(dv, w_ref[:, 768:1152])).astype(BF16).reshape(2, BAND, 768)

        @pl.when(z == 0)
        def _():
            dq = dq_ref[c].reshape(2 * BAND, 384)
            dx = dot_nt(dk, w_ref[:, 384:768]) + dot_nt(dv, w_ref[:, 768:1152]) + dot_nt(dq, w_ref[:, 0:384])
            ref[0] = dx.astype(BF16).reshape(2, BAND, 768)


def place_rows(scratch, value, first_block, rows, cols):
    me = my_chip()
    for i in range(value.shape[0] // rows):
        at = pl.multiple_of(((first_block + i) ^ me) * rows, 16)
        scratch[pl.ds(at, rows), cols] = value[i * rows : (i + 1) * rows].astype(BF16)


def flush(scratch, outs, sems):
    rows, half = outs[0].shape
    copies = []
    for i, out in enumerate(outs):
        src = scratch.at[pl.ds((i % 4) * rows, rows), pl.ds((i // 4) * half, half)]
        copies.append(pltpu.make_async_copy(src, out, sems.at[i]))
    for c in copies:
        c.start()
    for c in copies:
        c.wait()


def outer_grad_kernel(act_ref, df_ref, *refs):
    outs, scratch, sems = refs[:8], refs[8], refs[9]

    def step(j, _):
        cols = pl.ds(pl.multiple_of(j * 384, 384), 384)
        place_rows(scratch, dot_tn(act_ref[:, cols], df_ref[...]), j * 4, 96, slice(0, 768))
        return 0

    lax.fori_loop(0, 4, step, 0)
    flush(scratch, outs, sems)


def inner_grad_kernel(low_ref, du_ref, *refs):
    outs, scratch, sems = refs[:8], refs[8], refs[9]

    def step(j, _):
        cols = pl.ds(pl.multiple_of(j * 384, 384), 384)
        place_rows(scratch, dot_tn(low_ref[:, cols], du_ref[...]), j * 8, 48, slice(0, 1536))
        return 0

    lax.fori_loop(0, 2, step, 0)
    flush(scratch, outs, sems)


def projection_grad_kernel(x_ref, dq_ref, dk_ref, dv_ref, mix0_ref, mix1_ref, half_ref, *refs):
    outs, sums_ref, scratch, sems = refs[:8], refs[8], refs[9], refs[10]
    dq = dq_ref[...].reshape(4 * BAND, 384)
    sums_ref[0:1] = jnp.sum(dq.astype(F32), axis=0, keepdims=True)

    def count(s, acc):
        return acc + jnp.sum(dv_ref[s].reshape(2 * BAND, 384).astype(F32), axis=0, keepdims=True)

    sums_ref[1:2] = lax.fori_loop(0, 8, count, jnp.zeros((1, 384), F32))
    half = half_ref[...].reshape(2, 2, BAND, 384)

    def step(j, _):
        cols = pl.ds(pl.multiple_of(j * 384, 384), 384)
        x = x_ref[:, :, :, cols].reshape(16 * BAND, 384)
        place_rows(scratch, dot_tn(x[: 4 * BAND], dq), j * 8, 48, slice(0, 384))
        place_rows(scratch, dot_tn(x, dk_ref[...].reshape(16 * BAND, 384)), j * 8, 48, slice(384, 768))
        place_rows(scratch, dot_tn(x, dv_ref[...].reshape(16 * BAND, 384)), j * 8, 48, slice(768, 1152))
        rows = pl.ds(pl.multiple_of(j * 384, 384), 384)
        dwo = dot_nn(mix0_ref[rows], half[:, 0].reshape(2 * BAND, 384))
        dwo += dot_nn(mix1_ref[rows], half[:, 1].reshape(2 * BAND, 384))
        place_rows(scratch, dwo, j * 8, 48, slice(1152, 1536))
        return 0

    lax.fori_loop(0, 2, step, 0)
    flush(scratch, outs, sems)


def add(*terms):
    total = terms[0].astype(F32)
    for t in terms[1:]:
        total = total + t.astype(F32)
    return total


def scatter_groups(groups, first_route, second_route, near, far, both):
    from_both = send(groups[both], first_route)
    from_far = send(groups[far], first_route)
    passed = add(groups[near], from_both).astype(BF16)
    return add(groups[0], from_far, send(passed, second_route)).astype(BF16)


def scatter_z(block):
    rows = block.shape[0] // 4
    part = [block[i * rows : (i + 1) * rows] for i in range(4)]
    return add(part[0], send(part[1], Z1), send(part[2], Z2), send(part[3], Z3))


def scatter_sum(outs):
    first = scatter_groups(outs[:4], Y, X, 1, 2, 3)
    second = scatter_groups(outs[4:], X, Y, 2, 1, 3)
    return (scatter_z(first), scatter_z(second))


def flip(values, axis, index, bits):
    for bit in range(bits):
        shape = values.shape
        n = shape[axis]
        split = shape[:axis] + (n >> (bit + 1), 2, 1 << bit) + shape[axis + 1 :]
        swapped = jnp.flip(values.reshape(split), axis + 1).reshape(shape)
        values = jnp.where((index >> bit) & 1 == 1, swapped, values)
    return values


def per_device_paired(
    inputs, segments, w_query, b_query, w_key, w_value, b_value, w_output, b_output, gain_first,
    shift_first, w_inner, b_inner, w_outer, b_outer, gain_second, shift_second, cotangent,
):
    seq = lax.axis_index("seq")
    me, core = my_chip(), my_core()
    even = core == 0

    four = jnp.stack([w_query, w_key, w_value, w_output], axis=1).astype(BF16).reshape(24, 4, 2, 384)
    mine, theirs = (
        jnp.where(even, four[:, :, 0], four[:, :, 1]).reshape(24, 1536),
        jnp.where(even, four[:, :, 1], four[:, :, 0]).reshape(24, 1536),
    )
    got = send(theirs, CORE)
    square = jnp.where(even, jnp.concatenate([mine, got], 0), jnp.concatenate([got, mine], 0))
    wide = w_inner.astype(BF16).reshape(24, CHIPS, 2, 96)
    mine, theirs = (
        jnp.where(even, wide[:, :, 0], wide[:, :, 1]).reshape(24, 1536),
        jnp.where(even, wide[:, :, 1], wide[:, :, 0]).reshape(24, 1536),
    )
    got = send(theirs, CORE)
    inner_rows = jnp.where(even, jnp.concatenate([mine, got], 0), jnp.concatenate([got, mine], 0))
    outer_rows = w_outer.astype(BF16)

    own_vec = jnp.concatenate(
        [b_query, b_value, b_output, gain_first, shift_first, b_outer, gain_second, shift_second, b_inner]
    ).astype(BF16)
    spot = (jnp.arange(CHIPS)[:, None, None] == me) & (jnp.arange(2)[None, :, None] == core)
    vecs = jnp.where(spot, own_vec[None, None, :], jnp.zeros((), BF16))
    for route in (CORE, Z1, Z2, X, Y):
        vecs = vecs + send(vecs, route)
    vecs = vecs.astype(F32)
    vec8 = vecs[:, :, :192].reshape(CHIPS, 2, 8, 24).transpose(2, 0, 1, 3).reshape(8, 768)
    b1 = jnp.where(even, vecs[:, 0, 192:], vecs[:, 1, 192:]).reshape(1, 1536)
    bq = jnp.where(even, vec8[0:1, :384], vec8[0:1, 384:])
    bv = jnp.where(even, vec8[1:2, :384], vec8[1:2, 384:])

    tokens, cot = inputs[:, 0], cotangent[:, 0]
    square_a, square_d = gather_z(square)
    tokens_z = after(tokens, square_a)
    near = [tokens, send(tokens_z, Z1), send(tokens_z, Z2), send(tokens_z, Z3_INNER)]
    slots = []
    for part in near:
        slots += [part, send(part, CORE)]
    other_cot = send(cot, CORE)
    square_a, square_d = gather_xy(square_a, square_d)
    inner_a, inner_d = gather_z(after(inner_rows, near[1], near[2], near[3]))
    inner_a, inner_d = gather_xy(after(inner_a, *square_a), after(inner_d, *square_d))
    outer_a, outer_d = gather_z(after(outer_rows, near[1], near[2], near[3]))
    outer_a, outer_d = gather_xy(after(outer_a, *inner_a), after(outer_d, *inner_d))

    segs = segments[:, 0]
    segs = flip(segs.reshape(2, 8, BAND), 1, seq, 3)
    kseg = segs.reshape(2, 8 * BAND, 1)
    qseg = segs[:, :2].reshape(2, 1, 2 * BAND)

    slot_shape, head_shape = (2, BAND, 768), (2, BAND, 384)
    q, k, v, w_abs, x_all = call(
        project_kernel,
        [((2, *head_shape), BF16), ((8, *head_shape), BF16), ((8, *head_shape), BF16), ((768, 1536), BF16), ((8, *slot_shape), BF16)],
        18,
        in_specs=[IN_PLACE] * 16 + [IN_VMEM] * 2,
        scratch=[pltpu.SemaphoreType.DMA((40,))],
        cost=(2_800_000_000, 16_000_000),
    )(*slots, *square_a, *square_d, bq, bv)

    wo_half = w_abs[:, 1152:]
    wo_mine = jnp.where(even, wo_half[:384], wo_half[384:])
    wo_got = send(jnp.where(even, wo_half[384:], wo_half[:384]), CORE)
    wo = jnp.where(even, jnp.concatenate([wo_mine, wo_got], 1), jnp.concatenate([wo_got, wo_mine], 1))

    q_spec = pl.BlockSpec((2, 1, BAND, 384), lambda m: (0, m, 0, 0))
    k_spec = pl.BlockSpec((8, 1, BAND, 384), lambda m: (0, m, 0, 0))
    seg_specs = [
        pl.BlockSpec((1, 8 * BAND, 1), lambda m: (m, 0, 0)),
        pl.BlockSpec((1, 1, 2 * BAND), lambda m: (m, 0, 0)),
    ]
    t_spec = pl.BlockSpec((1, 384, 2 * BAND), lambda m: (m, 0, 0))
    lse_spec = pl.BlockSpec((1, 8, 2 * BAND), lambda m: (m, 0, 0))
    mix, mix_low, lse = call(
        attend_kernel,
        [((2, 384, 256), F32), ((2, 384, 256), BF16), ((2, 8, 256), F32)],
        5,
        grid=(2,),
        in_specs=[q_spec, k_spec, k_spec, *seg_specs],
        out_specs=[t_spec, t_spec, lse_spec],
        cost=(1_600_000_000, 8_000_000),
    )(q, k, v, kseg, qseg)
    mix_other = send(mix_low, CORE)

    branch = [dot_tn(mix_low[m], wo).astype(BF16).reshape(2, 1, BAND, 768) for m in range(2)]
    branch = jnp.concatenate(branch, axis=1).reshape(2, 2 * BAND, 768)
    branch = branch.reshape(4 * BAND, 768)
    branch_other = send(branch, CORE)
    n1, r1, hid_low, act, slope, f_own, w1, w2 = call(
        forward_kernel,
        [((512, 768), F32), ((512, 1), F32), ((512, 768), BF16), ((512, 1536), BF16), ((512, 1536), BF16), ((512, 768), BF16), ((768, 1536), BF16), ((1536, 768), BF16)],
        21,
        in_specs=[IN_PLACE] + [IN_VMEM] * 4 + [IN_PLACE] * 16,
        scratch=[pltpu.VMEM((2, *slot_shape), BF16), pltpu.SemaphoreType.DMA((65,))],
        cost=(2_500_000_000, 16_000_000),
    )(x_all, branch, branch_other, vec8, b1, *inner_a, *inner_d, *outer_a, *outer_d)

    result, df, dz2, du, dh_own, sums2, db1 = call(
        middle_kernel,
        [((256, 768), BF16), ((512, 768), BF16), ((512, 768), F32), ((512, 1536), BF16), ((512, 768), BF16), ((8, 768), F32), ((1, 1536), F32)],
        9,
        cost=(2_500_000_000, 16_000_000),
    )(n1, f_own, send(f_own, CORE), cot.reshape(256, 768), other_cot.reshape(256, 768), vec8, slope, w1, w2)
    dh_other = send(dh_own, CORE)

    piece = [pltpu.SemaphoreType.DMA((8,))]
    outer_terms = call(
        outer_grad_kernel,
        [((384, 384), BF16)] * 8,
        2,
        out_specs=[IN_PLACE] * 8,
        scratch=[pltpu.VMEM((1536, 768), BF16)] + piece,
        cost=(1_200_000_000, 6_000_000),
    )(act, df)
    outer_sum_a, outer_sum_d = scatter_sum(outer_terms)
    inner_terms = call(
        inner_grad_kernel,
        [((192, 768), BF16)] * 8,
        2,
        out_specs=[IN_PLACE] * 8,
        scratch=[pltpu.VMEM((768, 1536), BF16)] + piece,
        cost=(1_200_000_000, 6_000_000),
    )(hid_low, du)
    inner_sum_a, inner_sum_d = scatter_sum(inner_terms)

    dz1, do, do_half, da, sums1 = call(
        first_kernel,
        [((256, 768), F32), ((512, 768), BF16), ((512, 384), BF16), ((2, 384, 256), BF16), ((8, 768), F32)],
        7,
        cost=(300_000_000, 10_000_000),
    )(dz2, dh_own, dh_other, n1, r1, vec8, wo)

    dq, dk, dv = call(
        attend_back_kernel,
        [((2, *head_shape), BF16), ((8, *head_shape), BF16), ((8, *head_shape), BF16)],
        8,
        grid=(2,),
        in_specs=[q_spec, k_spec, k_spec, t_spec, t_spec, lse_spec, *seg_specs],
        out_specs=[q_spec, k_spec, k_spec],
        cost=(4_000_000_000, 12_000_000),
    )(q, k, v, mix, da, lse, kseg, qseg)

    by_z = pl.BlockSpec((1, *slot_shape), lambda z: (z, 0, 0, 0))
    heads_by_z = pl.BlockSpec((2, *head_shape), lambda z: (z, 0, 0, 0))
    dx_own, dx_send = call(
        token_grad_kernel,
        [((4, *slot_shape), BF16)] * 2,
        4,
        grid=(4,),
        in_specs=[pl.BlockSpec((2, *head_shape), lambda z: (0, 0, 0, 0)), heads_by_z, heads_by_z, pl.BlockSpec((768, 1536), lambda z: (0, 0))],
        out_specs=[by_z, by_z],
        cost=(2_700_000_000, 10_000_000),
    )(dq, dk, dv, w_abs)
    dx_got = send(dx_send, CORE)
    dx = [add(dx_own[z], dx_got[z]) for z in range(4)]
    low_dx = [d.astype(BF16) for d in dx]
    grad_tokens = add(
        dx[0], dz1.reshape(slot_shape), send(low_dx[1], Z1), send(low_dx[2], Z2), send(low_dx[3], Z3_INNER)
    ).astype(BF16)

    mix_full = [
        jnp.where(even, jnp.concatenate([mix_low[m], jnp.roll(mix_other[m], BAND, 1)], 0), jnp.concatenate([jnp.roll(mix_other[m], BAND, 1), mix_low[m]], 0))
        for m in range(2)
    ]
    *square_terms, sums0 = call(
        projection_grad_kernel,
        [((192, 768), BF16)] * 8 + [((8, 384), F32)],
        7,
        out_specs=[IN_PLACE] * 8 + [IN_VMEM],
        scratch=[pltpu.VMEM((768, 1536), BF16)] + piece,
        cost=(3_300_000_000, 12_000_000),
    )(x_all, dq, dk, dv, mix_full[0], mix_full[1], do_half)
    square_sum_a, square_sum_d = scatter_sum(square_terms)

    zero = jnp.zeros((1, 384), F32)
    bq_g, bv_g = (
        jnp.where(even, jnp.concatenate([sums0[i : i + 1], zero], 1), jnp.concatenate([zero, sums0[i : i + 1]], 1))
        for i in (0, 1)
    )
    eight = jnp.concatenate(
        [bq_g, bv_g, sums1[2:3], sums1[0:1], sums1[1:2], sums2[2:3], sums2[0:1], sums2[1:2]], 0
    )
    eight = eight.reshape(8, CHIPS, 2, 24).transpose(1, 2, 0, 3).reshape(CHIPS, 2, 192)
    db1 = db1.reshape(CHIPS, 1, 96)
    db1 = jnp.where(jnp.arange(2)[None, :, None] == core, db1, 0.0)
    vec_grads = jnp.concatenate([eight, db1], axis=2)
    for route in (CORE, Z1, Z2, X, Y):
        vec_grads = vec_grads + send(vec_grads, route)
    own = jnp.sum(jnp.where(spot, vec_grads, 0.0), axis=(0, 1))

    def to_owner(first, second):
        value = jnp.concatenate([first, second], axis=1)
        keep = jnp.where(even, value[:24], value[24:])
        other = jnp.where(even, value[24:], value[:24]).astype(BF16)
        return (keep, send(other, CORE).astype(F32))

    keep, got = (v.reshape(24, 4, 384) for v in to_owner(square_sum_a, square_sum_d))
    squares = jnp.where(even, jnp.concatenate([keep, got], 2), jnp.concatenate([got, keep], 2))
    keep, got = (v.reshape(24, CHIPS, 1, 96) for v in to_owner(inner_sum_a, inner_sum_d))
    grad_inner = jnp.where(even, jnp.concatenate([keep, got], 2), jnp.concatenate([got, keep], 2)).reshape(24, 3072)
    grad_outer = jnp.concatenate([outer_sum_a, outer_sum_d], axis=1)
    small = [own[24 * i : 24 * i + 24] for i in range(8)]
    return (
        result.reshape(2, 1, BAND, 768), grad_tokens[:, None],
        squares[:, 0], small[0], squares[:, 1], squares[:, 2], small[1], squares[:, 3], small[2],
        small[3], small[4], grad_inner, own[192:], grad_outer, small[5], small[6], small[7],
    )


def solution(mesh):
    in_specs = (
        P(None, "dp", "seq", None),
        P(None, "dp", None),
        P(("dp", "seq"), None),
        P(("dp", "seq")),
        P(("dp", "seq"), None),
        P(("dp", "seq"), None),
        P(("dp", "seq")),
        P(("dp", "seq"), None),
        P(("dp", "seq")),
        P(("dp", "seq")),
        P(("dp", "seq")),
        P(("dp", "seq"), None),
        P(("dp", "seq")),
        P(("dp", "seq"), None),
        P(("dp", "seq")),
        P(("dp", "seq")),
        P(("dp", "seq")),
        P(None, "dp", "seq", None),
    )
    out_specs = (
        P(None, "dp", "seq", None),
        P(None, "dp", "seq", None),
        P(("dp", "seq"), None),
        P(("dp", "seq")),
        P(("dp", "seq"), None),
        P(("dp", "seq"), None),
        P(("dp", "seq")),
        P(("dp", "seq"), None),
        P(("dp", "seq")),
        P(("dp", "seq")),
        P(("dp", "seq")),
        P(("dp", "seq"), None),
        P(("dp", "seq")),
        P(("dp", "seq"), None),
        P(("dp", "seq")),
        P(("dp", "seq")),
        P(("dp", "seq")),
    )
    paired = (mesh.shape["dp"], mesh.shape["seq"]) == (4, 8)
    return jax.shard_map(
        per_device_paired if paired else per_device, mesh=mesh, in_specs=in_specs, out_specs=out_specs, check_vma=False
    )
```

```python
import math

import jax
import jax.numpy as jnp
from jax import lax
from jax.experimental import pallas as pl
from jax.experimental.pallas import tpu as pltpu
from jax.sharding import PartitionSpec as P

HEADS = 12
HEAD_DIM = 64


def narrow(masters):
    return tuple((item.astype(jnp.bfloat16) for item in masters))


def fetch_forward(masters):
    lowered = narrow(masters)
    return (
        lax.all_gather(lowered[0], ("dp", "seq"), axis=0, tiled=True),
        lax.all_gather(lowered[1], ("dp", "seq"), axis=0, tiled=True),
        lax.all_gather(lowered[2], ("dp", "seq"), axis=0, tiled=True),
        lax.all_gather(lowered[3], ("dp", "seq"), axis=0, tiled=True),
        lax.all_gather(lowered[4], ("dp", "seq"), axis=0, tiled=True),
        lax.all_gather(lowered[5], ("dp", "seq"), axis=0, tiled=True),
        lax.all_gather(lowered[6], ("dp", "seq"), axis=0, tiled=True),
        lax.all_gather(lowered[7], ("dp", "seq"), axis=0, tiled=True),
        lax.all_gather(lowered[8], ("dp", "seq"), axis=0, tiled=True),
        lax.all_gather(lowered[9], ("dp", "seq"), axis=0, tiled=True),
        lax.all_gather(lowered[10], ("dp", "seq"), axis=0, tiled=True),
        lax.all_gather(lowered[11], ("dp", "seq"), axis=0, tiled=True),
        lax.all_gather(lowered[12], ("dp", "seq"), axis=0, tiled=True),
        lax.all_gather(lowered[13], ("dp", "seq"), axis=0, tiled=True),
        lax.all_gather(lowered[14], ("dp", "seq"), axis=0, tiled=True),
    )


def fetch_backward(masters):
    lowered = narrow(masters)
    return (
        lax.all_gather(lowered[0], ("dp", "seq"), axis=0, tiled=True),
        lax.all_gather(lowered[1], ("dp", "seq"), axis=0, tiled=True),
        lax.all_gather(lowered[2], ("dp", "seq"), axis=0, tiled=True),
        lax.all_gather(lowered[3], ("dp", "seq"), axis=0, tiled=True),
        lax.all_gather(lowered[4], ("dp", "seq"), axis=0, tiled=True),
        lax.all_gather(lowered[5], ("dp", "seq"), axis=0, tiled=True),
        lax.all_gather(lowered[6], ("dp", "seq"), axis=0, tiled=True),
        lax.all_gather(lowered[7], ("dp", "seq"), axis=0, tiled=True),
        lax.all_gather(lowered[8], ("dp", "seq"), axis=0, tiled=True),
        lax.all_gather(lowered[9], ("dp", "seq"), axis=0, tiled=True),
        lax.all_gather(lowered[10], ("dp", "seq"), axis=0, tiled=True),
        lax.all_gather(lowered[11], ("dp", "seq"), axis=0, tiled=True),
        lax.all_gather(lowered[12], ("dp", "seq"), axis=0, tiled=True),
        lax.all_gather(lowered[13], ("dp", "seq"), axis=0, tiled=True),
        lax.all_gather(lowered[14], ("dp", "seq"), axis=0, tiled=True),
    )


def sum_owners(terms):
    return (
        lax.psum_scatter(terms[0], ("dp", "seq"), scatter_dimension=0, tiled=True),
        lax.psum_scatter(terms[1], ("dp", "seq"), scatter_dimension=0, tiled=True),
        lax.psum_scatter(terms[2], ("dp", "seq"), scatter_dimension=0, tiled=True),
        lax.psum_scatter(terms[3], ("dp", "seq"), scatter_dimension=0, tiled=True),
        lax.psum_scatter(terms[4], ("dp", "seq"), scatter_dimension=0, tiled=True),
        lax.psum_scatter(terms[5], ("dp", "seq"), scatter_dimension=0, tiled=True),
        lax.psum_scatter(terms[6], ("dp", "seq"), scatter_dimension=0, tiled=True),
        lax.psum_scatter(terms[7], ("dp", "seq"), scatter_dimension=0, tiled=True),
        lax.psum_scatter(terms[8], ("dp", "seq"), scatter_dimension=0, tiled=True),
        lax.psum_scatter(terms[9], ("dp", "seq"), scatter_dimension=0, tiled=True),
        lax.psum_scatter(terms[10], ("dp", "seq"), scatter_dimension=0, tiled=True),
        lax.psum_scatter(terms[11], ("dp", "seq"), scatter_dimension=0, tiled=True),
        lax.psum_scatter(terms[12], ("dp", "seq"), scatter_dimension=0, tiled=True),
        lax.psum_scatter(terms[13], ("dp", "seq"), scatter_dimension=0, tiled=True),
        lax.psum_scatter(terms[14], ("dp", "seq"), scatter_dimension=0, tiled=True),
    )


def layer_norm(z, gain, shift):
    mean = jnp.mean(z, axis=-1, keepdims=True)
    centered = z - mean
    rstd = lax.rsqrt(jnp.mean(centered * centered, axis=-1, keepdims=True) + 1e-05)
    normed = centered * rstd
    return (normed * gain + shift, normed, rstd)


def norm_back(grad, normed, rstd, gain):
    scaled = grad * gain
    inner = (
        scaled
        - jnp.mean(scaled, axis=-1, keepdims=True)
        - normed * jnp.mean(scaled * normed, axis=-1, keepdims=True)
    )
    return (rstd * inner, jnp.sum(grad * normed, axis=0), jnp.sum(grad, axis=0))


def gelu_exact(value):
    return jax.nn.gelu(value, approximate=False)


def key_blocks(keys_all, values_all, seg_row):
    length = keys_all.shape[0]
    width = math.gcd(length, 1024)
    count = length // width
    keys_split = keys_all.reshape(count, width, HEADS, HEAD_DIM)
    values_split = values_all.reshape(count, width, HEADS, HEAD_DIM)
    return (keys_split, values_split, seg_row.reshape(count, width))


def block_scores(queries, keys, query_seg, key_seg):
    scores = jnp.einsum("qhd,khd->hqk", queries, keys, preferred_element_type=jnp.float32) * 0.125
    same = (query_seg[:, None] == key_seg[None, :])[None]
    return jnp.where(same, scores, -1e30)


def attend(queries, keys_all, values_all, seg_row, query_seg):
    rows = queries.shape[0]
    query_h = queries.reshape(rows, HEADS, HEAD_DIM)
    keys_split, values_split, seg_split = key_blocks(keys_all, values_all, seg_row)

    def first_pass(carry, block):
        top, total = carry
        keys, key_seg = block
        scores = block_scores(query_h, keys, query_seg, key_seg)
        new_top = jnp.maximum(top, jnp.max(scores, axis=-1))
        total = total * jnp.exp(top - new_top) + jnp.sum(
            jnp.exp(scores - new_top[..., None]), axis=-1
        )
        return ((new_top, total), None)

    start = (jnp.full((HEADS, rows), -1e30, jnp.float32), jnp.zeros((HEADS, rows), jnp.float32))
    (top, total), _ = lax.scan(first_pass, start, (keys_split, seg_split))
    lse = top + jnp.log(total)

    def second_pass(acc, block):
        keys, values, key_seg = block
        scores = block_scores(query_h, keys, query_seg, key_seg)
        probs = jnp.exp(scores - lse[..., None]).astype(jnp.bfloat16)
        return (
            acc + jnp.einsum("hqk,khd->qhd", probs, values, preferred_element_type=jnp.float32),
            None,
        )

    mixed, _ = lax.scan(
        second_pass,
        jnp.zeros((rows, HEADS, HEAD_DIM), jnp.float32),
        (keys_split, values_split, seg_split),
    )
    return (lse, mixed.reshape(rows, HEADS * HEAD_DIM))


def attend_back(queries, grad_mixed, lse, delta, keys_all, values_all, seg_row, query_seg):
    rows = queries.shape[0]
    query_h = queries.reshape(rows, HEADS, HEAD_DIM)
    grad_h = grad_mixed.reshape(rows, HEADS, HEAD_DIM)
    keys_split, values_split, seg_split = key_blocks(keys_all, values_all, seg_row)

    def step(grad_query, block):
        keys, values, key_seg = block
        scores = block_scores(query_h, keys, query_seg, key_seg)
        probs = jnp.exp(scores - lse[..., None])
        grad_probs = jnp.einsum("qhd,khd->hqk", grad_h, values, preferred_element_type=jnp.float32)
        grad_scores = (probs * (grad_probs - delta[..., None])).astype(jnp.bfloat16)
        grad_query = grad_query + jnp.einsum(
            "hqk,khd->qhd", grad_scores, keys, preferred_element_type=jnp.float32
        )
        grad_keys = (
            jnp.einsum("hqk,qhd->khd", grad_scores, query_h, preferred_element_type=jnp.float32)
            * 0.125
        )
        grad_values = jnp.einsum(
            "hqk,qhd->khd", probs.astype(jnp.bfloat16), grad_h, preferred_element_type=jnp.float32
        )
        width = keys.shape[0]
        joined = jnp.concatenate(
            [
                grad_keys.reshape(width, HEADS * HEAD_DIM),
                grad_values.reshape(width, HEADS * HEAD_DIM),
            ],
            axis=-1,
        )
        return (grad_query, joined)

    grad_query, joined = lax.scan(
        step, jnp.zeros((rows, HEADS, HEAD_DIM), jnp.float32), (keys_split, values_split, seg_split)
    )
    grad_query = (grad_query * 0.125).reshape(rows, HEADS * HEAD_DIM)
    return (grad_query, joined.reshape(keys_all.shape[0], 2 * HEADS * HEAD_DIM))


def outer_sum(left, right):
    return jnp.einsum("tf,tg->fg", left, right, preferred_element_type=jnp.float32)


def times_transposed(left, weight):
    return jnp.einsum("tg,fg->tf", left, weight, preferred_element_type=jnp.float32)


def column_sum(value):
    return jnp.sum(value.astype(jnp.float32), axis=0)


def per_device(
    inputs,
    segments,
    w_query,
    b_query,
    w_key,
    w_value,
    b_value,
    w_output,
    b_output,
    gain_first,
    shift_first,
    w_inner,
    b_inner,
    w_outer,
    b_outer,
    gain_second,
    shift_second,
    cotangent,
):
    masters = (
        w_query,
        b_query,
        w_key,
        w_value,
        b_value,
        w_output,
        b_output,
        gain_first,
        shift_first,
        w_inner,
        b_inner,
        w_outer,
        b_outer,
        gain_second,
        shift_second,
    )
    rows = inputs.shape[2]
    offset = lax.axis_index("seq") * rows
    results = []
    grad_rows = []
    totals = None
    for micro in range(inputs.shape[0]):
        tokens = inputs[micro, 0]
        seg_row = segments[micro, 0]
        query_seg = lax.dynamic_slice_in_dim(seg_row, offset, rows)
        full = fetch_forward(masters)
        wq, bq, wk, wv, bv, wo, bo, g1, s1, w1, b1, w2, b2, g2, s2 = full
        g1f, s1f, g2f, s2f = (
            g1.astype(jnp.float32),
            s1.astype(jnp.float32),
            g2.astype(jnp.float32),
            s2.astype(jnp.float32),
        )
        queries = (
            jnp.dot(tokens, wq, preferred_element_type=jnp.float32) + bq.astype(jnp.float32)
        ).astype(jnp.bfloat16)
        keys = jnp.dot(tokens, wk, preferred_element_type=jnp.float32).astype(jnp.bfloat16)
        values = (
            jnp.dot(tokens, wv, preferred_element_type=jnp.float32) + bv.astype(jnp.float32)
        ).astype(jnp.bfloat16)
        keys_all, values_all = (
            lax.all_gather(keys, "seq", axis=0, tiled=True),
            lax.all_gather(values, "seq", axis=0, tiled=True),
        )
        lse, mixed = attend(queries, keys_all, values_all, seg_row, query_seg)
        mixed_low = mixed.astype(jnp.bfloat16)
        branch = jnp.dot(mixed_low, wo, preferred_element_type=jnp.float32) + bo.astype(jnp.float32)
        hidden, normed_first, rstd_first = layer_norm(tokens.astype(jnp.float32) + branch, g1f, s1f)
        hidden_low = hidden.astype(jnp.bfloat16)
        inner = jnp.dot(hidden_low, w1, preferred_element_type=jnp.float32) + b1.astype(jnp.float32)
        active, gelu_pull = jax.vjp(gelu_exact, inner)
        active_low = active.astype(jnp.bfloat16)
        outer = jnp.dot(active_low, w2, preferred_element_type=jnp.float32) + b2.astype(jnp.float32)
        result, normed_second, rstd_second = layer_norm(hidden + outer, g2f, s2f)
        results.append(result.astype(jnp.bfloat16))
        wq, bq, wk, wv, bv, wo, bo, g1, s1, w1, b1, w2, b2, g2, s2 = fetch_backward(masters)
        keys_all, values_all = (
            lax.all_gather(keys, "seq", axis=0, tiled=True),
            lax.all_gather(values, "seq", axis=0, tiled=True),
        )
        grad_out = cotangent[micro, 0].astype(jnp.float32)
        grad_z2, grad_g2, grad_s2 = norm_back(grad_out, normed_second, rstd_second, g2f)
        grad_outer = grad_z2.astype(jnp.bfloat16)
        grad_w2 = outer_sum(active_low, grad_outer)
        grad_b2 = column_sum(grad_outer)
        grad_active = times_transposed(grad_outer, w2)
        grad_inner = gelu_pull(grad_active)[0].astype(jnp.bfloat16)
        grad_w1 = outer_sum(hidden_low, grad_inner)
        grad_b1 = column_sum(grad_inner)
        grad_hidden = times_transposed(grad_inner, w1) + grad_z2
        grad_z1, grad_g1, grad_s1 = norm_back(grad_hidden, normed_first, rstd_first, g1f)
        grad_branch = grad_z1.astype(jnp.bfloat16)
        grad_wo = outer_sum(mixed_low, grad_branch)
        grad_bo = column_sum(grad_branch)
        grad_mixed = times_transposed(grad_branch, wo).astype(jnp.bfloat16)
        delta = jnp.sum(
            (grad_mixed.astype(jnp.float32) * mixed).reshape(rows, HEADS, HEAD_DIM), axis=-1
        ).T
        grad_query, joined = attend_back(
            queries, grad_mixed, lse, delta, keys_all, values_all, seg_row, query_seg
        )
        summed = lax.psum_scatter(
            joined.astype(jnp.bfloat16), "seq", scatter_dimension=0, tiled=True
        ).astype(jnp.float32)
        width = summed.shape[1] // 2
        grad_keys = summed[:, :width].astype(jnp.bfloat16)
        grad_values = summed[:, width:].astype(jnp.bfloat16)
        grad_query = grad_query.astype(jnp.bfloat16)
        grad_wq = outer_sum(tokens, grad_query)
        grad_wk = outer_sum(tokens, grad_keys)
        grad_wv = outer_sum(tokens, grad_values)
        grad_bq = column_sum(grad_query)
        grad_bv = column_sum(grad_values)
        grad_tokens = (
            times_transposed(grad_query, wq)
            + times_transposed(grad_keys, wk)
            + times_transposed(grad_values, wv)
            + grad_z1
        )
        grad_rows.append(grad_tokens.astype(jnp.bfloat16))
        terms = (
            grad_wq,
            grad_bq,
            grad_wk,
            grad_wv,
            grad_bv,
            grad_wo,
            grad_bo,
            grad_g1,
            grad_s1,
            grad_w1,
            grad_b1,
            grad_w2,
            grad_b2,
            grad_g2,
            grad_s2,
        )
        totals = terms if totals is None else tuple((old + new for old, new in zip(totals, terms)))
    owned = sum_owners(totals)
    outputs = jnp.stack(results)[:, None]
    grad_inputs = jnp.stack(grad_rows)[:, None]
    return (
        outputs,
        grad_inputs,
        owned[0],
        owned[1],
        owned[2],
        owned[3],
        owned[4],
        owned[5],
        owned[6],
        owned[7],
        owned[8],
        owned[9],
        owned[10],
        owned[11],
        owned[12],
        owned[13],
        owned[14],
    )


BOTH = ("dp", "seq")
CHIPS = 16
BAND = 128
F32 = jnp.float32
BF16 = jnp.bfloat16
IN_VMEM = pl.BlockSpec(memory_space=pltpu.VMEM)
IN_PLACE = pl.BlockSpec(memory_space=pl.ANY)


def pairs(dp_bits, seq_bits, keep=lambda dp, seq: True):
    return [
        (dp * 8 + seq, (dp ^ dp_bits) * 8 + (seq ^ seq_bits))
        for dp in range(4)
        for seq in range(8)
        if keep(dp, seq)
    ]


CORE, Z1, Z2, Z3 = pairs(0, 1), pairs(0, 2), pairs(0, 4), pairs(0, 6)
X, Y = pairs(1, 0), pairs(2, 0)
MIDDLE = pairs(0, 6, lambda dp, seq: seq // 2 in (1, 2))
OUTWARD = pairs(0, 2, lambda dp, seq: seq // 2 in (1, 2))


def send(value, route):
    return lax.ppermute(value, BOTH, route)


def after(value, *events):
    return lax.optimization_barrier((value, *events))[0]


def after_both(values, events):
    return lax.optimization_barrier((tuple(values), tuple(events)))[0]


def my_chip():
    return lax.axis_index("dp") * 4 + lax.axis_index("seq") // 2


def my_core():
    return lax.axis_index("seq") % 2


def dot_nn(a, b):
    return lax.dot_general(a, b, (((1,), (0,)), ((), ())), preferred_element_type=F32)


def dot_nt(a, b):
    return lax.dot_general(a, b, (((1,), (1,)), ((), ())), preferred_element_type=F32)


def dot_tn(a, b):
    return lax.dot_general(a, b, (((0,), (0,)), ((), ())), preferred_element_type=F32)


def call(body, outs, n_in, in_specs=None, out_specs=None, scratch=(), grid=None, cost=None):
    kwargs = {} if grid is None else {"grid": grid}
    return pl.pallas_call(
        body,
        out_shape=[jax.ShapeDtypeStruct(s, d) for s, d in outs],
        in_specs=in_specs or [IN_VMEM] * n_in,
        out_specs=out_specs or [IN_VMEM] * len(outs),
        scratch_shapes=list(scratch),
        cost_estimate=pl.CostEstimate(flops=cost[0], bytes_accessed=cost[1], transcendentals=0)
        if cost
        else None,
        **kwargs,
    )


def line(block):
    return [block, send(block, Z1), send(block, Z2), send(block, Z3)]


def across(parts, rows):
    return tuple(
        jnp.concatenate(
            [p[:48, c : c + 768] for p in parts] + [p[48:, c : c + 768] for p in parts if rows > 48], axis=0
        )
        for c in (0, 768)
    )


def near_hop(first, second):
    return (
        jnp.concatenate([first, send(first, X)], axis=0),
        jnp.concatenate([second, send(second, Y)], axis=0),
    )


def far_hop(first, second):
    return (first, send(first, Y), second, send(second, X))


def placed(groups, target, sems, base):
    me = my_chip()
    pitch = groups[0].shape[0] // 2
    copies = []
    for half in range(2):
        for far in range(2):
            for near in range(2):
                for z in range(4):
                    across_bits = far * 8 + near * 4 if half == 0 else near * 8 + far * 4
                    at = pl.multiple_of(((across_bits + z) ^ me) * 48, 16)
                    copies.append(
                        pltpu.make_async_copy(
                            groups[half * 2 + far].at[pl.ds(near * pitch + z * 48, 48), :],
                            target.at[pl.ds(at, 48), pl.ds(half * 768, 768)],
                            sems.at[base + len(copies)],
                        )
                    )
    return copies


def placed_hidden(both, w1, w2, sems):
    me = my_chip() % 4
    first, second = [], []
    for line_index in range(4):
        for z in range(4):
            b, i = line_index * 4 + (z ^ me), line_index * 4 + z
            rows = both.at[pl.ds(i * 48, 48)]
            at1, at2 = pl.multiple_of(b * 48, 16), pl.multiple_of(b * 96, 16)
            first.append(
                pltpu.make_async_copy(rows.at[:, pl.ds(0, 1536)], w1.at[pl.ds(at1, 48)], sems.at[i])
            )
            for part in range(2):
                second.append(
                    pltpu.make_async_copy(
                        rows.at[:, pl.ds(1536 + 768 * part, 768)],
                        w2.at[pl.ds(at2 + 48 * part, 48)],
                        sems.at[16 + 2 * i + part],
                    )
                )
    return (first, second)


def prepare_kernel(*refs):
    weights, vecs, outer_ref = refs[0:4], refs[4:13], refs[13]
    mine_ref, theirs_ref, rows_ref = refs[14:]
    even = my_core() == 0
    theirs_ref[24:32] = jnp.zeros((8, 1536), BF16)
    for i, ref in enumerate(weights):
        w, cols = ref[...].astype(BF16), slice(384 * i, 384 * i + 384)
        mine_ref[0:24, cols] = jnp.where(even, w[:, :384], w[:, 384:])
        theirs_ref[0:24, cols] = jnp.where(even, w[:, 384:], w[:, :384])
    pieces = []
    for ref in vecs:
        pieces += [ref[...], jnp.zeros((1, 128 - ref.shape[1]), F32)]
    row = jnp.concatenate(pieces + [jnp.zeros((1, 384), F32)], axis=1)
    row = jnp.where(lax.broadcasted_iota(jnp.int32, (8, 1536), 0) == 0, row, 0.0).astype(BF16)
    mine_ref[24:32] = row
    theirs_ref[24:32] = row
    rows_ref[:, 0:768] = outer_ref[0:48].astype(BF16)
    rows_ref[:, 768:1536] = outer_ref[48:96].astype(BF16)


def chip_rows_kernel(mine_ref, got_ref, out_ref):
    even = my_core() == 0
    mine, got = mine_ref[...].astype(F32), got_ref[...].astype(F32)
    out_ref[0:24] = jnp.where(even, mine[:24], got[:24]).astype(BF16)
    out_ref[24:48] = jnp.where(even, got[:24], mine[:24]).astype(BF16)
    first = jnp.where(even, mine[24:32], got[24:32])
    second = jnp.where(even, got[24:32], mine[24:32])
    row = lax.broadcasted_iota(jnp.int32, (8, 1536), 0)
    out_ref[48:56] = jnp.where(row == 1, second[0:1], jnp.where(row == 0, first[0:1], 0.0)).astype(BF16)


def owner_kernel(first_ref, second_ref, *refs):
    parts, (keep_ref, other_ref) = refs[:3], refs[3:]
    even = my_core() == 0
    for c, ref in ((0, first_ref), (768, second_ref)):
        cols = slice(c, c + 768)
        a, b, d = (p[:, cols].astype(F32) for p in parts)
        rows = ref[0:48].astype(F32) + a[:48] + b[:48] + d[:48]
        keep_ref[0:24, cols] = jnp.where(even, rows[:24], rows[24:])
        other_ref[0:24, cols] = jnp.where(even, rows[24:], rows[:24]).astype(BF16)
        vec = ref[192:200].astype(F32) + a[48:56] + b[48:56] + d[48:56]
        zero = jnp.zeros((7, 768), F32)
        keep_ref[24:32, cols] = jnp.concatenate([jnp.where(even, vec[0:1], vec[1:2]), zero], axis=0)
        other_ref[24:32, cols] = jnp.concatenate([jnp.where(even, vec[1:2], vec[0:1]), zero], axis=0).astype(BF16)


def result_kernel(keep_ref, got_ref, *refs):
    outs, vecs = refs[:4], refs[4:]
    even = my_core() == 0
    for i, ref in enumerate(outs):
        cols = slice(384 * i, 384 * i + 384)
        keep, got = keep_ref[0:24, cols], got_ref[0:24, cols].astype(F32)
        ref[:, 0:384] = jnp.where(even, keep, got)
        ref[:, 384:768] = jnp.where(even, got, keep)
    vec = keep_ref[24:25] + got_ref[24:32].astype(F32)[0:1]
    for i, ref in enumerate(vecs):
        ref[...] = vec[:, 128 * i : 128 * i + ref.shape[1]]


def project_kernel(*refs):
    xs, theirs, groups = refs[0:5], refs[5], refs[6:10]
    bq_ref, bv_ref = refs[10:12]
    q_ref, k_ref, v_ref, w_ref, x_ref, sems = refs[12:]
    slots = [*zip((0, 1, 2, 4, 6), xs), *((2 * z + 3, theirs.at[z]) for z in range(3))]
    loads = [pltpu.make_async_copy(ref, x_ref.at[s], sems.at[32 + s]) for s, ref in slots]
    loads += placed(groups, w_ref, sems, 0)
    for c in loads:
        c.start()
    for c in loads:
        c.wait()
    bq, bv = bq_ref[...], bv_ref[...]

    def queries(s, _):
        x = x_ref[s].reshape(2 * BAND, 768)
        q = (dot_nn(x, w_ref[:, 0:384]) + bq).astype(BF16) * jnp.asarray(0.125, BF16)
        q_ref[s] = q.reshape(2, BAND, 384)
        return 0

    lax.fori_loop(0, 2, queries, 0)

    def slot(s, _):
        x = x_ref[s].reshape(2 * BAND, 768)
        k_ref[s] = dot_nn(x, w_ref[:, 384:768]).astype(BF16).reshape(2, BAND, 384)
        v_ref[s] = (dot_nn(x, w_ref[:, 768:1152]) + bv).astype(BF16).reshape(2, BAND, 384)
        return 0

    lax.fori_loop(0, 8, slot, 0)


def attend_kernel(q_ref, k_ref, v_ref, kseg_ref, qseg_ref, mix_ref, low_ref, lse_ref):
    mask = jnp.where(kseg_ref[0] == qseg_ref[0], 0.0, -1e30)

    def pair(j, _):
        both = pl.ds(pl.multiple_of(128 * j, 128), 128)
        q2 = q_ref[:, 0, :, both].reshape(2 * BAND, 128)
        k2 = k_ref[:, 0, :, both].reshape(8 * BAND, 128)
        v2 = v_ref[:, 0, :, both].reshape(8 * BAND, 128)
        for h in range(2):
            cols = slice(64 * h, 64 * h + 64)
            s = dot_nt(k2[:, cols], q2[:, cols]) + mask
            top = jnp.max(s, axis=0, keepdims=True)
            e = jnp.exp(s - top)
            total = jnp.sum(e, axis=0, keepdims=True)
            mixed = dot_tn(v2[:, cols], e.astype(BF16)) * (1.0 / total)
            rows = pl.ds(pl.multiple_of(128 * j + 64 * h, 64), 64)
            mix_ref[0, rows] = mixed
            low_ref[0, rows] = mixed.astype(BF16)
            lse_ref[0, pl.ds(2 * j + h, 1)] = top + jnp.log(total)
        return 0

    lax.fori_loop(0, 3, pair, 0)


def norm(z):
    mean = jnp.mean(z, axis=-1, keepdims=True)
    centered = z - mean
    rstd = lax.rsqrt(jnp.mean(centered * centered, axis=-1, keepdims=True) + 1e-05)
    return (centered * rstd, rstd)


def norm_grad(grad, normed, rstd, gain):
    scaled = grad * gain
    return rstd * (
        scaled
        - jnp.mean(scaled, axis=-1, keepdims=True)
        - normed * jnp.mean(scaled * normed, axis=-1, keepdims=True)
    )


def forward_kernel(*refs):
    x_ref, own_ref, other_ref, vec_ref, b1_ref = refs[0:5]
    both = refs[5]
    n1_ref, r1_ref, low_ref, act_ref, slope_ref, f_ref, w1_ref, w2_ref, tok_ref, sems = refs[6:]
    loads1, loads2 = placed_hidden(both, w1_ref, w2_ref, sems)
    tokens = pltpu.make_async_copy(x_ref.at[pl.ds(0, 2)], tok_ref, sems.at[48])
    for c in [tokens] + loads1 + loads2:
        c.start()
    tokens.wait()
    bo, g1, s1 = vec_ref[2:3], vec_ref[3:4], vec_ref[4:5]

    def rows(i, _):
        r = pl.ds(i * 128, 128)
        o = pl.ds((i ^ 2) * 128, 128)
        z = tok_ref[i // 2, i % 2].astype(F32) + (own_ref[r].astype(F32) + other_ref[o].astype(F32)) + bo
        n, rstd = norm(z)
        n1_ref[r] = n
        r1_ref[r] = rstd
        low_ref[r] = (n * g1 + s1).astype(BF16)
        return 0

    lax.fori_loop(0, 4, rows, 0)
    for c in loads1:
        c.wait()

    def inner(j, _):
        cols = pl.ds(pl.multiple_of(j * 256, 256), 256)
        u = dot_nn(low_ref[...], w1_ref[:, cols]) + b1_ref[:, cols]
        cdf = 0.5 * (1.0 + lax.erf(u * (1.0 / math.sqrt(2.0))))
        act_ref[:, cols] = (u * cdf).astype(BF16)
        slope = cdf + u * (jnp.exp(-0.5 * u * u) * (1.0 / math.sqrt(2.0 * math.pi)))
        slope_ref[:, cols] = slope.astype(BF16)
        return 0

    lax.fori_loop(0, 6, inner, 0)
    for c in loads2:
        c.wait()

    def outer(j, _):
        cols = pl.ds(pl.multiple_of(j * 256, 256), 256)
        f_ref[:, cols] = dot_nn(act_ref[...], w2_ref[:, cols]).astype(BF16)
        return 0

    lax.fori_loop(0, 3, outer, 0)


def middle_kernel(
    n1_ref, own_ref, other_ref, cot_ref, pcot_ref, vec_ref, out_ref, df_ref, dz_ref, sums_ref,
):
    g1, s1, b2, g2, s2 = (vec_ref[i : i + 1] for i in (3, 4, 5, 6, 7))

    def rows(i, which):
        ref, base = which
        r, o = pl.ds(base + i * 128, 128), pl.ds(256 - base + i * 128, 128)
        z = n1_ref[r] * g1 + s1 + (own_ref[r].astype(F32) + other_ref[o].astype(F32)) + b2
        n, rstd = norm(z)
        grad = ref[pl.ds(i * 128, 128)].astype(F32)
        dz = norm_grad(grad, n, rstd, g2)
        dz_ref[r] = dz
        df_ref[r] = dz.astype(BF16)
        return (r, n, grad, dz)

    sums_ref[...] = jnp.zeros_like(sums_ref)

    def own_rows(i, _):
        r, n, grad, dz = rows(i, (cot_ref, 0))
        out_ref[r] = (n * g2 + s2).astype(BF16)
        sums_ref[0:1] += jnp.sum(grad * n, axis=0, keepdims=True)
        sums_ref[1:2] += jnp.sum(grad, axis=0, keepdims=True)
        sums_ref[2:3] += jnp.sum(dz.astype(BF16).astype(F32), axis=0, keepdims=True)
        return 0

    def other_rows(i, _):
        rows(i, (pcot_ref, 256))
        return 0

    lax.fori_loop(0, 2, own_rows, 0)
    lax.fori_loop(0, 2, other_rows, 0)


def hidden_kernel(df_ref, slope_ref, w1_ref, w2_ref, du_ref, dh_ref, db1_ref):
    def hidden(j, _):
        cols = pl.ds(pl.multiple_of(j * 256, 256), 256)
        du = (dot_nt(df_ref[...], w2_ref[cols, :]) * slope_ref[:, cols].astype(F32)).astype(BF16)
        du_ref[:, cols] = du
        db1_ref[:, cols] = jnp.sum(du.astype(F32), axis=0, keepdims=True)
        return 0

    lax.fori_loop(0, 6, hidden, 0)

    def back(j, _):
        cols = pl.ds(pl.multiple_of(j * 256, 256), 256)
        dh_ref[:, cols] = dot_nt(du_ref[...], w1_ref[cols, :]).astype(BF16)
        return 0

    lax.fori_loop(0, 3, back, 0)


def first_kernel(dz_ref, own_ref, other_ref, n1_ref, r1_ref, vec_ref, wo_ref, dz1_ref, do_ref, half_ref, da_ref, sums_ref):
    g1 = vec_ref[3:4]
    core = my_core()
    sums_ref[...] = jnp.zeros_like(sums_ref)

    def rows(i):
        r, o = pl.ds(i * 128, 128), pl.ds((i ^ 2) * 128, 128)
        grad = dz_ref[r] + (own_ref[r].astype(F32) + other_ref[o].astype(F32))
        n = n1_ref[r]
        dz = norm_grad(grad, n, r1_ref[r], g1)
        low = dz.astype(BF16)
        do_ref[r] = low
        half_ref[r] = jnp.where(core == 0, low[:, :384], low[:, 384:])
        return (r, n, grad, dz, low)

    def own_rows(i, _):
        r, n, grad, dz, low = rows(i)
        dz1_ref[r] = dz
        sums_ref[0:1] += jnp.sum(grad * n, axis=0, keepdims=True)
        sums_ref[1:2] += jnp.sum(grad, axis=0, keepdims=True)
        sums_ref[2:3] += jnp.sum(low.astype(F32), axis=0, keepdims=True)
        return 0

    def other_rows(i, _):
        rows(i)
        return 0

    lax.fori_loop(0, 2, own_rows, 0)
    lax.fori_loop(2, 4, other_rows, 0)
    for m in range(2):
        for c in range(2):
            part = do_ref[pl.ds((c * 2 + m) * BAND, BAND), :]
            da_ref[m, :, c * BAND : (c + 1) * BAND] = dot_nt(wo_ref[...], part).astype(BF16)


def attend_back_kernel(q_ref, k_ref, v_ref, mix_ref, da_ref, lse_ref, kseg_ref, qseg_ref, dq_ref, dk_ref, dv_ref):
    mask = jnp.where(kseg_ref[0] == qseg_ref[0], 0.0, -1e30)

    def pair(j, _):
        both = pl.ds(pl.multiple_of(128 * j, 128), 128)
        q2 = q_ref[:, 0, :, both].reshape(2 * BAND, 128)
        k2 = k_ref[:, 0, :, both].reshape(8 * BAND, 128)
        v2 = v_ref[:, 0, :, both].reshape(8 * BAND, 128)
        dks, dvs, dqs = [], [], []
        for h in range(2):
            cols = slice(64 * h, 64 * h + 64)
            rows = pl.ds(pl.multiple_of(128 * j + 64 * h, 64), 64)
            k, v, qh, da = k2[:, cols], v2[:, cols], q2[:, cols], da_ref[0, rows]
            p = jnp.exp(dot_nt(k, qh) + mask - lse_ref[0, pl.ds(2 * j + h, 1)])
            delta = jnp.sum(da.astype(F32) * mix_ref[0, rows], axis=0, keepdims=True)
            ds = (p * (dot_nn(v, da) - delta)).astype(BF16)
            dvs.append(dot_nt(p.astype(BF16), da))
            dks.append(dot_nn(ds, qh))
            dqs.append(dot_tn(k, ds))
        dk_ref[:, :, both] = jnp.concatenate(dks, axis=1).astype(BF16).reshape(8, BAND, 128)
        dv_ref[:, :, both] = jnp.concatenate(dvs, axis=1).astype(BF16).reshape(8, BAND, 128)
        dq = jnp.transpose(jnp.concatenate(dqs, axis=0) * 0.125)
        dq_ref[:, :, both] = dq.astype(BF16).reshape(2, BAND, 128)
        return 0

    lax.fori_loop(0, 3, pair, 0)


def token_grad_kernel(dq_ref, dk_ref, dv_ref, w_ref, own_ref, send_ref):
    def step(z, _):
        dk = dk_ref[pl.ds(2 * z, 2)].reshape(2 * BAND, 384)
        dv = dv_ref[pl.ds(2 * z, 2)].reshape(2 * BAND, 384)
        dx = dot_nt(dk, w_ref[:, 384:768]) + dot_nt(dv, w_ref[:, 768:1152])
        own_ref[z] = dx[:BAND].astype(BF16)
        send_ref[z] = dx[BAND:].astype(BF16)
        return 0

    lax.fori_loop(1, 4, step, 0)
    dx = dot_nt(dk_ref[0:2].reshape(2 * BAND, 384), w_ref[:, 384:768])
    dx += dot_nt(dv_ref[0:2].reshape(2 * BAND, 384), w_ref[:, 768:1152])
    dx += dot_nt(dq_ref[...].reshape(2 * BAND, 384), w_ref[:, 0:384])
    own_ref[0] = dx[:BAND].astype(BF16)
    send_ref[0] = dx[BAND:].astype(BF16)


def stored_at(block):
    p = block ^ my_chip()
    y, x, z = p // 8, (p // 4) % 2, p % 4
    return ((y, x * 4 + z), (x, y * 4 + z))


def place_rows(halves, block, first, second):
    for ref, (away, row), value in zip(halves, stored_at(block), (first, second)):
        ref[away, pl.ds(pl.multiple_of(row * 48, 16), 48)] = value


def flush(halves, outs, sems):
    copies = [
        pltpu.make_async_copy(halves[i // 2].at[i % 2], out.at[pl.ds(0, 384)], sems.at[i])
        for i, out in enumerate(outs)
    ]
    return copies


def finish(copies):
    for c in copies:
        c.start()
    for c in copies:
        c.wait()


def outer_grad_kernel(act_ref, df_ref, out_ref):
    me = my_chip() % 4

    def step(j, _):
        cols = pl.ds(pl.multiple_of(j * 384, 384), 384)
        value = dot_tn(act_ref[:, cols], df_ref[...]).astype(BF16)
        for i in range(4):
            rows = pl.ds(pl.multiple_of((j * 4 + (i ^ me)) * 48, 16), 48)
            out_ref[rows, 0:768] = value[96 * i : 96 * i + 48]
            out_ref[rows, 768:1536] = value[96 * i + 48 : 96 * i + 96]
        return 0

    lax.fori_loop(0, 4, step, 0)


def inner_grad_kernel(low_ref, du_ref, out_ref):
    me = my_chip() % 4

    def step(j, _):
        cols = pl.ds(pl.multiple_of(j * 384, 384), 384)
        value = dot_tn(low_ref[:, cols], du_ref[...]).astype(BF16)
        for i in range(8):
            rows = pl.ds(pl.multiple_of((j * 8 + (i ^ me)) * 48, 16), 48)
            out_ref[rows, :] = value[48 * i : 48 * i + 48]
        return 0

    lax.fori_loop(0, 2, step, 0)


def projection_grad_kernel(x_ref, *refs):
    dqs, dks, dvs, (mix0, mix1, other_ref, half_ref, vec_ref) = refs[0:2], refs[2:4], refs[4:6], refs[6:11]
    refs = refs[11:]
    outs, halves, dwo_ref, sems = refs[:4], refs[4:6], refs[6], refs[7]
    core = my_core()
    half = half_ref[...].reshape(2, 2, BAND, 384)
    own = [half[:, m].reshape(2 * BAND, 384) for m in range(2)]
    dwo = dot_nn(mix0[...], own[0]) + dot_nn(mix1[...], own[1])
    dwo_ref[pl.ds(pl.multiple_of(core * 384, 384), 384)] = dwo.astype(BF16)
    other = [jnp.concatenate([half[1, m], half[0, m]], axis=0) for m in range(2)]
    dwo = dot_nn(other_ref[0], other[0]) + dot_nn(other_ref[1], other[1])
    dwo_ref[pl.ds(pl.multiple_of((1 - core) * 384, 384), 384)] = dwo.astype(BF16)

    def step(j, _):
        cols = pl.ds(pl.multiple_of(j * 384, 384), 384)
        x = [x_ref[:, m, :, cols].reshape(8 * BAND, 384) for m in range(2)]

        def total(refs, count):
            terms = [dot_tn(x[m][: count * BAND], refs[m][...].reshape(count * BAND, 384)) for m in range(2)]
            return (terms[0] + terms[1]).astype(BF16)

        dwq, dwk, dwv = total(dqs, 2), total(dks, 8), total(dvs, 8)
        for i in range(8):
            rows = slice(48 * i, 48 * i + 48)
            dwo = dwo_ref[pl.ds(pl.multiple_of(j * 384 + 48 * i, 16), 48)]
            place_rows(
                halves,
                j * 8 + i,
                jnp.concatenate([dwq[rows], dwk[rows]], axis=1),
                jnp.concatenate([dwv[rows], dwo], axis=1),
            )
        return 0

    lax.fori_loop(0, 2, step, 0)
    copies = flush(halves, outs, sems)
    for i, out in enumerate(outs):
        copies.append(pltpu.make_async_copy(vec_ref.at[i], out.at[pl.ds(384, 64)], sems.at[4 + i]))
    finish(copies)


def add(*terms):
    total = terms[0].astype(F32)
    for t in terms[1:]:
        total = total + t.astype(F32)
    return total


def first_hop(terms):
    return (terms[0], send(terms[1], Y), terms[2], send(terms[3], X))


def halves_of(g, near, rows):
    return jnp.concatenate(
        [g[192 * near : 192 * near + 192]] + ([g[384 + 32 * near : 416 + 32 * near]] if rows > 48 else [])
    )


def near_terms(hop, rows):
    return tuple(
        add(halves_of(hop[i], 1, rows), halves_of(hop[i + 1], 1, rows)).astype(BF16) for i in (0, 2)
    )


def hop_terms(low):
    return (send(low[0], X), send(low[1], Y))


def far_terms(hop, got, rows):
    return tuple(
        add(halves_of(hop[i], 0, rows), halves_of(hop[i + 1], 0, rows), got[i // 2]).astype(BF16) for i in (0, 2)
    )


def along_line(blocks):
    return (blocks[0], send(blocks[1], Z1), send(blocks[2], Z2), send(blocks[3], Z3))


def line_parts(halves, rows):
    return along_line(
        [
            jnp.concatenate(
                [
                    jnp.concatenate(
                        [h[48 * z : 48 * z + 48]] + ([h[192 + 8 * z : 200 + 8 * z]] if rows > 48 else []), axis=0
                    )
                    for h in halves
                ],
                axis=1,
            )
            for z in range(4)
        ]
    )


def block_parts(block):
    return along_line([block[48 * z : 48 * z + 48] for z in range(4)])


def flip(values, axis, index, bits):
    for bit in range(bits):
        shape = values.shape
        n = shape[axis]
        split = shape[:axis] + (n >> (bit + 1), 2, 1 << bit) + shape[axis + 1 :]
        swapped = jnp.flip(values.reshape(split), axis + 1).reshape(shape)
        values = jnp.where((index >> bit) & 1 == 1, swapped, values)
    return values


def per_device_paired(
    inputs, segments, w_query, b_query, w_key, w_value, b_value, w_output, b_output, gain_first,
    shift_first, w_inner, b_inner, w_outer, b_outer, gain_second, shift_second, cotangent,
):
    seq = lax.axis_index("seq")
    me, core = my_chip(), my_core()
    even = core == 0

    def in_order(mine, got, axis):
        return jnp.where(even, jnp.concatenate([mine, got], axis), jnp.concatenate([got, mine], axis))

    lanes = [b_query, b_value, b_output, gain_first, shift_first, b_outer, gain_second, shift_second, b_inner]
    mine, theirs, outer_rows = call(
        prepare_kernel, [((32, 1536), BF16), ((32, 1536), BF16), ((48, 1536), BF16)], 14
    )(w_query, w_key, w_value, w_output, *(v.reshape(1, -1) for v in lanes), w_outer)
    (square,) = call(chip_rows_kernel, [((56, 1536), BF16)], 2)(mine, send(theirs, CORE))
    wide = w_inner.astype(BF16).reshape(24, CHIPS, 2, 96)
    mine, theirs = (
        jnp.where(even, wide[:, :, 0], wide[:, :, 1]).reshape(24, 1536),
        jnp.where(even, wide[:, :, 1], wide[:, :, 0]).reshape(24, 1536),
    )
    inner_rows = in_order(mine, send(theirs, CORE), 0)
    tokens, cot = inputs[:, 0], cotangent[:, 0]
    segs = segments[:, 0]
    segs = flip(segs.reshape(2, 8, BAND), 1, seq, 3)
    kseg = segs.reshape(2, 8 * BAND, 1)
    qseg = segs[:, :2].reshape(2, 1, 2 * BAND)

    other_tokens = send(tokens, CORE)
    hidden_rows = jnp.concatenate([inner_rows, outer_rows], axis=1)
    square, hidden_rows, other_tokens = after_both((square, hidden_rows, other_tokens), ())
    square = across(line(square), 56)
    hidden_rows, square = after_both((hidden_rows, square), ())
    hidden = line(hidden_rows)
    got = (send(square[0], X), send(square[1], Y))
    got, square = after_both((got, square), hidden[1:2])
    square = far_hop(*(jnp.concatenate(pair, axis=0) for pair in zip(square, got)))
    hidden, tokens = after_both((hidden, tokens), square)
    hidden = lax.all_gather(jnp.concatenate(hidden, axis=0), "dp", axis=0, tiled=True)
    beside, opposite = send(tokens, Z1), send(tokens, MIDDLE)
    square, beside, opposite = after_both((square, beside, opposite), ())
    outside = (seq // 2 == 0) | (seq // 2 == 3)
    second = jnp.where(outside, send(opposite, OUTWARD), send(beside, MIDDLE))
    theirs = send(jnp.stack([beside, second, opposite]), CORE)
    slots = [tokens, other_tokens, beside, second, opposite, theirs]

    places = jnp.arange(CHIPS)
    order = ((places[:, None] ^ me) == places[None, :]).astype(BF16)
    vecs = []
    for half, turn in ((square[:2], (0, 1, 2, 3)), (square[2:], (0, 2, 1, 3))):
        rows = [g[224 * near + 192 : 224 * near + 224].reshape(4, 8, 768)[:, :2] for g in half for near in (0, 1)]
        vecs.append(jnp.concatenate([rows[i] for i in turn], axis=0))
    vecs = jnp.concatenate(vecs, axis=2).reshape(CHIPS, 2 * 1536)
    vecs = dot_nn(order, vecs).reshape(CHIPS, 2, 12, 128)
    vec8 = vecs[:, :, :8, :24].transpose(2, 0, 1, 3).reshape(8, 768)
    b1 = jnp.where(even, vecs[:, 0, 8, :96], vecs[:, 1, 8, :96]).reshape(1, 1536)
    bq = jnp.where(even, vec8[0:1, :384], vec8[0:1, 384:])
    bv = jnp.where(even, vec8[1:2, :384], vec8[1:2, 384:])

    slot_shape, head_shape = (2, BAND, 768), (2, BAND, 384)
    q, k, v, w_abs, x_all = call(
        project_kernel,
        [((2, *head_shape), BF16), ((8, *head_shape), BF16), ((8, *head_shape), BF16), ((768, 1536), BF16), ((8, *slot_shape), BF16)],
        12,
        in_specs=[IN_PLACE] * 10 + [IN_VMEM] * 2,
        scratch=[pltpu.SemaphoreType.DMA((40,))],
        cost=(2_800_000_000, 16_000_000),
    )(*slots, *square, bq, bv)
    wo_half = w_abs[:, 1152:]
    wo_mine = jnp.where(even, wo_half[:384], wo_half[384:])
    wo_got = send(jnp.where(even, wo_half[384:], wo_half[:384]), CORE)
    wo = in_order(wo_mine, wo_got, 1)

    def attention_specs(m=None):
        micro = (lambda i: i) if m is None else (lambda i: m)
        q_spec = pl.BlockSpec((2, 1, BAND, 384), lambda i: (0, micro(i), 0, 0))
        k_spec = pl.BlockSpec((8, 1, BAND, 384), lambda i: (0, micro(i), 0, 0))
        t_spec = pl.BlockSpec((1, 384, 2 * BAND), lambda i: (micro(i), 0, 0))
        lse_spec = pl.BlockSpec((1, 8, 2 * BAND), lambda i: (micro(i), 0, 0))
        segs = [
            pl.BlockSpec((1, 8 * BAND, 1), lambda i: (micro(i), 0, 0)),
            pl.BlockSpec((1, 1, 2 * BAND), lambda i: (micro(i), 0, 0)),
        ]
        return ([q_spec, k_spec, k_spec], [t_spec, t_spec, lse_spec], segs)

    qkv_specs, mix_specs, seg_specs = attention_specs()
    other_cot = send(after(cot, q), CORE)

    mix, mix_low, lse = call(
        attend_kernel,
        [((2, 384, 256), F32), ((2, 384, 256), BF16), ((2, 8, 256), F32)],
        5,
        grid=(2,),
        in_specs=qkv_specs + seg_specs,
        out_specs=mix_specs,
        cost=(1_600_000_000, 8_000_000),
    )(q, k, v, kseg, qseg)
    branch = [dot_tn(mix_low[m], wo).astype(BF16).reshape(2, 1, BAND, 768) for m in range(2)]
    branch = jnp.concatenate(branch, axis=1).reshape(4 * BAND, 768)
    branch_other = send(branch, CORE)
    n1, r1, hid_low, act, slope, f_own, w1, w2 = call(
        forward_kernel,
        [((512, 768), F32), ((512, 1), F32), ((512, 768), BF16), ((512, 1536), BF16), ((512, 1536), BF16), ((512, 768), BF16), ((768, 1536), BF16), ((1536, 768), BF16)],
        6,
        in_specs=[IN_PLACE] + [IN_VMEM] * 4 + [IN_PLACE],
        scratch=[pltpu.VMEM((2, *slot_shape), BF16), pltpu.SemaphoreType.DMA((49,))],
        cost=(2_500_000_000, 16_000_000),
    )(x_all, branch, branch_other, vec8, b1, hidden)
    mix_other = send(after(mix_low, n1), CORE)
    result, df, dz2, sums2 = call(
        middle_kernel,
        [((256, 768), BF16), ((512, 768), BF16), ((512, 768), F32), ((8, 768), F32)],
        6,
        cost=(50_000_000, 8_000_000),
    )(n1, f_own, send(f_own, CORE), cot.reshape(256, 768), other_cot.reshape(256, 768), vec8)

    piece = [pltpu.VMEM((2, 384, 768), BF16)] * 2
    (outer_terms,) = call(outer_grad_kernel, [((768, 1536), BF16)], 2, cost=(1_200_000_000, 6_000_000))(act, df)
    outer_block = lax.psum_scatter(outer_terms, "dp", scatter_dimension=0, tiled=True)
    du, dh_own, db1 = call(
        hidden_kernel,
        [((512, 1536), BF16), ((512, 768), BF16), ((1, 1536), F32)],
        4,
        cost=(2_400_000_000, 9_000_000),
    )(after(df, outer_terms), slope, w1, w2)
    dh_other = send(dh_own, CORE)
    (inner_terms,) = call(inner_grad_kernel, [((768, 1536), BF16)], 2, cost=(1_200_000_000, 6_000_000))(hid_low, du)
    inner_block = lax.psum_scatter(inner_terms, "dp", scatter_dimension=0, tiled=True)
    dh_own = after(dh_own, inner_terms)
    dz1, do, do_half, da, sums1 = call(
        first_kernel,
        [((256, 768), F32), ((512, 768), BF16), ((512, 384), BF16), ((2, 384, 256), BF16), ((8, 768), F32)],
        7,
        cost=(300_000_000, 10_000_000),
    )(dz2, dh_own, dh_other, n1, r1, vec8, wo)

    def back(m, events):
        specs = attention_specs(m)
        return call(
            attend_back_kernel,
            [((2, BAND, 384), BF16), ((8, BAND, 384), BF16), ((8, BAND, 384), BF16)],
            8,
            grid=(1,),
            in_specs=specs[0] + specs[1] + specs[2],
            out_specs=[pl.BlockSpec((n, BAND, 384), lambda i: (0, 0, 0)) for n in (2, 8, 8)],
            cost=(2_000_000_000, 6_000_000),
        )(q, k, v, mix, after(da, *events), lse, kseg, qseg)

    def token_grads(grads, events):
        own, away = call(
            token_grad_kernel, [((4, BAND, 768), BF16)] * 2, 4, cost=(1_350_000_000, 5_000_000)
        )(*after_both(grads, events), w_abs)
        return (own, away, send(away, CORE))

    def core_sums(own, got):
        return [add(own[z], got[z]) if z == 0 else add(own[z], got[z]).astype(BF16) for z in range(4)]

    def line_sums(sums):
        return (sums[0], send(sums[1], Z1), send(sums[2], Z2), send(sums[3], MIDDLE))

    grads0 = back(0, ())
    dx0, _, got0 = token_grads(grads0, ())
    grads1 = back(1, (dx0, outer_block))
    outer_parts = after_both(block_parts(outer_block), grads1[:1])
    low0 = core_sums(dx0, after(got0, grads1[0]))
    grads1, _ = lax.optimization_barrier((grads1, (outer_parts, low0)))
    sent0 = line_sums(low0)

    def widen(value):
        zero = jnp.zeros_like(value)
        return in_order(value, zero, 1)

    def column(index):
        return sum(jnp.sum(g[index].astype(F32), axis=(0, 1)) for g in (grads0, grads1))[None]

    eight = jnp.concatenate(
        [widen(column(0)), widen(column(2)), sums1[2:3], sums1[0:1], sums1[1:2], sums2[2:3], sums2[0:1], sums2[1:2]], 0
    )
    eight = jnp.pad(eight.reshape(8, CHIPS, 2, 24), ((0, 0), (0, 0), (0, 0), (0, 104))).transpose(1, 2, 0, 3)
    db1 = jnp.where(jnp.arange(2)[None, :, None] == core, db1.reshape(CHIPS, 1, 96), 0.0)
    db1 = jnp.pad(db1, ((0, 0), (0, 0), (0, 416)))
    vec_grads = jnp.concatenate([eight.reshape(CHIPS, 2, 1024), db1], axis=2).reshape(CHIPS, 3072)
    vec_grads = dot_nn(order, vec_grads.astype(BF16)).astype(BF16).reshape(2, 2, 4, 2, 1536)
    vec_grads = jnp.pad(vec_grads, ((0, 0), (0, 0), (0, 0), (0, 6), (0, 0)))
    vec_first = vec_grads[..., :768].reshape(2, 64, 768)
    vec_second = vec_grads[..., 768:].transpose(1, 0, 2, 3, 4).reshape(2, 64, 768)
    square_terms = call(
        projection_grad_kernel,
        [((448, 768), BF16)] * 4,
        12,
        out_specs=[IN_PLACE] * 4,
        scratch=piece + [pltpu.VMEM((768, 384), BF16), pltpu.SemaphoreType.DMA((8,))],
        cost=(3_300_000_000, 12_000_000),
    )(x_all, grads0[0], grads1[0], grads0[1], grads1[1], grads0[2], grads1[2], mix_low[0], mix_low[1], mix_other, do_half, jnp.concatenate([vec_first, vec_second]))
    square_hop = first_hop(square_terms)
    dx1, _, got1 = token_grads(grads1, square_terms[:1])
    inner_block, sent0 = after_both((inner_block, sent0), (dx1,))
    inner_parts = block_parts(inner_block)
    square_hop, inner_parts, got1 = after_both((square_hop, inner_parts, got1), (dx1,))
    square_sent = hop_terms(near_terms(square_hop, 56))
    sent1 = line_sums(core_sums(dx1, got1))
    square_sent, sent1, square_hop = after_both((square_sent, sent1, square_hop), ())
    square_half = far_terms(square_hop, square_sent, 56)
    square_parts = line_parts(square_half, 56)

    outer_total = add(*outer_parts)
    inner_total = add(*inner_parts)
    grad_outer = jnp.concatenate([outer_total[:, :768], outer_total[:, 768:]], axis=0)
    keep = jnp.where(even, inner_total[:24], inner_total[24:])
    got = send(jnp.where(even, inner_total[24:], inner_total[:24]).astype(BF16), CORE).astype(F32)
    grad_inner = in_order(keep.reshape(24, CHIPS, 1, 96), got.reshape(24, CHIPS, 1, 96), 2).reshape(24, 3072)
    keep, other = call(owner_kernel, [((32, 1536), F32), ((32, 1536), BF16)], 5)(*square_half, *square_parts[1:])
    grads = call(
        result_kernel,
        [((24, 768), F32)] * 4 + [((1, 24), F32)] * 8 + [((1, 96), F32)],
        2,
    )(keep, send(other, CORE))
    squares, small = grads[:4], [g.reshape(-1) for g in grads[4:]]
    dz1 = dz1.reshape(slot_shape)
    grad_tokens = jnp.stack([add(dz1[m], *sent).astype(BF16) for m, sent in enumerate((sent0, sent1))])
    return (
        result.reshape(2, 1, BAND, 768), grad_tokens[:, None],
        squares[0], small[0], squares[1], squares[2], small[1], squares[3], small[2],
        small[3], small[4], grad_inner, small[8], grad_outer, small[5], small[6], small[7],
    )


def solution(mesh):
    in_specs = (
        P(None, "dp", "seq", None),
        P(None, "dp", None),
        P(("dp", "seq"), None),
        P(("dp", "seq")),
        P(("dp", "seq"), None),
        P(("dp", "seq"), None),
        P(("dp", "seq")),
        P(("dp", "seq"), None),
        P(("dp", "seq")),
        P(("dp", "seq")),
        P(("dp", "seq")),
        P(("dp", "seq"), None),
        P(("dp", "seq")),
        P(("dp", "seq"), None),
        P(("dp", "seq")),
        P(("dp", "seq")),
        P(("dp", "seq")),
        P(None, "dp", "seq", None),
    )
    out_specs = (
        P(None, "dp", "seq", None),
        P(None, "dp", "seq", None),
        P(("dp", "seq"), None),
        P(("dp", "seq")),
        P(("dp", "seq"), None),
        P(("dp", "seq"), None),
        P(("dp", "seq")),
        P(("dp", "seq"), None),
        P(("dp", "seq")),
        P(("dp", "seq")),
        P(("dp", "seq")),
        P(("dp", "seq"), None),
        P(("dp", "seq")),
        P(("dp", "seq"), None),
        P(("dp", "seq")),
        P(("dp", "seq")),
        P(("dp", "seq")),
    )
    paired = (mesh.shape["dp"], mesh.shape["seq"]) == (4, 8)
    return jax.shard_map(
        per_device_paired if paired else per_device, mesh=mesh, in_specs=in_specs, out_specs=out_specs, check_vma=False
    )
```

```python
import math

import jax
import jax.numpy as jnp
from jax import lax
from jax.experimental import pallas as pl
from jax.experimental.pallas import tpu as pltpu
from jax.sharding import PartitionSpec as P

HEADS = 12
HEAD_DIM = 64


def narrow(masters):
    return tuple((item.astype(jnp.bfloat16) for item in masters))


def fetch_forward(masters):
    lowered = narrow(masters)
    return (
        lax.all_gather(lowered[0], ("dp", "seq"), axis=0, tiled=True),
        lax.all_gather(lowered[1], ("dp", "seq"), axis=0, tiled=True),
        lax.all_gather(lowered[2], ("dp", "seq"), axis=0, tiled=True),
        lax.all_gather(lowered[3], ("dp", "seq"), axis=0, tiled=True),
        lax.all_gather(lowered[4], ("dp", "seq"), axis=0, tiled=True),
        lax.all_gather(lowered[5], ("dp", "seq"), axis=0, tiled=True),
        lax.all_gather(lowered[6], ("dp", "seq"), axis=0, tiled=True),
        lax.all_gather(lowered[7], ("dp", "seq"), axis=0, tiled=True),
        lax.all_gather(lowered[8], ("dp", "seq"), axis=0, tiled=True),
        lax.all_gather(lowered[9], ("dp", "seq"), axis=0, tiled=True),
        lax.all_gather(lowered[10], ("dp", "seq"), axis=0, tiled=True),
        lax.all_gather(lowered[11], ("dp", "seq"), axis=0, tiled=True),
        lax.all_gather(lowered[12], ("dp", "seq"), axis=0, tiled=True),
        lax.all_gather(lowered[13], ("dp", "seq"), axis=0, tiled=True),
        lax.all_gather(lowered[14], ("dp", "seq"), axis=0, tiled=True),
    )


def fetch_backward(masters):
    lowered = narrow(masters)
    return (
        lax.all_gather(lowered[0], ("dp", "seq"), axis=0, tiled=True),
        lax.all_gather(lowered[1], ("dp", "seq"), axis=0, tiled=True),
        lax.all_gather(lowered[2], ("dp", "seq"), axis=0, tiled=True),
        lax.all_gather(lowered[3], ("dp", "seq"), axis=0, tiled=True),
        lax.all_gather(lowered[4], ("dp", "seq"), axis=0, tiled=True),
        lax.all_gather(lowered[5], ("dp", "seq"), axis=0, tiled=True),
        lax.all_gather(lowered[6], ("dp", "seq"), axis=0, tiled=True),
        lax.all_gather(lowered[7], ("dp", "seq"), axis=0, tiled=True),
        lax.all_gather(lowered[8], ("dp", "seq"), axis=0, tiled=True),
        lax.all_gather(lowered[9], ("dp", "seq"), axis=0, tiled=True),
        lax.all_gather(lowered[10], ("dp", "seq"), axis=0, tiled=True),
        lax.all_gather(lowered[11], ("dp", "seq"), axis=0, tiled=True),
        lax.all_gather(lowered[12], ("dp", "seq"), axis=0, tiled=True),
        lax.all_gather(lowered[13], ("dp", "seq"), axis=0, tiled=True),
        lax.all_gather(lowered[14], ("dp", "seq"), axis=0, tiled=True),
    )


def sum_owners(terms):
    return (
        lax.psum_scatter(terms[0], ("dp", "seq"), scatter_dimension=0, tiled=True),
        lax.psum_scatter(terms[1], ("dp", "seq"), scatter_dimension=0, tiled=True),
        lax.psum_scatter(terms[2], ("dp", "seq"), scatter_dimension=0, tiled=True),
        lax.psum_scatter(terms[3], ("dp", "seq"), scatter_dimension=0, tiled=True),
        lax.psum_scatter(terms[4], ("dp", "seq"), scatter_dimension=0, tiled=True),
        lax.psum_scatter(terms[5], ("dp", "seq"), scatter_dimension=0, tiled=True),
        lax.psum_scatter(terms[6], ("dp", "seq"), scatter_dimension=0, tiled=True),
        lax.psum_scatter(terms[7], ("dp", "seq"), scatter_dimension=0, tiled=True),
        lax.psum_scatter(terms[8], ("dp", "seq"), scatter_dimension=0, tiled=True),
        lax.psum_scatter(terms[9], ("dp", "seq"), scatter_dimension=0, tiled=True),
        lax.psum_scatter(terms[10], ("dp", "seq"), scatter_dimension=0, tiled=True),
        lax.psum_scatter(terms[11], ("dp", "seq"), scatter_dimension=0, tiled=True),
        lax.psum_scatter(terms[12], ("dp", "seq"), scatter_dimension=0, tiled=True),
        lax.psum_scatter(terms[13], ("dp", "seq"), scatter_dimension=0, tiled=True),
        lax.psum_scatter(terms[14], ("dp", "seq"), scatter_dimension=0, tiled=True),
    )


def layer_norm(z, gain, shift):
    mean = jnp.mean(z, axis=-1, keepdims=True)
    centered = z - mean
    rstd = lax.rsqrt(jnp.mean(centered * centered, axis=-1, keepdims=True) + 1e-05)
    normed = centered * rstd
    return (normed * gain + shift, normed, rstd)


def norm_back(grad, normed, rstd, gain):
    scaled = grad * gain
    inner = (
        scaled
        - jnp.mean(scaled, axis=-1, keepdims=True)
        - normed * jnp.mean(scaled * normed, axis=-1, keepdims=True)
    )
    return (rstd * inner, jnp.sum(grad * normed, axis=0), jnp.sum(grad, axis=0))


def gelu_exact(value):
    return jax.nn.gelu(value, approximate=False)


def key_blocks(keys_all, values_all, seg_row):
    length = keys_all.shape[0]
    width = math.gcd(length, 1024)
    count = length // width
    keys_split = keys_all.reshape(count, width, HEADS, HEAD_DIM)
    values_split = values_all.reshape(count, width, HEADS, HEAD_DIM)
    return (keys_split, values_split, seg_row.reshape(count, width))


def block_scores(queries, keys, query_seg, key_seg):
    scores = jnp.einsum("qhd,khd->hqk", queries, keys, preferred_element_type=jnp.float32) * 0.125
    same = (query_seg[:, None] == key_seg[None, :])[None]
    return jnp.where(same, scores, -1e30)


def attend(queries, keys_all, values_all, seg_row, query_seg):
    rows = queries.shape[0]
    query_h = queries.reshape(rows, HEADS, HEAD_DIM)
    keys_split, values_split, seg_split = key_blocks(keys_all, values_all, seg_row)

    def first_pass(carry, block):
        top, total = carry
        keys, key_seg = block
        scores = block_scores(query_h, keys, query_seg, key_seg)
        new_top = jnp.maximum(top, jnp.max(scores, axis=-1))
        total = total * jnp.exp(top - new_top) + jnp.sum(
            jnp.exp(scores - new_top[..., None]), axis=-1
        )
        return ((new_top, total), None)

    start = (jnp.full((HEADS, rows), -1e30, jnp.float32), jnp.zeros((HEADS, rows), jnp.float32))
    (top, total), _ = lax.scan(first_pass, start, (keys_split, seg_split))
    lse = top + jnp.log(total)

    def second_pass(acc, block):
        keys, values, key_seg = block
        scores = block_scores(query_h, keys, query_seg, key_seg)
        probs = jnp.exp(scores - lse[..., None]).astype(jnp.bfloat16)
        return (
            acc + jnp.einsum("hqk,khd->qhd", probs, values, preferred_element_type=jnp.float32),
            None,
        )

    mixed, _ = lax.scan(
        second_pass,
        jnp.zeros((rows, HEADS, HEAD_DIM), jnp.float32),
        (keys_split, values_split, seg_split),
    )
    return (lse, mixed.reshape(rows, HEADS * HEAD_DIM))


def attend_back(queries, grad_mixed, lse, delta, keys_all, values_all, seg_row, query_seg):
    rows = queries.shape[0]
    query_h = queries.reshape(rows, HEADS, HEAD_DIM)
    grad_h = grad_mixed.reshape(rows, HEADS, HEAD_DIM)
    keys_split, values_split, seg_split = key_blocks(keys_all, values_all, seg_row)

    def step(grad_query, block):
        keys, values, key_seg = block
        scores = block_scores(query_h, keys, query_seg, key_seg)
        probs = jnp.exp(scores - lse[..., None])
        grad_probs = jnp.einsum("qhd,khd->hqk", grad_h, values, preferred_element_type=jnp.float32)
        grad_scores = (probs * (grad_probs - delta[..., None])).astype(jnp.bfloat16)
        grad_query = grad_query + jnp.einsum(
            "hqk,khd->qhd", grad_scores, keys, preferred_element_type=jnp.float32
        )
        grad_keys = (
            jnp.einsum("hqk,qhd->khd", grad_scores, query_h, preferred_element_type=jnp.float32)
            * 0.125
        )
        grad_values = jnp.einsum(
            "hqk,qhd->khd", probs.astype(jnp.bfloat16), grad_h, preferred_element_type=jnp.float32
        )
        width = keys.shape[0]
        joined = jnp.concatenate(
            [
                grad_keys.reshape(width, HEADS * HEAD_DIM),
                grad_values.reshape(width, HEADS * HEAD_DIM),
            ],
            axis=-1,
        )
        return (grad_query, joined)

    grad_query, joined = lax.scan(
        step, jnp.zeros((rows, HEADS, HEAD_DIM), jnp.float32), (keys_split, values_split, seg_split)
    )
    grad_query = (grad_query * 0.125).reshape(rows, HEADS * HEAD_DIM)
    return (grad_query, joined.reshape(keys_all.shape[0], 2 * HEADS * HEAD_DIM))


def outer_sum(left, right):
    return jnp.einsum("tf,tg->fg", left, right, preferred_element_type=jnp.float32)


def times_transposed(left, weight):
    return jnp.einsum("tg,fg->tf", left, weight, preferred_element_type=jnp.float32)


def column_sum(value):
    return jnp.sum(value.astype(jnp.float32), axis=0)


def per_device(
    inputs,
    segments,
    w_query,
    b_query,
    w_key,
    w_value,
    b_value,
    w_output,
    b_output,
    gain_first,
    shift_first,
    w_inner,
    b_inner,
    w_outer,
    b_outer,
    gain_second,
    shift_second,
    cotangent,
):
    masters = (
        w_query,
        b_query,
        w_key,
        w_value,
        b_value,
        w_output,
        b_output,
        gain_first,
        shift_first,
        w_inner,
        b_inner,
        w_outer,
        b_outer,
        gain_second,
        shift_second,
    )
    rows = inputs.shape[2]
    offset = lax.axis_index("seq") * rows
    results = []
    grad_rows = []
    totals = None
    for micro in range(inputs.shape[0]):
        tokens = inputs[micro, 0]
        seg_row = segments[micro, 0]
        query_seg = lax.dynamic_slice_in_dim(seg_row, offset, rows)
        full = fetch_forward(masters)
        wq, bq, wk, wv, bv, wo, bo, g1, s1, w1, b1, w2, b2, g2, s2 = full
        g1f, s1f, g2f, s2f = (
            g1.astype(jnp.float32),
            s1.astype(jnp.float32),
            g2.astype(jnp.float32),
            s2.astype(jnp.float32),
        )
        queries = (
            jnp.dot(tokens, wq, preferred_element_type=jnp.float32) + bq.astype(jnp.float32)
        ).astype(jnp.bfloat16)
        keys = jnp.dot(tokens, wk, preferred_element_type=jnp.float32).astype(jnp.bfloat16)
        values = (
            jnp.dot(tokens, wv, preferred_element_type=jnp.float32) + bv.astype(jnp.float32)
        ).astype(jnp.bfloat16)
        keys_all, values_all = (
            lax.all_gather(keys, "seq", axis=0, tiled=True),
            lax.all_gather(values, "seq", axis=0, tiled=True),
        )
        lse, mixed = attend(queries, keys_all, values_all, seg_row, query_seg)
        mixed_low = mixed.astype(jnp.bfloat16)
        branch = jnp.dot(mixed_low, wo, preferred_element_type=jnp.float32) + bo.astype(jnp.float32)
        hidden, normed_first, rstd_first = layer_norm(tokens.astype(jnp.float32) + branch, g1f, s1f)
        hidden_low = hidden.astype(jnp.bfloat16)
        inner = jnp.dot(hidden_low, w1, preferred_element_type=jnp.float32) + b1.astype(jnp.float32)
        active, gelu_pull = jax.vjp(gelu_exact, inner)
        active_low = active.astype(jnp.bfloat16)
        outer = jnp.dot(active_low, w2, preferred_element_type=jnp.float32) + b2.astype(jnp.float32)
        result, normed_second, rstd_second = layer_norm(hidden + outer, g2f, s2f)
        results.append(result.astype(jnp.bfloat16))
        wq, bq, wk, wv, bv, wo, bo, g1, s1, w1, b1, w2, b2, g2, s2 = fetch_backward(masters)
        keys_all, values_all = (
            lax.all_gather(keys, "seq", axis=0, tiled=True),
            lax.all_gather(values, "seq", axis=0, tiled=True),
        )
        grad_out = cotangent[micro, 0].astype(jnp.float32)
        grad_z2, grad_g2, grad_s2 = norm_back(grad_out, normed_second, rstd_second, g2f)
        grad_outer = grad_z2.astype(jnp.bfloat16)
        grad_w2 = outer_sum(active_low, grad_outer)
        grad_b2 = column_sum(grad_outer)
        grad_active = times_transposed(grad_outer, w2)
        grad_inner = gelu_pull(grad_active)[0].astype(jnp.bfloat16)
        grad_w1 = outer_sum(hidden_low, grad_inner)
        grad_b1 = column_sum(grad_inner)
        grad_hidden = times_transposed(grad_inner, w1) + grad_z2
        grad_z1, grad_g1, grad_s1 = norm_back(grad_hidden, normed_first, rstd_first, g1f)
        grad_branch = grad_z1.astype(jnp.bfloat16)
        grad_wo = outer_sum(mixed_low, grad_branch)
        grad_bo = column_sum(grad_branch)
        grad_mixed = times_transposed(grad_branch, wo).astype(jnp.bfloat16)
        delta = jnp.sum(
            (grad_mixed.astype(jnp.float32) * mixed).reshape(rows, HEADS, HEAD_DIM), axis=-1
        ).T
        grad_query, joined = attend_back(
            queries, grad_mixed, lse, delta, keys_all, values_all, seg_row, query_seg
        )
        summed = lax.psum_scatter(
            joined.astype(jnp.bfloat16), "seq", scatter_dimension=0, tiled=True
        ).astype(jnp.float32)
        width = summed.shape[1] // 2
        grad_keys = summed[:, :width].astype(jnp.bfloat16)
        grad_values = summed[:, width:].astype(jnp.bfloat16)
        grad_query = grad_query.astype(jnp.bfloat16)
        grad_wq = outer_sum(tokens, grad_query)
        grad_wk = outer_sum(tokens, grad_keys)
        grad_wv = outer_sum(tokens, grad_values)
        grad_bq = column_sum(grad_query)
        grad_bv = column_sum(grad_values)
        grad_tokens = (
            times_transposed(grad_query, wq)
            + times_transposed(grad_keys, wk)
            + times_transposed(grad_values, wv)
            + grad_z1
        )
        grad_rows.append(grad_tokens.astype(jnp.bfloat16))
        terms = (
            grad_wq,
            grad_bq,
            grad_wk,
            grad_wv,
            grad_bv,
            grad_wo,
            grad_bo,
            grad_g1,
            grad_s1,
            grad_w1,
            grad_b1,
            grad_w2,
            grad_b2,
            grad_g2,
            grad_s2,
        )
        totals = terms if totals is None else tuple((old + new for old, new in zip(totals, terms)))
    owned = sum_owners(totals)
    outputs = jnp.stack(results)[:, None]
    grad_inputs = jnp.stack(grad_rows)[:, None]
    return (
        outputs,
        grad_inputs,
        owned[0],
        owned[1],
        owned[2],
        owned[3],
        owned[4],
        owned[5],
        owned[6],
        owned[7],
        owned[8],
        owned[9],
        owned[10],
        owned[11],
        owned[12],
        owned[13],
        owned[14],
    )


BOTH = ("dp", "seq")
CHIPS = 16
BAND = 128
F32 = jnp.float32
BF16 = jnp.bfloat16
IN_VMEM = pl.BlockSpec(memory_space=pltpu.VMEM)
IN_PLACE = pl.BlockSpec(memory_space=pl.ANY)


def pairs(dp_bits, seq_bits, keep=lambda dp, seq: True):
    return [
        (dp * 8 + seq, (dp ^ dp_bits) * 8 + (seq ^ seq_bits))
        for dp in range(4)
        for seq in range(8)
        if keep(dp, seq)
    ]


CORE, Z1, Z2, Z3 = pairs(0, 1), pairs(0, 2), pairs(0, 4), pairs(0, 6)
X, Y = pairs(1, 0), pairs(2, 0)
MIDDLE = pairs(0, 6, lambda dp, seq: seq // 2 in (1, 2))


def send(value, route):
    return lax.ppermute(value, BOTH, route)


def after(value, *events):
    return lax.optimization_barrier((value, *events))[0]


def after_both(values, events):
    return lax.optimization_barrier((tuple(values), tuple(events)))[0]


def my_chip():
    return lax.axis_index("dp") * 4 + lax.axis_index("seq") // 2


def my_core():
    return lax.axis_index("seq") % 2


def dot_nn(a, b):
    return lax.dot_general(a, b, (((1,), (0,)), ((), ())), preferred_element_type=F32)


def dot_nt(a, b):
    return lax.dot_general(a, b, (((1,), (1,)), ((), ())), preferred_element_type=F32)


def dot_tn(a, b):
    return lax.dot_general(a, b, (((0,), (0,)), ((), ())), preferred_element_type=F32)


def call(body, outs, n_in, in_specs=None, out_specs=None, scratch=(), grid=None, cost=None):
    kwargs = {} if grid is None else {"grid": grid}
    return pl.pallas_call(
        body,
        out_shape=[jax.ShapeDtypeStruct(s, d) for s, d in outs],
        in_specs=in_specs or [IN_VMEM] * n_in,
        out_specs=out_specs or [IN_VMEM] * len(outs),
        scratch_shapes=list(scratch),
        cost_estimate=pl.CostEstimate(flops=cost[0], bytes_accessed=cost[1], transcendentals=0)
        if cost
        else None,
        **kwargs,
    )


def line(block):
    return [block, send(block, Z1), send(block, Z2), send(block, Z3)]


def lines(block):
    return lax.all_gather(block, "dp", axis=0, tiled=True)


def placed(rows, target, sems, base):
    me = my_chip() % 4
    copies = []
    for i in range(CHIPS):
        at = pl.multiple_of(((i // 4) * 4 + ((i % 4) ^ me)) * 48, 16)
        copies.append(
            pltpu.make_async_copy(
                rows.at[pl.ds((i // 4) * 224 + (i % 4) * 48, 48)], target.at[pl.ds(at, 48)], sems.at[base + i]
            )
        )
    return copies


def x_then_y(first, second):
    return (send(first, X), send(second, Y))


def y_then_x(first, second):
    return (send(first, Y), send(second, X))


def placed_hidden(groups, targets, sems):
    me = my_chip()
    copies = ([], [])
    for i, group in enumerate(groups):
        which, far, near = i // 4, (i // 2) % 2, i % 2
        for z in range(4):
            b = (far * (8, 4)[which] + near * (4, 8)[which] + z) ^ me
            for part in range(1 + which):
                cols = pl.ds(768 * part, 768) if which else pl.ds(0, 1536)
                at = pl.multiple_of(b * (48, 96)[which] + 48 * part, 16)
                sem = sems.at[16 * which + len(copies[which])]
                rows = group.at[pl.ds(z * 48, 48), cols]
                copies[which].append(pltpu.make_async_copy(rows, targets[which].at[pl.ds(at, 48)], sem))
    return copies


def prepare_kernel(*refs):
    weights, vecs, outer_ref = refs[0:4], refs[4:13], refs[13]
    mine_ref, theirs_ref, rows_ref = refs[14:]
    even = my_core() == 0
    theirs_ref[24:32] = jnp.zeros((8, 1536), BF16)
    for i, ref in enumerate(weights):
        w, cols = ref[...].astype(BF16), slice(384 * i, 384 * i + 384)
        mine_ref[0:24, cols] = jnp.where(even, w[:, :384], w[:, 384:])
        theirs_ref[0:24, cols] = jnp.where(even, w[:, 384:], w[:, :384])
    pieces = []
    for ref in vecs:
        pieces += [ref[...], jnp.zeros((1, 128 - ref.shape[1]), F32)]
    row = jnp.concatenate(pieces + [jnp.zeros((1, 384), F32)], axis=1)
    row = jnp.where(lax.broadcasted_iota(jnp.int32, (8, 1536), 0) == 0, row, 0.0).astype(BF16)
    mine_ref[24:32] = row
    theirs_ref[24:32] = row
    rows_ref[:, 0:768] = outer_ref[0:48].astype(BF16)
    rows_ref[:, 768:1536] = outer_ref[48:96].astype(BF16)


def chip_rows_kernel(mine_ref, got_ref, out_ref):
    even = my_core() == 0
    mine, got = mine_ref[...].astype(F32), got_ref[...].astype(F32)
    out_ref[0:24] = jnp.where(even, mine[:24], got[:24]).astype(BF16)
    out_ref[24:48] = jnp.where(even, got[:24], mine[:24]).astype(BF16)
    first = jnp.where(even, mine[24:32], got[24:32])
    second = jnp.where(even, got[24:32], mine[24:32])
    row = lax.broadcasted_iota(jnp.int32, (8, 1536), 0)
    out_ref[48:56] = jnp.where(row == 1, second[0:1], jnp.where(row == 0, first[0:1], 0.0)).astype(BF16)


def owner_kernel(first_ref, second_ref, *refs):
    parts, (keep_ref, other_ref) = refs[:3], refs[3:]
    even = my_core() == 0
    for c, ref in ((0, first_ref), (768, second_ref)):
        cols = slice(c, c + 768)
        a, b, d = (p[:, cols].astype(F32) for p in parts)
        rows = ref[0:48].astype(F32) + a[:48] + b[:48] + d[:48]
        keep_ref[0:24, cols] = jnp.where(even, rows[:24], rows[24:])
        other_ref[0:24, cols] = jnp.where(even, rows[24:], rows[:24]).astype(BF16)
        vec = ref[192:200].astype(F32) + a[48:56] + b[48:56] + d[48:56]
        zero = jnp.zeros((7, 768), F32)
        keep_ref[24:32, cols] = jnp.concatenate([jnp.where(even, vec[0:1], vec[1:2]), zero], axis=0)
        other_ref[24:32, cols] = jnp.concatenate([jnp.where(even, vec[1:2], vec[0:1]), zero], axis=0).astype(BF16)


def result_kernel(keep_ref, got_ref, *refs):
    outs, vecs = refs[:4], refs[4:]
    even = my_core() == 0
    for i, ref in enumerate(outs):
        cols = slice(384 * i, 384 * i + 384)
        keep, got = keep_ref[0:24, cols], got_ref[0:24, cols].astype(F32)
        ref[:, 0:384] = jnp.where(even, keep, got)
        ref[:, 384:768] = jnp.where(even, got, keep)
    vec = keep_ref[24:25] + got_ref[24:32].astype(F32)[0:1]
    for i, ref in enumerate(vecs):
        ref[...] = vec[:, 128 * i : 128 * i + ref.shape[1]]


def project_kernel(*refs):
    xs, theirs, rows = refs[0:5], refs[5], refs[6]
    bq_ref, bv_ref = refs[7:9]
    q_ref, k_ref, v_ref, w_ref, x_ref, sems = refs[9:]
    slots = [*zip((0, 1, 2, 4, 6), xs), *((2 * z + 3, theirs.at[z]) for z in range(3))]
    loads = [pltpu.make_async_copy(ref, x_ref.at[s], sems.at[32 + s]) for s, ref in slots]
    loads += placed(rows, w_ref, sems, 0)
    for c in loads:
        c.start()
    for c in loads:
        c.wait()
    bq, bv = bq_ref[...], bv_ref[...]

    def queries(s, _):
        x = x_ref[s].reshape(2 * BAND, 768)
        q = (dot_nn(x, w_ref[:, 0:384]) + bq).astype(BF16) * jnp.asarray(0.125, BF16)
        q_ref[s] = q.reshape(2, BAND, 384)
        return 0

    lax.fori_loop(0, 2, queries, 0)

    def slot(s, _):
        x = x_ref[s].reshape(2 * BAND, 768)
        k_ref[s] = dot_nn(x, w_ref[:, 384:768]).astype(BF16).reshape(2, BAND, 384)
        v_ref[s] = (dot_nn(x, w_ref[:, 768:1152]) + bv).astype(BF16).reshape(2, BAND, 384)
        return 0

    lax.fori_loop(0, 8, slot, 0)


def fill_mask(mask_ref, kseg_ref, qseg_ref):
    for c in range(4):
        rows = slice(256 * c, 256 * c + 256)
        mask_ref[rows] = jnp.where(kseg_ref[0, rows] == qseg_ref[0], 0.0, -1e30)


def attend_kernel(
    q_ref, k_ref, v_ref, kseg_ref, qseg_ref, rows_ref, got_ref,
    mix_ref, low_ref, lse_ref, out_ref, wo_ref, mask_ref, score_ref, weight_ref, sems,
):
    core, me = my_core(), my_chip() % 4
    first = pl.program_id(0) == 0
    loads = []
    for i in range(8):
        at = pl.ds(pl.multiple_of((i // 4) * 192 + ((i % 4) ^ me) * 48, 16), 48)
        row = (i // 4) * 224 + (i % 4) * 48
        mine = rows_ref.at[pl.ds(pl.multiple_of(core * 448 + row, 16), 48), pl.ds(1152, 384)]
        for j, src in enumerate((mine, got_ref.at[pl.ds(row, 48)])):
            cols = pl.ds(pl.multiple_of((core if j == 0 else 1 - core) * 384, 128), 384)
            loads.append(pltpu.make_async_copy(src, wo_ref.at[at, cols], sems.at[2 * i + j]))

    @pl.when(first)
    def _():
        for c in loads:
            c.start()

    fill_mask(mask_ref, kseg_ref, qseg_ref)

    def pair(j, _):
        both = pl.ds(pl.multiple_of(128 * j, 128), 128)
        q2 = q_ref[:, 0, :, both].reshape(2 * BAND, 128)

        def score(c, tops):
            rows = pl.ds(pl.multiple_of(256 * c, 256), 256)
            k2 = k_ref[pl.ds(2 * c, 2), 0, :, both].reshape(256, 128)
            new = []
            for h in range(2):
                cols = slice(64 * h, 64 * h + 64)
                s = dot_nt(k2[:, cols], q2[:, cols]) + mask_ref[rows]
                score_ref[h, rows] = s
                new.append(jnp.maximum(tops[h], jnp.max(s, axis=0, keepdims=True)))
            return tuple(new)

        tops = lax.fori_loop(0, 4, score, (jnp.full((1, 256), -1e30, F32),) * 2, unroll=True)

        def weigh(c, totals):
            rows = pl.ds(pl.multiple_of(256 * c, 256), 256)
            new = []
            for h in range(2):
                e = jnp.exp(score_ref[h, rows] - tops[h])
                weight_ref[h, rows] = e.astype(BF16)
                new.append(totals[h] + jnp.sum(e, axis=0, keepdims=True))
            return tuple(new)

        totals = lax.fori_loop(0, 4, weigh, (jnp.zeros((1, 256), F32),) * 2, unroll=True)
        v2 = v_ref[:, 0, :, both].reshape(8 * BAND, 128)
        for h in range(2):
            mixed = dot_tn(v2[:, 64 * h : 64 * h + 64], weight_ref[h]) * (1.0 / totals[h])
            rows = pl.ds(pl.multiple_of(128 * j + 64 * h, 64), 64)
            mix_ref[0, rows] = mixed
            low_ref[0, rows] = mixed.astype(BF16)
            lse_ref[0, pl.ds(2 * j + h, 1)] = tops[h] + jnp.log(totals[h])
        return 0

    lax.fori_loop(0, 3, pair, 0)

    @pl.when(first)
    def _():
        for c in loads:
            c.wait()

    out_ref[:, 0] = dot_tn(low_ref[0], wo_ref[...]).astype(BF16).reshape(2, BAND, 768)


def norm(z):
    mean = jnp.mean(z, axis=-1, keepdims=True)
    centered = z - mean
    rstd = lax.rsqrt(jnp.mean(centered * centered, axis=-1, keepdims=True) + 1e-05)
    return (centered * rstd, rstd)


def norm_grad(grad, normed, rstd, gain):
    scaled = grad * gain
    return rstd * (
        scaled
        - jnp.mean(scaled, axis=-1, keepdims=True)
        - normed * jnp.mean(scaled * normed, axis=-1, keepdims=True)
    )


def forward_kernel(*refs):
    x_ref, own_ref, other_ref, vec_ref, b1_ref = refs[0:5]
    n1_ref, r1_ref, low_ref, act_ref, slope_ref, f_ref, w1_ref, w2_ref, tok_buf, own_buf, other_buf, sems = refs[13:]
    loads1, loads2 = placed_hidden(refs[5:13], (w1_ref, w2_ref), sems)
    early = [
        pltpu.make_async_copy(src, dst, sems.at[48 + i])
        for i, (src, dst) in enumerate(
            ((x_ref.at[pl.ds(0, 2)], tok_buf), (own_ref, own_buf), (other_ref, other_buf))
        )
    ]
    for c in early + loads1 + loads2:
        c.start()
    for c in early:
        c.wait()
    bo, g1, s1 = vec_ref[2:3], vec_ref[3:4], vec_ref[4:5]

    def rows(i, _):
        r = pl.ds(i * 128, 128)
        c, m = i // 2, i % 2
        z = tok_buf[c, m].astype(F32) + (own_buf[c, m].astype(F32) + other_buf[1 - c, m].astype(F32)) + bo
        n, rstd = norm(z)
        n1_ref[r] = n
        r1_ref[r] = rstd
        low_ref[r] = (n * g1 + s1).astype(BF16)
        return 0

    lax.fori_loop(0, 4, rows, 0)
    for c in loads1:
        c.wait()

    def inner(j, _):
        cols = pl.ds(pl.multiple_of(j * 256, 256), 256)
        u = dot_nn(low_ref[...], w1_ref[:, cols]) + b1_ref[:, cols]
        cdf = 0.5 * (1.0 + lax.erf(u * (1.0 / math.sqrt(2.0))))
        act_ref[:, cols] = (u * cdf).astype(BF16)
        slope = cdf + u * (jnp.exp(-0.5 * u * u) * (1.0 / math.sqrt(2.0 * math.pi)))
        slope_ref[:, cols] = slope.astype(BF16)
        return 0

    lax.fori_loop(0, 6, inner, 0)
    for c in loads2:
        c.wait()

    def outer(j, _):
        cols = pl.ds(pl.multiple_of(j * 256, 256), 256)
        f_ref[:, cols] = dot_nn(act_ref[...], w2_ref[:, cols]).astype(BF16)
        return 0

    lax.fori_loop(0, 3, outer, 0)


def middle_kernel(
    n1_ref, own_ref, other_ref, cot_ref, theirs_ref, vec_ref, out_ref, df_ref, dz_ref, sums_ref, pcot_ref, sem,
):
    load = pltpu.make_async_copy(theirs_ref.at[3], pcot_ref, sem)
    load.start()
    g1, s1, b2, g2, s2 = (vec_ref[i : i + 1] for i in (3, 4, 5, 6, 7))

    def rows(i, which):
        ref, base = which
        r, o = pl.ds(base + i * 128, 128), pl.ds(256 - base + i * 128, 128)
        z = n1_ref[r] * g1 + s1 + (own_ref[r].astype(F32) + other_ref[o].astype(F32)) + b2
        n, rstd = norm(z)
        grad = ref[i].astype(F32)
        dz = norm_grad(grad, n, rstd, g2)
        dz_ref[r] = dz
        df_ref[r] = dz.astype(BF16)
        return (r, n, grad, dz)

    sums_ref[...] = jnp.zeros_like(sums_ref)

    def own_rows(i, _):
        r, n, grad, dz = rows(i, (cot_ref, 0))
        out_ref[r] = (n * g2 + s2).astype(BF16)
        sums_ref[0:1] += jnp.sum(grad * n, axis=0, keepdims=True)
        sums_ref[1:2] += jnp.sum(grad, axis=0, keepdims=True)
        sums_ref[2:3] += jnp.sum(dz.astype(BF16).astype(F32), axis=0, keepdims=True)
        return 0

    def other_rows(i, _):
        rows(i, (pcot_ref, 256))
        return 0

    lax.fori_loop(0, 2, own_rows, 0)
    load.wait()
    lax.fori_loop(0, 2, other_rows, 0)


def hidden_kernel(df_ref, slope_ref, w1_ref, w2_ref, du_ref, dh_ref, db1_ref):
    def hidden(j, _):
        cols = pl.ds(pl.multiple_of(j * 256, 256), 256)
        du = (dot_nt(df_ref[...], w2_ref[cols, :]) * slope_ref[:, cols].astype(F32)).astype(BF16)
        du_ref[:, cols] = du
        db1_ref[:, cols] = jnp.sum(du.astype(F32), axis=0, keepdims=True)
        return 0

    lax.fori_loop(0, 6, hidden, 0)

    def back(j, _):
        cols = pl.ds(pl.multiple_of(j * 256, 256), 256)
        dh_ref[:, cols] = dot_nt(du_ref[...], w1_ref[cols, :]).astype(BF16)
        return 0

    lax.fori_loop(0, 3, back, 0)


def first_kernel(
    dz_ref, own_ref, other_ref, n1_ref, r1_ref, vec_ref, wo_ref, dz1_ref, do_ref, half_ref, da_ref, sums_ref,
):
    g1 = vec_ref[3:4]
    core = my_core()
    sums_ref[...] = jnp.zeros_like(sums_ref)

    def rows(i):
        r, o = pl.ds(i * 128, 128), pl.ds((i ^ 2) * 128, 128)
        grad = dz_ref[r] + (own_ref[r].astype(F32) + other_ref[o].astype(F32))
        n = n1_ref[r]
        dz = norm_grad(grad, n, r1_ref[r], g1)
        low = dz.astype(BF16)
        do_ref[r] = low
        half_ref[r] = jnp.where(core == 0, low[:, :384], low[:, 384:])
        return (r, n, grad, dz, low)

    def own_rows(i, _):
        r, n, grad, dz, low = rows(i)
        dz1_ref[r] = dz
        sums_ref[0:1] += jnp.sum(grad * n, axis=0, keepdims=True)
        sums_ref[1:2] += jnp.sum(grad, axis=0, keepdims=True)
        sums_ref[2:3] += jnp.sum(low.astype(F32), axis=0, keepdims=True)
        return 0

    def other_rows(i, _):
        rows(i)
        return 0

    lax.fori_loop(0, 2, own_rows, 0)
    lax.fori_loop(2, 4, other_rows, 0)
    for m in range(2):
        for c in range(2):
            part = do_ref[pl.ds((c * 2 + m) * BAND, BAND), :]
            da_ref[m, :, c * BAND : (c + 1) * BAND] = dot_nt(wo_ref[...], part).astype(BF16)


def attend_back_kernel(
    q_ref, k_ref, v_ref, mix_ref, da_ref, lse_ref, kseg_ref, qseg_ref, w_ref, dq_ref, dk_ref, dv_ref, own_ref, send_ref, sums_ref,
    mask_ref,
):
    fill_mask(mask_ref, kseg_ref, qseg_ref)

    def pair(j, _):
        both = pl.ds(pl.multiple_of(128 * j, 128), 128)
        q2 = q_ref[:, 0, :, both].reshape(2 * BAND, 128)
        das, deltas, lses = [], [], []
        for h in range(2):
            rows = pl.ds(pl.multiple_of(128 * j + 64 * h, 64), 64)
            das.append(da_ref[0, rows])
            deltas.append(jnp.sum(das[h].astype(F32) * mix_ref[0, rows], axis=0, keepdims=True))
            lses.append(lse_ref[0, pl.ds(2 * j + h, 1)])
        k2 = k_ref[:, 0, :, both].reshape(8 * BAND, 128)
        v2 = v_ref[:, 0, :, both].reshape(8 * BAND, 128)
        dks, dvs, dqs = [], [], []
        for h in range(2):
            cols = slice(64 * h, 64 * h + 64)
            k, v, qh, da = k2[:, cols], v2[:, cols], q2[:, cols], das[h]
            p = jnp.exp(dot_nt(k, qh) + mask_ref[...] - lses[h])
            ds = (p * (dot_nn(v, da) - deltas[h])).astype(BF16)
            dvs.append(dot_nt(p.astype(BF16), da))
            dks.append(dot_nn(ds, qh))
            dqs.append(dot_tn(k, ds))
        dk_ref[:, :, both] = jnp.concatenate(dks, axis=1).astype(BF16).reshape(8, BAND, 128)
        dv_ref[:, :, both] = jnp.concatenate(dvs, axis=1).astype(BF16).reshape(8, BAND, 128)
        dq = jnp.transpose(jnp.concatenate(dqs, axis=0) * 0.125)
        dq_ref[:, :, both] = dq.astype(BF16).reshape(2, BAND, 128)
        return 0

    lax.fori_loop(0, 3, pair, 0)

    sums_ref[0:1] = jnp.sum(dq_ref[...].reshape(2 * BAND, 384).astype(F32), axis=0, keepdims=True)
    sums_ref[1:2] = jnp.sum(dv_ref[...].reshape(8 * BAND, 384).astype(F32), axis=0, keepdims=True)

    def step(z, _):
        dk = dk_ref[pl.ds(2 * z, 2)].reshape(2 * BAND, 384)
        dv = dv_ref[pl.ds(2 * z, 2)].reshape(2 * BAND, 384)
        dx = dot_nt(dk, w_ref[:, 384:768]) + dot_nt(dv, w_ref[:, 768:1152])
        own_ref[z] = dx[:BAND].astype(BF16)
        send_ref[z] = dx[BAND:].astype(BF16)
        return 0

    lax.fori_loop(1, 4, step, 0)
    dx = dot_nt(dk_ref[0:2].reshape(2 * BAND, 384), w_ref[:, 384:768])
    dx += dot_nt(dv_ref[0:2].reshape(2 * BAND, 384), w_ref[:, 768:1152])
    dx += dot_nt(dq_ref[...].reshape(2 * BAND, 384), w_ref[:, 0:384])
    own_ref[0] = dx[:BAND].astype(BF16)
    send_ref[0] = dx[BAND:].astype(BF16)


def inner_grad_kernel(low_ref, du_ref, out_ref):
    me = my_chip() % 4

    def step(j, _):
        cols = pl.ds(pl.multiple_of(j * 384, 384), 384)
        value = dot_tn(low_ref[:, cols], du_ref[...]).astype(BF16)
        for i in range(8):
            rows = pl.ds(pl.multiple_of((j * 8 + (i ^ me)) * 48, 16), 48)
            out_ref[rows, :] = value[48 * i : 48 * i + 48]
        return 0

    lax.fori_loop(0, 2, step, 0)


def stored_at(block):
    p = block ^ my_chip()
    y, x, z = p // 8, (p // 4) % 2, p % 4
    return ((y, x * 4 + z), (x, y * 4 + z))


def place_rows(halves, block, first, second):
    for ref, (away, row), value in zip(halves, stored_at(block), (first, second)):
        ref[away, pl.ds(pl.multiple_of(row * 48, 16), 48)] = value


def flush(halves, outs, sems):
    copies = [
        pltpu.make_async_copy(halves[i // 2].at[i % 2], out.at[pl.ds(0, 384)], sems.at[i])
        for i, out in enumerate(outs)
    ]
    return copies


def finish(copies):
    for c in copies:
        c.start()
    for c in copies:
        c.wait()


def outer_grad_kernel(act_ref, df_ref, *refs):
    outs, halves, sems = refs[:4], refs[4:6], refs[6]

    def step(j, _):
        cols = pl.ds(pl.multiple_of(j * 384, 384), 384)
        value = dot_tn(act_ref[:, cols], df_ref[...]).astype(BF16)
        for i in range(4):
            place_rows(halves, j * 4 + i, value[96 * i : 96 * i + 48], value[96 * i + 48 : 96 * i + 96])
        return 0

    lax.fori_loop(0, 4, step, 0)
    finish(flush(halves, outs, sems))


def projection_grad_kernel(x_ref, *refs):
    dqs, dks, dvs, (mix0, mix1, other_ref, half_ref, vec_ref) = refs[0:2], refs[2:4], refs[4:6], refs[6:11]
    refs = refs[11:]
    outs, halves, dwo_ref, sems = refs[:4], refs[4:6], refs[6], refs[7]
    core = my_core()
    half = half_ref[...].reshape(2, 2, BAND, 384)
    own = [half[:, m].reshape(2 * BAND, 384) for m in range(2)]
    dwo = dot_nn(mix0[...], own[0]) + dot_nn(mix1[...], own[1])
    dwo_ref[pl.ds(pl.multiple_of(core * 384, 384), 384)] = dwo.astype(BF16)
    other = [jnp.concatenate([half[1, m], half[0, m]], axis=0) for m in range(2)]
    dwo = dot_nn(other_ref[0], other[0]) + dot_nn(other_ref[1], other[1])
    dwo_ref[pl.ds(pl.multiple_of((1 - core) * 384, 384), 384)] = dwo.astype(BF16)

    def step(j, _):
        cols = pl.ds(pl.multiple_of(j * 384, 384), 384)
        x = [x_ref[:, m, :, cols].reshape(8 * BAND, 384) for m in range(2)]

        def total(refs, count):
            terms = [dot_tn(x[m][: count * BAND], refs[m][...].reshape(count * BAND, 384)) for m in range(2)]
            return (terms[0] + terms[1]).astype(BF16)

        dwq, dwk, dwv = total(dqs, 2), total(dks, 8), total(dvs, 8)
        for i in range(8):
            rows = slice(48 * i, 48 * i + 48)
            dwo = dwo_ref[pl.ds(pl.multiple_of(j * 384 + 48 * i, 16), 48)]
            place_rows(
                halves,
                j * 8 + i,
                jnp.concatenate([dwq[rows], dwk[rows]], axis=1),
                jnp.concatenate([dwv[rows], dwo], axis=1),
            )
        return 0

    lax.fori_loop(0, 2, step, 0)
    copies = flush(halves, outs, sems)
    for i, out in enumerate(outs):
        copies.append(pltpu.make_async_copy(vec_ref.at[i], out.at[pl.ds(384, 64)], sems.at[4 + i]))
    finish(copies)


def add(*terms):
    total = terms[0].astype(F32)
    for t in terms[1:]:
        total = total + t.astype(F32)
    return total


def first_hop(terms):
    return (terms[0], send(terms[1], Y), terms[2], send(terms[3], X))


def halves_of(g, near, rows):
    return jnp.concatenate(
        [g[192 * near : 192 * near + 192]] + ([g[384 + 32 * near : 416 + 32 * near]] if rows > 48 else [])
    )


def near_terms(hop, rows):
    return tuple(
        add(halves_of(hop[i], 1, rows), halves_of(hop[i + 1], 1, rows)).astype(BF16) for i in (0, 2)
    )


def hop_terms(low):
    return (send(low[0], X), send(low[1], Y))


def far_terms(hop, got, rows):
    return tuple(
        add(halves_of(hop[i], 0, rows), halves_of(hop[i + 1], 0, rows), got[i // 2]).astype(BF16) for i in (0, 2)
    )


def along_line(blocks):
    return (blocks[0], send(blocks[1], Z1), send(blocks[2], Z2), send(blocks[3], Z3))


def line_parts(halves, rows):
    return along_line(
        [
            jnp.concatenate(
                [
                    jnp.concatenate(
                        [h[48 * z : 48 * z + 48]] + ([h[192 + 8 * z : 200 + 8 * z]] if rows > 48 else []), axis=0
                    )
                    for h in halves
                ],
                axis=1,
            )
            for z in range(4)
        ]
    )


def block_parts(block):
    return along_line([block[48 * z : 48 * z + 48] for z in range(4)])


def flip(values, axis, index, bits):
    for bit in range(bits):
        shape = values.shape
        n = shape[axis]
        split = shape[:axis] + (n >> (bit + 1), 2, 1 << bit) + shape[axis + 1 :]
        swapped = jnp.flip(values.reshape(split), axis + 1).reshape(shape)
        values = jnp.where((index >> bit) & 1 == 1, swapped, values)
    return values


def per_device_paired(
    inputs, segments, w_query, b_query, w_key, w_value, b_value, w_output, b_output, gain_first,
    shift_first, w_inner, b_inner, w_outer, b_outer, gain_second, shift_second, cotangent,
):
    seq = lax.axis_index("seq")
    me, core = my_chip(), my_core()
    even = core == 0

    def in_order(mine, got, axis):
        return jnp.where(even, jnp.concatenate([mine, got], axis), jnp.concatenate([got, mine], axis))

    lanes = [b_query, b_value, b_output, gain_first, shift_first, b_outer, gain_second, shift_second, b_inner]
    mine, theirs, outer_rows = call(
        prepare_kernel, [((32, 1536), BF16), ((32, 1536), BF16), ((48, 1536), BF16)], 14
    )(w_query, w_key, w_value, w_output, *(v.reshape(1, -1) for v in lanes), w_outer)
    (square,) = call(chip_rows_kernel, [((56, 1536), BF16)], 2)(mine, send(theirs, CORE))
    wide = after(w_inner, mine).astype(BF16).reshape(24, CHIPS, 2, 96)
    mine, theirs = (
        jnp.where(even, wide[:, :, 0], wide[:, :, 1]).reshape(24, 1536),
        jnp.where(even, wide[:, :, 1], wide[:, :, 0]).reshape(24, 1536),
    )
    inner_rows = in_order(mine, send(theirs, CORE), 0)
    tokens, cot = inputs[:, 0], cotangent[:, 0]
    segs = segments[:, 0]
    segs = flip(segs.reshape(2, 8, BAND), 1, seq, 3)
    kseg = segs.reshape(2, 8 * BAND, 1)
    qseg = segs[:, :2].reshape(2, 1, 2 * BAND)

    other_tokens = send(tokens, CORE)
    hidden_rows = jnp.concatenate([inner_rows, outer_rows], axis=1)
    square, hidden_rows, other_tokens = after_both((square, hidden_rows, other_tokens), ())
    square = line(square)
    square = jnp.concatenate([p[:48] for p in square] + [p[48:] for p in square], axis=0)
    square, hidden_rows = after_both((square, hidden_rows), ())
    square = lines(square)
    hidden = line(hidden_rows)
    hidden, tokens = after_both((hidden, tokens), (kseg, qseg))
    hidden = [jnp.concatenate([h[:, c : c + 1536] for h in hidden], axis=0) for c in (0, 1536)]
    places = jnp.arange(CHIPS)
    order = ((places[:, None] ^ me) == places[None, :]).astype(BF16)
    line_order = ((places[:, None] ^ (me % 4)) == places[None, :]).astype(BF16)
    vecs = square.reshape(4, 224, 1536)[:, 192:].reshape(CHIPS, 8, 1536)[:, :2].reshape(CHIPS, 2 * 1536)
    vecs = dot_nn(line_order, vecs).reshape(CHIPS, 2, 12, 128)
    vec8 = vecs[:, :, :8, :24].transpose(2, 0, 1, 3).reshape(8, 768)
    b1 = jnp.where(even, vecs[:, 0, 8, :96], vecs[:, 1, 8, :96]).reshape(1, 1536)
    bq = jnp.where(even, vec8[0:1, :384], vec8[0:1, 384:])
    bv = jnp.where(even, vec8[1:2, :384], vec8[1:2, 384:])

    wo_rows = square[:, 1152:]
    wo_got = send(jnp.where(even, wo_rows[448:], wo_rows[:448]), CORE)

    near = x_then_y(*hidden)
    beside, second, opposite = send(tokens, Z1), send(tokens, Z2), send(tokens, MIDDLE)
    theirs = send(jnp.stack(after_both((beside, second, opposite, cot), (near, vec8, b1, bq, bv, wo_got))), CORE)
    slots = [tokens, other_tokens, beside, second, opposite, theirs]
    far = y_then_x(*hidden)

    slot_shape, head_shape = (2, BAND, 768), (2, BAND, 384)
    q, k, v, w_abs, x_all = call(
        project_kernel,
        [((2, *head_shape), BF16), ((8, *head_shape), BF16), ((8, *head_shape), BF16), ((768, 1536), BF16), ((8, *slot_shape), BF16)],
        9,
        in_specs=[IN_PLACE] * 7 + [IN_VMEM] * 2,
        scratch=[pltpu.SemaphoreType.DMA((40,))],
        cost=(2_800_000_000, 16_000_000),
    )(*slots, square, bq, bv)
    def attention_specs(m=None):
        micro = (lambda i: i) if m is None else (lambda i: m)
        q_spec = pl.BlockSpec((2, 1, BAND, 384), lambda i: (0, micro(i), 0, 0))
        k_spec = pl.BlockSpec((8, 1, BAND, 384), lambda i: (0, micro(i), 0, 0))
        t_spec = pl.BlockSpec((1, 384, 2 * BAND), lambda i: (micro(i), 0, 0))
        lse_spec = pl.BlockSpec((1, 8, 2 * BAND), lambda i: (micro(i), 0, 0))
        segs = [
            pl.BlockSpec((1, 8 * BAND, 1), lambda i: (micro(i), 0, 0)),
            pl.BlockSpec((1, 1, 2 * BAND), lambda i: (micro(i), 0, 0)),
        ]
        return ([q_spec, k_spec, k_spec], [t_spec, t_spec, lse_spec], segs)

    qkv_specs, mix_specs, seg_specs = attention_specs()
    near, (q, k, v) = after_both((near, (q, k, v)), far)
    both = y_then_x(*near)
    mix, mix_low, lse, branch, wo = call(
        attend_kernel,
        [((2, 384, 256), F32), ((2, 384, 256), BF16), ((2, 8, 256), F32), ((2, *slot_shape), BF16), ((384, 768), BF16)],
        7,
        grid=(2,),
        in_specs=qkv_specs + seg_specs + [IN_PLACE] * 2,
        out_specs=[
            *mix_specs,
            pl.BlockSpec((2, 1, BAND, 768), lambda i: (0, i, 0, 0)),
            pl.BlockSpec((384, 768), lambda i: (0, 0)),
        ],
        scratch=[
            pltpu.VMEM((1024, 256), F32),
            pltpu.VMEM((2, 1024, 256), F32),
            pltpu.VMEM((2, 1024, 256), BF16),
            pltpu.SemaphoreType.DMA((16,)),
        ],
        cost=(1_900_000_000, 10_000_000),
    )(q, k, v, kseg, qseg, square, wo_got)
    branch, both = after_both((branch, both), ())
    hidden = [g[i] for i in range(2) for g in (hidden, near, far, both)]
    branch_other = send(branch, CORE)
    n1, r1, hid_low, act, slope, f_own, w1, w2 = call(
        forward_kernel,
        [((512, 768), F32), ((512, 1), F32), ((512, 768), BF16), ((512, 1536), BF16), ((512, 1536), BF16), ((512, 768), BF16), ((768, 1536), BF16), ((1536, 768), BF16)],
        13,
        in_specs=[IN_PLACE] * 3 + [IN_VMEM] * 2 + [IN_PLACE] * 8,
        scratch=[pltpu.VMEM((2, *slot_shape), BF16)] * 3 + [pltpu.SemaphoreType.DMA((51,))],
        cost=(2_500_000_000, 16_000_000),
    )(x_all, branch, branch_other, vec8, b1, *hidden)
    mix_other = send(after(mix_low, n1), CORE)
    result, df, dz2, sums2 = call(
        middle_kernel,
        [((256, 768), BF16), ((512, 768), BF16), ((512, 768), F32), ((8, 768), F32)],
        6,
        in_specs=[IN_VMEM] * 4 + [IN_PLACE, IN_VMEM],
        scratch=[pltpu.VMEM(slot_shape, BF16), pltpu.SemaphoreType.DMA],
        cost=(50_000_000, 8_000_000),
    )(n1, f_own, send(f_own, CORE), cot, theirs, vec8)

    piece = [pltpu.VMEM((2, 384, 768), BF16)] * 2
    outer_terms = call(
        outer_grad_kernel,
        [((384, 768), BF16)] * 4,
        2,
        out_specs=[IN_PLACE] * 4,
        scratch=piece + [pltpu.SemaphoreType.DMA((4,))],
        cost=(1_200_000_000, 6_000_000),
    )(act, df)
    outer_hop = first_hop(outer_terms)
    du, dh_own, db1 = call(
        hidden_kernel,
        [((512, 1536), BF16), ((512, 768), BF16), ((1, 1536), F32)],
        4,
        cost=(2_400_000_000, 9_000_000),
    )(after(df, *outer_terms), slope, w1, w2)
    dh_other = send(dh_own, CORE)
    (inner_terms,) = call(inner_grad_kernel, [((768, 1536), BF16)], 2, cost=(1_200_000_000, 6_000_000))(hid_low, du)
    inner_block = lax.psum_scatter(inner_terms, "dp", scatter_dimension=0, tiled=True)
    outer_hop = after_both(outer_hop, (inner_terms,))
    outer_low = near_terms(outer_hop, 48)
    dh_own = after(dh_own, inner_terms, *outer_low)
    outer_sent = hop_terms(outer_low)
    dz1, do, do_half, da, sums1 = call(
        first_kernel,
        [((256, 768), F32), ((512, 768), BF16), ((512, 384), BF16), ((2, 384, 256), BF16), ((8, 768), F32)],
        7,
        cost=(300_000_000, 10_000_000),
    )(dz2, dh_own, dh_other, n1, r1, vec8, wo)

    def back(m, events):
        specs = attention_specs(m)
        shapes = [(2, BAND, 384), (8, BAND, 384), (8, BAND, 384), (4, BAND, 768), (4, BAND, 768)]
        return call(
            attend_back_kernel,
            [(shape, BF16) for shape in shapes] + [((8, 384), F32)],
            9,
            grid=(1,),
            in_specs=specs[0] + specs[1] + specs[2] + [pl.BlockSpec((768, 1536), lambda i: (0, 0))],
            out_specs=[pl.BlockSpec(shape, lambda i: (0, 0, 0)) for shape in shapes] + [pl.BlockSpec((8, 384), lambda i: (0, 0))],
            scratch=[pltpu.VMEM((1024, 256), F32)],
            cost=(3_400_000_000, 10_000_000),
        )(q, k, v, mix, after(da, *events), lse, kseg, qseg, w_abs)

    def core_sums(own, got):
        return [add(own[z], got[z]) if z == 0 else add(own[z], got[z]).astype(BF16) for z in range(4)]

    def line_sums(sums):
        return (sums[0], send(sums[1], Z1), send(sums[2], Z2), send(sums[3], MIDDLE))

    outer_hop, outer_sent = after_both((outer_hop, outer_sent), (da,))
    outer_half = far_terms(outer_hop, outer_sent, 48)
    *grads0, dx0, dx_send, sums_q0 = back(0, outer_half)
    outer_parts = line_parts(outer_half, 48)
    got0 = send(dx_send, CORE)
    *grads1, dx1, dx_send, sums_q1 = back(1, (dx0,))
    outer_parts, got0, dx0 = after_both((outer_parts, got0, dx0), grads1[:1])
    got1 = send(dx_send, CORE)
    low0 = core_sums(dx0, got0)
    grads1, _ = lax.optimization_barrier((grads1, (outer_parts, low0, inner_block)))
    inner_parts = block_parts(inner_block)
    sent0 = line_sums(low0)

    def widen(value):
        zero = jnp.zeros_like(value)
        return in_order(value, zero, 1)

    sums_q = sums_q0 + sums_q1
    eight = jnp.concatenate(
        [widen(sums_q[0:1]), widen(sums_q[1:2]), sums1[2:3], sums1[0:1], sums1[1:2], sums2[2:3], sums2[0:1], sums2[1:2]], 0
    )
    eight = jnp.pad(eight.reshape(8, CHIPS, 2, 24), ((0, 0), (0, 0), (0, 0), (0, 104))).transpose(1, 2, 0, 3)
    db1 = jnp.where(jnp.arange(2)[None, :, None] == core, db1.reshape(CHIPS, 1, 96), 0.0)
    db1 = jnp.pad(db1, ((0, 0), (0, 0), (0, 416)))
    vec_grads = jnp.concatenate([eight.reshape(CHIPS, 2, 1024), db1], axis=2).reshape(CHIPS, 3072)
    vec_grads = dot_nn(order, vec_grads.astype(BF16)).astype(BF16).reshape(2, 2, 4, 2, 1536)
    vec_grads = jnp.pad(vec_grads, ((0, 0), (0, 0), (0, 0), (0, 6), (0, 0)))
    vec_first = vec_grads[..., :768].reshape(2, 64, 768)
    vec_second = vec_grads[..., 768:].transpose(1, 0, 2, 3, 4).reshape(2, 64, 768)
    square_terms = call(
        projection_grad_kernel,
        [((448, 768), BF16)] * 4,
        12,
        out_specs=[IN_PLACE] * 4,
        scratch=piece + [pltpu.VMEM((768, 384), BF16), pltpu.SemaphoreType.DMA((8,))],
        cost=(3_300_000_000, 12_000_000),
    )(x_all, grads0[0], grads1[0], grads0[1], grads1[1], grads0[2], grads1[2], mix_low[0], mix_low[1], mix_other, do_half, jnp.concatenate([vec_first, vec_second]))
    square_hop = first_hop(square_terms)
    inner_parts, got1 = after_both((inner_parts, got1), square_terms)
    sent1 = line_sums(core_sums(dx1, got1))
    square_hop, sent0 = after_both((square_hop, sent0), ())
    square_sent = hop_terms(near_terms(square_hop, 56))
    square_half = far_terms(square_hop, square_sent, 56)
    square_parts = line_parts(square_half, 56)

    outer_total = add(*outer_parts)
    inner_total = add(*inner_parts)
    grad_outer = jnp.concatenate([outer_total[:, :768], outer_total[:, 768:]], axis=0)
    keep = jnp.where(even, inner_total[:24], inner_total[24:])
    got = send(jnp.where(even, inner_total[24:], inner_total[:24]).astype(BF16), CORE).astype(F32)
    grad_inner = in_order(keep.reshape(24, CHIPS, 1, 96), got.reshape(24, CHIPS, 1, 96), 2).reshape(24, 3072)
    keep, other = call(owner_kernel, [((32, 1536), F32), ((32, 1536), BF16)], 5)(*square_half, *square_parts[1:])
    grads = call(
        result_kernel,
        [((24, 768), F32)] * 4 + [((1, 24), F32)] * 8 + [((1, 96), F32)],
        2,
    )(keep, send(other, CORE))
    squares, small = grads[:4], [g.reshape(-1) for g in grads[4:]]
    dz1 = dz1.reshape(slot_shape)
    grad_tokens = jnp.stack([add(dz1[m], *sent).astype(BF16) for m, sent in enumerate((sent0, sent1))])
    return (
        result.reshape(2, 1, BAND, 768), grad_tokens[:, None],
        squares[0], small[0], squares[1], squares[2], small[1], squares[3], small[2],
        small[3], small[4], grad_inner, small[8], grad_outer, small[5], small[6], small[7],
    )


def solution(mesh):
    in_specs = (
        P(None, "dp", "seq", None),
        P(None, "dp", None),
        P(("dp", "seq"), None),
        P(("dp", "seq")),
        P(("dp", "seq"), None),
        P(("dp", "seq"), None),
        P(("dp", "seq")),
        P(("dp", "seq"), None),
        P(("dp", "seq")),
        P(("dp", "seq")),
        P(("dp", "seq")),
        P(("dp", "seq"), None),
        P(("dp", "seq")),
        P(("dp", "seq"), None),
        P(("dp", "seq")),
        P(("dp", "seq")),
        P(("dp", "seq")),
        P(None, "dp", "seq", None),
    )
    out_specs = (
        P(None, "dp", "seq", None),
        P(None, "dp", "seq", None),
        P(("dp", "seq"), None),
        P(("dp", "seq")),
        P(("dp", "seq"), None),
        P(("dp", "seq"), None),
        P(("dp", "seq")),
        P(("dp", "seq"), None),
        P(("dp", "seq")),
        P(("dp", "seq")),
        P(("dp", "seq")),
        P(("dp", "seq"), None),
        P(("dp", "seq")),
        P(("dp", "seq"), None),
        P(("dp", "seq")),
        P(("dp", "seq")),
        P(("dp", "seq")),
    )
    paired = (mesh.shape["dp"], mesh.shape["seq"]) == (4, 8)
    return jax.shard_map(
        per_device_paired if paired else per_device, mesh=mesh, in_specs=in_specs, out_specs=out_specs, check_vma=False
    )
```

```python
import math

import jax
import jax.numpy as jnp
from jax import lax
from jax.experimental import pallas as pl
from jax.experimental.pallas import tpu as pltpu
from jax.sharding import PartitionSpec as P

HEADS = 12
HEAD_DIM = 64


def narrow(masters):
    return tuple((item.astype(jnp.bfloat16) for item in masters))


def fetch_forward(masters):
    lowered = narrow(masters)
    return (
        lax.all_gather(lowered[0], ("dp", "seq"), axis=0, tiled=True),
        lax.all_gather(lowered[1], ("dp", "seq"), axis=0, tiled=True),
        lax.all_gather(lowered[2], ("dp", "seq"), axis=0, tiled=True),
        lax.all_gather(lowered[3], ("dp", "seq"), axis=0, tiled=True),
        lax.all_gather(lowered[4], ("dp", "seq"), axis=0, tiled=True),
        lax.all_gather(lowered[5], ("dp", "seq"), axis=0, tiled=True),
        lax.all_gather(lowered[6], ("dp", "seq"), axis=0, tiled=True),
        lax.all_gather(lowered[7], ("dp", "seq"), axis=0, tiled=True),
        lax.all_gather(lowered[8], ("dp", "seq"), axis=0, tiled=True),
        lax.all_gather(lowered[9], ("dp", "seq"), axis=0, tiled=True),
        lax.all_gather(lowered[10], ("dp", "seq"), axis=0, tiled=True),
        lax.all_gather(lowered[11], ("dp", "seq"), axis=0, tiled=True),
        lax.all_gather(lowered[12], ("dp", "seq"), axis=0, tiled=True),
        lax.all_gather(lowered[13], ("dp", "seq"), axis=0, tiled=True),
        lax.all_gather(lowered[14], ("dp", "seq"), axis=0, tiled=True),
    )


def fetch_backward(masters):
    lowered = narrow(masters)
    return (
        lax.all_gather(lowered[0], ("dp", "seq"), axis=0, tiled=True),
        lax.all_gather(lowered[1], ("dp", "seq"), axis=0, tiled=True),
        lax.all_gather(lowered[2], ("dp", "seq"), axis=0, tiled=True),
        lax.all_gather(lowered[3], ("dp", "seq"), axis=0, tiled=True),
        lax.all_gather(lowered[4], ("dp", "seq"), axis=0, tiled=True),
        lax.all_gather(lowered[5], ("dp", "seq"), axis=0, tiled=True),
        lax.all_gather(lowered[6], ("dp", "seq"), axis=0, tiled=True),
        lax.all_gather(lowered[7], ("dp", "seq"), axis=0, tiled=True),
        lax.all_gather(lowered[8], ("dp", "seq"), axis=0, tiled=True),
        lax.all_gather(lowered[9], ("dp", "seq"), axis=0, tiled=True),
        lax.all_gather(lowered[10], ("dp", "seq"), axis=0, tiled=True),
        lax.all_gather(lowered[11], ("dp", "seq"), axis=0, tiled=True),
        lax.all_gather(lowered[12], ("dp", "seq"), axis=0, tiled=True),
        lax.all_gather(lowered[13], ("dp", "seq"), axis=0, tiled=True),
        lax.all_gather(lowered[14], ("dp", "seq"), axis=0, tiled=True),
    )


def sum_owners(terms):
    return (
        lax.psum_scatter(terms[0], ("dp", "seq"), scatter_dimension=0, tiled=True),
        lax.psum_scatter(terms[1], ("dp", "seq"), scatter_dimension=0, tiled=True),
        lax.psum_scatter(terms[2], ("dp", "seq"), scatter_dimension=0, tiled=True),
        lax.psum_scatter(terms[3], ("dp", "seq"), scatter_dimension=0, tiled=True),
        lax.psum_scatter(terms[4], ("dp", "seq"), scatter_dimension=0, tiled=True),
        lax.psum_scatter(terms[5], ("dp", "seq"), scatter_dimension=0, tiled=True),
        lax.psum_scatter(terms[6], ("dp", "seq"), scatter_dimension=0, tiled=True),
        lax.psum_scatter(terms[7], ("dp", "seq"), scatter_dimension=0, tiled=True),
        lax.psum_scatter(terms[8], ("dp", "seq"), scatter_dimension=0, tiled=True),
        lax.psum_scatter(terms[9], ("dp", "seq"), scatter_dimension=0, tiled=True),
        lax.psum_scatter(terms[10], ("dp", "seq"), scatter_dimension=0, tiled=True),
        lax.psum_scatter(terms[11], ("dp", "seq"), scatter_dimension=0, tiled=True),
        lax.psum_scatter(terms[12], ("dp", "seq"), scatter_dimension=0, tiled=True),
        lax.psum_scatter(terms[13], ("dp", "seq"), scatter_dimension=0, tiled=True),
        lax.psum_scatter(terms[14], ("dp", "seq"), scatter_dimension=0, tiled=True),
    )


def layer_norm(z, gain, shift):
    mean = jnp.mean(z, axis=-1, keepdims=True)
    centered = z - mean
    rstd = lax.rsqrt(jnp.mean(centered * centered, axis=-1, keepdims=True) + 1e-05)
    normed = centered * rstd
    return (normed * gain + shift, normed, rstd)


def norm_back(grad, normed, rstd, gain):
    scaled = grad * gain
    inner = (
        scaled
        - jnp.mean(scaled, axis=-1, keepdims=True)
        - normed * jnp.mean(scaled * normed, axis=-1, keepdims=True)
    )
    return (rstd * inner, jnp.sum(grad * normed, axis=0), jnp.sum(grad, axis=0))


def gelu_exact(value):
    return jax.nn.gelu(value, approximate=False)


def key_blocks(keys_all, values_all, seg_row):
    length = keys_all.shape[0]
    width = math.gcd(length, 1024)
    count = length // width
    keys_split = keys_all.reshape(count, width, HEADS, HEAD_DIM)
    values_split = values_all.reshape(count, width, HEADS, HEAD_DIM)
    return (keys_split, values_split, seg_row.reshape(count, width))


def block_scores(queries, keys, query_seg, key_seg):
    scores = jnp.einsum("qhd,khd->hqk", queries, keys, preferred_element_type=jnp.float32) * 0.125
    same = (query_seg[:, None] == key_seg[None, :])[None]
    return jnp.where(same, scores, -1e30)


def attend(queries, keys_all, values_all, seg_row, query_seg):
    rows = queries.shape[0]
    query_h = queries.reshape(rows, HEADS, HEAD_DIM)
    keys_split, values_split, seg_split = key_blocks(keys_all, values_all, seg_row)

    def first_pass(carry, block):
        top, total = carry
        keys, key_seg = block
        scores = block_scores(query_h, keys, query_seg, key_seg)
        new_top = jnp.maximum(top, jnp.max(scores, axis=-1))
        total = total * jnp.exp(top - new_top) + jnp.sum(
            jnp.exp(scores - new_top[..., None]), axis=-1
        )
        return ((new_top, total), None)

    start = (jnp.full((HEADS, rows), -1e30, jnp.float32), jnp.zeros((HEADS, rows), jnp.float32))
    (top, total), _ = lax.scan(first_pass, start, (keys_split, seg_split))
    lse = top + jnp.log(total)

    def second_pass(acc, block):
        keys, values, key_seg = block
        scores = block_scores(query_h, keys, query_seg, key_seg)
        probs = jnp.exp(scores - lse[..., None]).astype(jnp.bfloat16)
        return (
            acc + jnp.einsum("hqk,khd->qhd", probs, values, preferred_element_type=jnp.float32),
            None,
        )

    mixed, _ = lax.scan(
        second_pass,
        jnp.zeros((rows, HEADS, HEAD_DIM), jnp.float32),
        (keys_split, values_split, seg_split),
    )
    return (lse, mixed.reshape(rows, HEADS * HEAD_DIM))


def attend_back(queries, grad_mixed, lse, delta, keys_all, values_all, seg_row, query_seg):
    rows = queries.shape[0]
    query_h = queries.reshape(rows, HEADS, HEAD_DIM)
    grad_h = grad_mixed.reshape(rows, HEADS, HEAD_DIM)
    keys_split, values_split, seg_split = key_blocks(keys_all, values_all, seg_row)

    def step(grad_query, block):
        keys, values, key_seg = block
        scores = block_scores(query_h, keys, query_seg, key_seg)
        probs = jnp.exp(scores - lse[..., None])
        grad_probs = jnp.einsum("qhd,khd->hqk", grad_h, values, preferred_element_type=jnp.float32)
        grad_scores = (probs * (grad_probs - delta[..., None])).astype(jnp.bfloat16)
        grad_query = grad_query + jnp.einsum(
            "hqk,khd->qhd", grad_scores, keys, preferred_element_type=jnp.float32
        )
        grad_keys = (
            jnp.einsum("hqk,qhd->khd", grad_scores, query_h, preferred_element_type=jnp.float32)
            * 0.125
        )
        grad_values = jnp.einsum(
            "hqk,qhd->khd", probs.astype(jnp.bfloat16), grad_h, preferred_element_type=jnp.float32
        )
        width = keys.shape[0]
        joined = jnp.concatenate(
            [
                grad_keys.reshape(width, HEADS * HEAD_DIM),
                grad_values.reshape(width, HEADS * HEAD_DIM),
            ],
            axis=-1,
        )
        return (grad_query, joined)

    grad_query, joined = lax.scan(
        step, jnp.zeros((rows, HEADS, HEAD_DIM), jnp.float32), (keys_split, values_split, seg_split)
    )
    grad_query = (grad_query * 0.125).reshape(rows, HEADS * HEAD_DIM)
    return (grad_query, joined.reshape(keys_all.shape[0], 2 * HEADS * HEAD_DIM))


def outer_sum(left, right):
    return jnp.einsum("tf,tg->fg", left, right, preferred_element_type=jnp.float32)


def times_transposed(left, weight):
    return jnp.einsum("tg,fg->tf", left, weight, preferred_element_type=jnp.float32)


def column_sum(value):
    return jnp.sum(value.astype(jnp.float32), axis=0)


def per_device(
    inputs,
    segments,
    w_query,
    b_query,
    w_key,
    w_value,
    b_value,
    w_output,
    b_output,
    gain_first,
    shift_first,
    w_inner,
    b_inner,
    w_outer,
    b_outer,
    gain_second,
    shift_second,
    cotangent,
):
    masters = (
        w_query,
        b_query,
        w_key,
        w_value,
        b_value,
        w_output,
        b_output,
        gain_first,
        shift_first,
        w_inner,
        b_inner,
        w_outer,
        b_outer,
        gain_second,
        shift_second,
    )
    rows = inputs.shape[2]
    offset = lax.axis_index("seq") * rows
    results = []
    grad_rows = []
    totals = None
    for micro in range(inputs.shape[0]):
        tokens = inputs[micro, 0]
        seg_row = segments[micro, 0]
        query_seg = lax.dynamic_slice_in_dim(seg_row, offset, rows)
        full = fetch_forward(masters)
        wq, bq, wk, wv, bv, wo, bo, g1, s1, w1, b1, w2, b2, g2, s2 = full
        g1f, s1f, g2f, s2f = (
            g1.astype(jnp.float32),
            s1.astype(jnp.float32),
            g2.astype(jnp.float32),
            s2.astype(jnp.float32),
        )
        queries = (
            jnp.dot(tokens, wq, preferred_element_type=jnp.float32) + bq.astype(jnp.float32)
        ).astype(jnp.bfloat16)
        keys = jnp.dot(tokens, wk, preferred_element_type=jnp.float32).astype(jnp.bfloat16)
        values = (
            jnp.dot(tokens, wv, preferred_element_type=jnp.float32) + bv.astype(jnp.float32)
        ).astype(jnp.bfloat16)
        keys_all, values_all = (
            lax.all_gather(keys, "seq", axis=0, tiled=True),
            lax.all_gather(values, "seq", axis=0, tiled=True),
        )
        lse, mixed = attend(queries, keys_all, values_all, seg_row, query_seg)
        mixed_low = mixed.astype(jnp.bfloat16)
        branch = jnp.dot(mixed_low, wo, preferred_element_type=jnp.float32) + bo.astype(jnp.float32)
        hidden, normed_first, rstd_first = layer_norm(tokens.astype(jnp.float32) + branch, g1f, s1f)
        hidden_low = hidden.astype(jnp.bfloat16)
        inner = jnp.dot(hidden_low, w1, preferred_element_type=jnp.float32) + b1.astype(jnp.float32)
        active, gelu_pull = jax.vjp(gelu_exact, inner)
        active_low = active.astype(jnp.bfloat16)
        outer = jnp.dot(active_low, w2, preferred_element_type=jnp.float32) + b2.astype(jnp.float32)
        result, normed_second, rstd_second = layer_norm(hidden + outer, g2f, s2f)
        results.append(result.astype(jnp.bfloat16))
        wq, bq, wk, wv, bv, wo, bo, g1, s1, w1, b1, w2, b2, g2, s2 = fetch_backward(masters)
        keys_all, values_all = (
            lax.all_gather(keys, "seq", axis=0, tiled=True),
            lax.all_gather(values, "seq", axis=0, tiled=True),
        )
        grad_out = cotangent[micro, 0].astype(jnp.float32)
        grad_z2, grad_g2, grad_s2 = norm_back(grad_out, normed_second, rstd_second, g2f)
        grad_outer = grad_z2.astype(jnp.bfloat16)
        grad_w2 = outer_sum(active_low, grad_outer)
        grad_b2 = column_sum(grad_outer)
        grad_active = times_transposed(grad_outer, w2)
        grad_inner = gelu_pull(grad_active)[0].astype(jnp.bfloat16)
        grad_w1 = outer_sum(hidden_low, grad_inner)
        grad_b1 = column_sum(grad_inner)
        grad_hidden = times_transposed(grad_inner, w1) + grad_z2
        grad_z1, grad_g1, grad_s1 = norm_back(grad_hidden, normed_first, rstd_first, g1f)
        grad_branch = grad_z1.astype(jnp.bfloat16)
        grad_wo = outer_sum(mixed_low, grad_branch)
        grad_bo = column_sum(grad_branch)
        grad_mixed = times_transposed(grad_branch, wo).astype(jnp.bfloat16)
        delta = jnp.sum(
            (grad_mixed.astype(jnp.float32) * mixed).reshape(rows, HEADS, HEAD_DIM), axis=-1
        ).T
        grad_query, joined = attend_back(
            queries, grad_mixed, lse, delta, keys_all, values_all, seg_row, query_seg
        )
        summed = lax.psum_scatter(
            joined.astype(jnp.bfloat16), "seq", scatter_dimension=0, tiled=True
        ).astype(jnp.float32)
        width = summed.shape[1] // 2
        grad_keys = summed[:, :width].astype(jnp.bfloat16)
        grad_values = summed[:, width:].astype(jnp.bfloat16)
        grad_query = grad_query.astype(jnp.bfloat16)
        grad_wq = outer_sum(tokens, grad_query)
        grad_wk = outer_sum(tokens, grad_keys)
        grad_wv = outer_sum(tokens, grad_values)
        grad_bq = column_sum(grad_query)
        grad_bv = column_sum(grad_values)
        grad_tokens = (
            times_transposed(grad_query, wq)
            + times_transposed(grad_keys, wk)
            + times_transposed(grad_values, wv)
            + grad_z1
        )
        grad_rows.append(grad_tokens.astype(jnp.bfloat16))
        terms = (
            grad_wq,
            grad_bq,
            grad_wk,
            grad_wv,
            grad_bv,
            grad_wo,
            grad_bo,
            grad_g1,
            grad_s1,
            grad_w1,
            grad_b1,
            grad_w2,
            grad_b2,
            grad_g2,
            grad_s2,
        )
        totals = terms if totals is None else tuple((old + new for old, new in zip(totals, terms)))
    owned = sum_owners(totals)
    outputs = jnp.stack(results)[:, None]
    grad_inputs = jnp.stack(grad_rows)[:, None]
    return (
        outputs,
        grad_inputs,
        owned[0],
        owned[1],
        owned[2],
        owned[3],
        owned[4],
        owned[5],
        owned[6],
        owned[7],
        owned[8],
        owned[9],
        owned[10],
        owned[11],
        owned[12],
        owned[13],
        owned[14],
    )


BOTH = ("dp", "seq")
CHIPS = 16
BAND = 128
F32 = jnp.float32
BF16 = jnp.bfloat16
IN_VMEM = pl.BlockSpec(memory_space=pltpu.VMEM)
IN_PLACE = pl.BlockSpec(memory_space=pl.ANY)


def pairs(dp_bits, seq_bits, keep=lambda dp, seq: True):
    return [
        (dp * 8 + seq, (dp ^ dp_bits) * 8 + (seq ^ seq_bits))
        for dp in range(4)
        for seq in range(8)
        if keep(dp, seq)
    ]


CORE, Z1, Z2, Z3 = pairs(0, 1), pairs(0, 2), pairs(0, 4), pairs(0, 6)
X, Y = pairs(1, 0), pairs(2, 0)
MIDDLE = pairs(0, 6, lambda dp, seq: seq // 2 in (1, 2))


def send(value, route):
    return lax.ppermute(value, BOTH, route)


def after(value, *events):
    return lax.optimization_barrier((value, *events))[0]


def after_both(values, events):
    return lax.optimization_barrier((tuple(values), tuple(events)))[0]


def my_chip():
    return lax.axis_index("dp") * 4 + lax.axis_index("seq") // 2


def my_core():
    return lax.axis_index("seq") % 2


def dot_nn(a, b):
    return lax.dot_general(a, b, (((1,), (0,)), ((), ())), preferred_element_type=F32)


def dot_nt(a, b):
    return lax.dot_general(a, b, (((1,), (1,)), ((), ())), preferred_element_type=F32)


def dot_tn(a, b):
    return lax.dot_general(a, b, (((0,), (0,)), ((), ())), preferred_element_type=F32)


def call(body, outs, n_in, in_specs=None, out_specs=None, scratch=(), grid=None, cost=None):
    kwargs = {} if grid is None else {"grid": grid}
    return pl.pallas_call(
        body,
        out_shape=[jax.ShapeDtypeStruct(s, d) for s, d in outs],
        in_specs=in_specs or [IN_VMEM] * n_in,
        out_specs=out_specs or [IN_VMEM] * len(outs),
        scratch_shapes=list(scratch),
        cost_estimate=pl.CostEstimate(flops=cost[0], bytes_accessed=cost[1], transcendentals=0)
        if cost
        else None,
        **kwargs,
    )


def line(block):
    return [block, send(block, Z1), send(block, Z2), send(block, Z3)]


def lines(block):
    return lax.all_gather(block, "dp", axis=0, tiled=True)


def placed(rows, target, sems, base):
    me = my_chip() % 4
    copies = []
    for i in range(CHIPS):
        at = pl.multiple_of(((i // 4) * 4 + ((i % 4) ^ me)) * 48, 16)
        copies.append(
            pltpu.make_async_copy(
                rows.at[pl.ds((i // 4) * 224 + (i % 4) * 48, 48)], target.at[pl.ds(at, 48)], sems.at[base + i]
            )
        )
    return copies


def x_then_y(first, second):
    return (send(first, X), send(second, Y))


def y_then_x(first, second):
    return (send(first, Y), send(second, X))


def placed_hidden(groups, targets, sems):
    me = my_chip()
    copies = ([], [])
    for i, group in enumerate(groups):
        which, far, near = i // 4, (i // 2) % 2, i % 2
        for z in range(4):
            b = (far * (8, 4)[which] + near * (4, 8)[which] + z) ^ me
            for part in range(1 + which):
                cols = pl.ds(768 * part, 768) if which else pl.ds(0, 1536)
                at = pl.multiple_of(b * (48, 96)[which] + 48 * part, 16)
                sem = sems.at[16 * which + len(copies[which])]
                rows = group.at[pl.ds(z * 48, 48), cols]
                copies[which].append(pltpu.make_async_copy(rows, targets[which].at[pl.ds(at, 48)], sem))
    return copies


def prepare_kernel(*refs):
    weights, vecs, outer_ref = refs[0:4], refs[4:13], refs[13]
    mine_ref, theirs_ref, rows_ref = refs[14:]
    even = my_core() == 0
    theirs_ref[24:32] = jnp.zeros((8, 1536), BF16)
    for i, ref in enumerate(weights):
        w, cols = ref[...].astype(BF16), slice(384 * i, 384 * i + 384)
        mine_ref[0:24, cols] = jnp.where(even, w[:, :384], w[:, 384:])
        theirs_ref[0:24, cols] = jnp.where(even, w[:, 384:], w[:, :384])
    pieces = []
    for ref in vecs:
        pieces += [ref[...], jnp.zeros((1, 128 - ref.shape[1]), F32)]
    row = jnp.concatenate(pieces + [jnp.zeros((1, 384), F32)], axis=1)
    row = jnp.where(lax.broadcasted_iota(jnp.int32, (8, 1536), 0) == 0, row, 0.0).astype(BF16)
    mine_ref[24:32] = row
    theirs_ref[24:32] = row
    rows_ref[:, 0:768] = outer_ref[0:48].astype(BF16)
    rows_ref[:, 768:1536] = outer_ref[48:96].astype(BF16)


def chip_rows_kernel(mine_ref, got_ref, out_ref):
    even = my_core() == 0
    mine, got = mine_ref[...].astype(F32), got_ref[...].astype(F32)
    out_ref[0:24] = jnp.where(even, mine[:24], got[:24]).astype(BF16)
    out_ref[24:48] = jnp.where(even, got[:24], mine[:24]).astype(BF16)
    first = jnp.where(even, mine[24:32], got[24:32])
    second = jnp.where(even, got[24:32], mine[24:32])
    row = lax.broadcasted_iota(jnp.int32, (8, 1536), 0)
    out_ref[48:56] = jnp.where(row == 1, second[0:1], jnp.where(row == 0, first[0:1], 0.0)).astype(BF16)


def owner_kernel(first_ref, second_ref, *refs):
    parts, (keep_ref, other_ref) = refs[:3], refs[3:]
    even = my_core() == 0
    for c, ref in ((0, first_ref), (768, second_ref)):
        cols = slice(c, c + 768)
        a, b, d = (p[:, cols].astype(F32) for p in parts)
        rows = ref[0:48].astype(F32) + a[:48] + b[:48] + d[:48]
        keep_ref[0:24, cols] = jnp.where(even, rows[:24], rows[24:])
        other_ref[0:24, cols] = jnp.where(even, rows[24:], rows[:24]).astype(BF16)
        vec = ref[192:200].astype(F32) + a[48:56] + b[48:56] + d[48:56]
        zero = jnp.zeros((7, 768), F32)
        keep_ref[24:32, cols] = jnp.concatenate([jnp.where(even, vec[0:1], vec[1:2]), zero], axis=0)
        other_ref[24:32, cols] = jnp.concatenate([jnp.where(even, vec[1:2], vec[0:1]), zero], axis=0).astype(BF16)


def result_kernel(keep_ref, got_ref, *refs):
    outs, vecs = refs[:4], refs[4:]
    even = my_core() == 0
    for i, ref in enumerate(outs):
        cols = slice(384 * i, 384 * i + 384)
        keep, got = keep_ref[0:24, cols], got_ref[0:24, cols].astype(F32)
        ref[:, 0:384] = jnp.where(even, keep, got)
        ref[:, 384:768] = jnp.where(even, got, keep)
    vec = keep_ref[24:25] + got_ref[24:32].astype(F32)[0:1]
    for i, ref in enumerate(vecs):
        ref[...] = vec[:, 128 * i : 128 * i + ref.shape[1]]


def project_kernel(*refs):
    xs, theirs, rows = refs[0:5], refs[5], refs[6]
    bq_ref, bv_ref = refs[7:9]
    q_ref, k_out, v_out, w_out, x_out, k_ref, v_ref, w_ref, x_ref, sems = refs[9:]
    stores = [pltpu.make_async_copy(w_ref, w_out, sems.at[40]), pltpu.make_async_copy(x_ref, x_out, sems.at[41])]
    slots = [*zip((0, 1, 2, 4, 6), xs), *((2 * z + 3, theirs.at[z]) for z in range(3))]
    loads = [pltpu.make_async_copy(ref, x_ref.at[s], sems.at[32 + s]) for s, ref in slots]
    loads += placed(rows, w_ref, sems, 0)
    for c in loads:
        c.start()
    for c in loads:
        c.wait()
    for c in stores:
        c.start()
    bq, bv = bq_ref[...], bv_ref[...]

    q = (dot_nn(x_ref[0:2].reshape(4 * BAND, 768), w_ref[:, 0:384]) + bq).astype(BF16) * jnp.asarray(0.125, BF16)
    q_ref[...] = q.reshape(2, 2, BAND, 384)

    def slots4(i, _):
        four = pl.ds(4 * i, 4)
        both = dot_nn(x_ref[four].reshape(8 * BAND, 768), w_ref[:, 384:1152])
        k_ref[four] = both[:, :384].astype(BF16).reshape(4, 2, BAND, 384)
        v_ref[four] = (both[:, 384:] + bv).astype(BF16).reshape(4, 2, BAND, 384)
        for n, (src, dst) in enumerate(((k_ref, k_out), (v_ref, v_out))):
            pltpu.make_async_copy(src.at[four], dst.at[four], sems.at[42 + 2 * i + n]).start()
        return 0

    lax.fori_loop(0, 2, slots4, 0)
    for i in range(2):
        for n, (src, dst) in enumerate(((k_ref, k_out), (v_ref, v_out))):
            four = pl.ds(4 * i, 4)
            stores.append(pltpu.make_async_copy(src.at[four], dst.at[four], sems.at[42 + 2 * i + n]))
    for c in stores:
        c.wait()


def fill_mask(mask_ref, kseg_ref, qseg_ref):
    for c in range(4):
        rows = slice(256 * c, 256 * c + 256)
        mask_ref[rows] = jnp.where(kseg_ref[0, rows] == qseg_ref[0], 0.0, -1e30)


def attend_kernel(
    q_ref, k_ref, v_ref, kseg_ref, qseg_ref, rows_ref, got_ref,
    mix_ref, low_ref, lse_ref, out_ref, wo_ref, mask_ref, score_ref, weight_ref, sems,
):
    core, me = my_core(), my_chip() % 4
    first = pl.program_id(0) == 0
    loads = []
    for i in range(8):
        at = pl.ds(pl.multiple_of((i // 4) * 192 + ((i % 4) ^ me) * 48, 16), 48)
        row = (i // 4) * 224 + (i % 4) * 48
        mine = rows_ref.at[pl.ds(pl.multiple_of(core * 448 + row, 16), 48), pl.ds(1152, 384)]
        for j, src in enumerate((mine, got_ref.at[pl.ds(row, 48)])):
            cols = pl.ds(pl.multiple_of((core if j == 0 else 1 - core) * 384, 128), 384)
            loads.append(pltpu.make_async_copy(src, wo_ref.at[at, cols], sems.at[2 * i + j]))

    @pl.when(first)
    def _():
        for c in loads:
            c.start()

    fill_mask(mask_ref, kseg_ref, qseg_ref)

    def pair(j, _):
        both = pl.ds(pl.multiple_of(128 * j, 128), 128)
        q2 = q_ref[:, 0, :, both].reshape(2 * BAND, 128)

        def score(c, tops):
            rows = pl.ds(pl.multiple_of(256 * c, 256), 256)
            k2 = k_ref[pl.ds(2 * c, 2), 0, :, both].reshape(256, 128)
            new = []
            for h in range(2):
                cols = slice(64 * h, 64 * h + 64)
                s = dot_nt(k2[:, cols], q2[:, cols]) + mask_ref[rows]
                score_ref[h, rows] = s
                new.append(jnp.maximum(tops[h], jnp.max(s, axis=0, keepdims=True)))
            return tuple(new)

        tops = lax.fori_loop(0, 4, score, (jnp.full((1, 256), -1e30, F32),) * 2, unroll=True)

        def weigh(c, totals):
            rows = pl.ds(pl.multiple_of(256 * c, 256), 256)
            new = []
            for h in range(2):
                e = jnp.exp(score_ref[h, rows] - tops[h])
                weight_ref[h, rows] = e.astype(BF16)
                new.append(totals[h] + jnp.sum(e, axis=0, keepdims=True))
            return tuple(new)

        totals = lax.fori_loop(0, 4, weigh, (jnp.zeros((1, 256), F32),) * 2, unroll=True)
        v2 = v_ref[:, 0, :, both].reshape(8 * BAND, 128)
        for h in range(2):
            mixed = dot_tn(v2[:, 64 * h : 64 * h + 64], weight_ref[h]) * (1.0 / totals[h])
            rows = pl.ds(pl.multiple_of(128 * j + 64 * h, 64), 64)
            mix_ref[0, rows] = mixed
            low_ref[0, rows] = mixed.astype(BF16)
            lse_ref[0, pl.ds(2 * j + h, 1)] = tops[h] + jnp.log(totals[h])
        return 0

    lax.fori_loop(0, 3, pair, 0)

    @pl.when(first)
    def _():
        for c in loads:
            c.wait()

    out_ref[:, 0] = dot_tn(low_ref[0], wo_ref[...]).astype(BF16).reshape(2, BAND, 768)


def norm(z):
    mean = jnp.mean(z, axis=-1, keepdims=True)
    centered = z - mean
    rstd = lax.rsqrt(jnp.mean(centered * centered, axis=-1, keepdims=True) + 1e-05)
    return (centered * rstd, rstd)


def norm_grad(grad, normed, rstd, gain):
    scaled = grad * gain
    return rstd * (
        scaled
        - jnp.mean(scaled, axis=-1, keepdims=True)
        - normed * jnp.mean(scaled * normed, axis=-1, keepdims=True)
    )


def forward_kernel(*refs):
    x_ref, own_ref, other_ref, vec_ref, b1_ref = refs[0:5]
    n1_out, r1_ref, low_out, act_out, slope_out, f_ref, w1_out, w2_out = refs[13:21]
    n1_ref, low_ref, act_ref, slope_ref, w1_ref, w2_ref, tok_buf, own_buf, other_buf, sems = refs[21:]
    results = ((n1_ref, n1_out), (low_ref, low_out), (w1_ref, w1_out), (act_ref, act_out), (slope_ref, slope_out), (w2_ref, w2_out))
    stores = [pltpu.make_async_copy(src, dst, sems.at[51 + i]) for i, (src, dst) in enumerate(results)]
    loads1, loads2 = placed_hidden(refs[5:13], (w1_ref, w2_ref), sems)
    early = [
        pltpu.make_async_copy(src, dst, sems.at[48 + i])
        for i, (src, dst) in enumerate(
            ((x_ref.at[pl.ds(0, 2)], tok_buf), (own_ref, own_buf), (other_ref, other_buf))
        )
    ]
    for c in early + loads1 + loads2:
        c.start()
    for c in early:
        c.wait()
    bo, g1, s1 = vec_ref[2:3], vec_ref[3:4], vec_ref[4:5]

    def rows(i, _):
        r = pl.ds(i * 128, 128)
        c, m = i // 2, i % 2
        z = tok_buf[c, m].astype(F32) + (own_buf[c, m].astype(F32) + other_buf[1 - c, m].astype(F32)) + bo
        n, rstd = norm(z)
        n1_ref[r] = n
        r1_ref[r] = rstd
        low_ref[r] = (n * g1 + s1).astype(BF16)
        return 0

    lax.fori_loop(0, 4, rows, 0)
    for c in loads1:
        c.wait()
    for c in stores[:3]:
        c.start()

    def inner(j, _):
        cols = pl.ds(pl.multiple_of(j * 256, 256), 256)
        u = dot_nn(low_ref[...], w1_ref[:, cols]) + b1_ref[:, cols]
        cdf = 0.5 * (1.0 + lax.erf(u * (1.0 / math.sqrt(2.0))))
        act_ref[:, cols] = (u * cdf).astype(BF16)
        slope = cdf + u * (jnp.exp(-0.5 * u * u) * (1.0 / math.sqrt(2.0 * math.pi)))
        slope_ref[:, cols] = slope.astype(BF16)
        return 0

    lax.fori_loop(0, 6, inner, 0)
    for c in loads2:
        c.wait()
    for c in stores[3:]:
        c.start()

    def outer(j, _):
        cols = pl.ds(pl.multiple_of(j * 256, 256), 256)
        f_ref[:, cols] = dot_nn(act_ref[...], w2_ref[:, cols]).astype(BF16)
        return 0

    lax.fori_loop(0, 3, outer, 0)
    for c in stores:
        c.wait()


def middle_kernel(
    n1_ref, own_ref, other_ref, cot_ref, theirs_ref, vec_ref, out_ref, df_ref, dz_ref, sums_ref, pcot_ref, sem,
):
    load = pltpu.make_async_copy(theirs_ref.at[3], pcot_ref, sem)
    load.start()
    g1, s1, b2, g2, s2 = (vec_ref[i : i + 1] for i in (3, 4, 5, 6, 7))

    def rows(i, which):
        ref, base = which
        r, o = pl.ds(base + i * 128, 128), pl.ds(256 - base + i * 128, 128)
        z = n1_ref[r] * g1 + s1 + (own_ref[r].astype(F32) + other_ref[o].astype(F32)) + b2
        n, rstd = norm(z)
        grad = ref[i].astype(F32)
        dz = norm_grad(grad, n, rstd, g2)
        dz_ref[r] = dz
        df_ref[r] = dz.astype(BF16)
        return (r, n, grad, dz)

    sums_ref[...] = jnp.zeros_like(sums_ref)

    def own_rows(i, _):
        r, n, grad, dz = rows(i, (cot_ref, 0))
        out_ref[r] = (n * g2 + s2).astype(BF16)
        sums_ref[0:1] += jnp.sum(grad * n, axis=0, keepdims=True)
        sums_ref[1:2] += jnp.sum(grad, axis=0, keepdims=True)
        sums_ref[2:3] += jnp.sum(dz.astype(BF16).astype(F32), axis=0, keepdims=True)
        return 0

    def other_rows(i, _):
        rows(i, (pcot_ref, 256))
        return 0

    lax.fori_loop(0, 2, own_rows, 0)
    load.wait()
    lax.fori_loop(0, 2, other_rows, 0)


def hidden_kernel(df_ref, slope_ref, w1_in, w2_ref, du_out, dh_ref, db1_ref, w1_ref, du_ref, sems):
    load = pltpu.make_async_copy(w1_in, w1_ref, sems.at[0])
    store = pltpu.make_async_copy(du_ref, du_out, sems.at[1])
    load.start()

    def hidden(j, _):
        cols = pl.ds(pl.multiple_of(j * 256, 256), 256)
        du = (dot_nt(df_ref[...], w2_ref[cols, :]) * slope_ref[:, cols].astype(F32)).astype(BF16)
        du_ref[:, cols] = du
        db1_ref[:, cols] = jnp.sum(du.astype(F32), axis=0, keepdims=True)
        return 0

    lax.fori_loop(0, 6, hidden, 0)
    store.start()
    load.wait()

    def back(j, _):
        cols = pl.ds(pl.multiple_of(j * 256, 256), 256)
        dh_ref[:, cols] = dot_nt(du_ref[...], w1_ref[cols, :]).astype(BF16)
        return 0

    lax.fori_loop(0, 3, back, 0)
    store.wait()


def first_kernel(
    dz_ref, own_ref, other_ref, n1_ref, r1_ref, vec_ref, wo_ref, dz1_ref, do_ref, half_ref, da_ref, sums_ref,
):
    g1 = vec_ref[3:4]
    core = my_core()
    sums_ref[...] = jnp.zeros_like(sums_ref)

    def rows(i):
        r, o = pl.ds(i * 128, 128), pl.ds((i ^ 2) * 128, 128)
        grad = dz_ref[r] + (own_ref[r].astype(F32) + other_ref[o].astype(F32))
        n = n1_ref[r]
        dz = norm_grad(grad, n, r1_ref[r], g1)
        low = dz.astype(BF16)
        do_ref[r] = low
        half_ref[r] = jnp.where(core == 0, low[:, :384], low[:, 384:])
        return (r, n, grad, dz, low)

    def own_rows(i, _):
        r, n, grad, dz, low = rows(i)
        dz1_ref[r] = dz
        sums_ref[0:1] += jnp.sum(grad * n, axis=0, keepdims=True)
        sums_ref[1:2] += jnp.sum(grad, axis=0, keepdims=True)
        sums_ref[2:3] += jnp.sum(low.astype(F32), axis=0, keepdims=True)
        return 0

    def other_rows(i, _):
        rows(i)
        return 0

    lax.fori_loop(0, 2, own_rows, 0)
    lax.fori_loop(2, 4, other_rows, 0)
    for m in range(2):
        for c in range(2):
            part = do_ref[pl.ds((c * 2 + m) * BAND, BAND), :]
            da_ref[m, :, c * BAND : (c + 1) * BAND] = dot_nt(wo_ref[...], part).astype(BF16)


def attend_back_kernel(
    q_ref, k_ref, v_ref, mix_ref, da_ref, lse_ref, kseg_ref, qseg_ref, w_in, dq_ref, dkv_ref, own_ref, send_ref, sums_ref,
    mask_ref, w_ref, sem,
):
    load = pltpu.make_async_copy(w_in, w_ref, sem)
    load.start()
    fill_mask(mask_ref, kseg_ref, qseg_ref)

    def pair(j, _):
        both = pl.ds(pl.multiple_of(128 * j, 128), 128)
        q2 = q_ref[:, 0, :, both].reshape(2 * BAND, 128)
        das, deltas, lses = [], [], []
        for h in range(2):
            rows = pl.ds(pl.multiple_of(128 * j + 64 * h, 64), 64)
            das.append(da_ref[0, rows])
            deltas.append(jnp.sum(das[h].astype(F32) * mix_ref[0, rows], axis=0, keepdims=True))
            lses.append(lse_ref[0, pl.ds(2 * j + h, 1)])
        k2 = k_ref[:, 0, :, both].reshape(8 * BAND, 128)
        v2 = v_ref[:, 0, :, both].reshape(8 * BAND, 128)
        dks, dvs, dqs = [], [], []
        for h in range(2):
            cols = slice(64 * h, 64 * h + 64)
            k, v, qh, da = k2[:, cols], v2[:, cols], q2[:, cols], das[h]
            p = jnp.exp(dot_nt(k, qh) + mask_ref[...] - lses[h])
            ds = (p * (dot_nn(v, da) - deltas[h])).astype(BF16)
            dvs.append(dot_nt(p.astype(BF16), da))
            dks.append(dot_nn(ds, qh))
            dqs.append(dot_tn(k, ds))
        later = pl.ds(pl.multiple_of(384 + 128 * j, 128), 128)
        dkv_ref[:, :, both] = jnp.concatenate(dks, axis=1).astype(BF16).reshape(8, BAND, 128)
        dkv_ref[:, :, later] = jnp.concatenate(dvs, axis=1).astype(BF16).reshape(8, BAND, 128)
        dq = jnp.transpose(jnp.concatenate(dqs, axis=0) * 0.125)
        dq_ref[:, :, both] = dq.astype(BF16).reshape(2, BAND, 128)
        return 0

    lax.fori_loop(0, 3, pair, 0)

    load.wait()
    sums_ref[0:1] = jnp.sum(dq_ref[...].reshape(2 * BAND, 384).astype(F32), axis=0, keepdims=True)
    sums_ref[1:2] = jnp.sum(dkv_ref[:, :, 384:].reshape(8 * BAND, 384).astype(F32), axis=0, keepdims=True)

    def step(i, _):
        dx = dot_nt(dkv_ref[pl.ds(4 * i, 4)].reshape(4 * BAND, 768), w_ref[:, 384:1152])
        for z in range(2):
            own_ref[2 * i + z] = dx[2 * z * BAND : (2 * z + 1) * BAND].astype(BF16)
            send_ref[2 * i + z] = dx[(2 * z + 1) * BAND : (2 * z + 2) * BAND].astype(BF16)
        return 0

    lax.fori_loop(0, 2, step, 0)
    dx = dot_nt(dq_ref[...].reshape(2 * BAND, 384), w_ref[:, 0:384])
    own_ref[0] = (own_ref[0].astype(F32) + dx[:BAND]).astype(BF16)
    send_ref[0] = (send_ref[0].astype(F32) + dx[BAND:]).astype(BF16)


def inner_grad_kernel(low_ref, du_ref, out_ref):
    me = my_chip() % 4

    def step(j, _):
        cols = pl.ds(pl.multiple_of(j * 384, 384), 384)
        value = dot_tn(low_ref[:, cols], du_ref[...]).astype(BF16)
        for i in range(8):
            rows = pl.ds(pl.multiple_of((j * 8 + (i ^ me)) * 48, 16), 48)
            out_ref[rows, :] = value[48 * i : 48 * i + 48]
        return 0

    lax.fori_loop(0, 2, step, 0)


def stored_at(block):
    p = block ^ my_chip()
    y, x, z = p // 8, (p // 4) % 2, p % 4
    return ((y, x * 4 + z), (x, y * 4 + z))


def place_rows(halves, block, first, second):
    for ref, (away, row), value in zip(halves, stored_at(block), (first, second)):
        ref[away, pl.ds(pl.multiple_of(row * 48, 16), 48)] = value


def flush(halves, outs, sems):
    copies = [
        pltpu.make_async_copy(halves[i // 2].at[i % 2], out.at[pl.ds(0, 384)], sems.at[i])
        for i, out in enumerate(outs)
    ]
    return copies


def finish(copies):
    for c in copies:
        c.start()
    for c in copies:
        c.wait()


def outer_grad_kernel(act_ref, df_ref, *refs):
    outs, halves, sems = refs[:4], refs[4:6], refs[6]

    def step(j, _):
        cols = pl.ds(pl.multiple_of(j * 384, 384), 384)
        value = dot_tn(act_ref[:, cols], df_ref[...]).astype(BF16)
        for i in range(4):
            place_rows(halves, j * 4 + i, value[96 * i : 96 * i + 48], value[96 * i + 48 : 96 * i + 96])
        return 0

    lax.fori_loop(0, 4, step, 0)
    finish(flush(halves, outs, sems))


def projection_grad_kernel(x_ref, *refs):
    dqs, dkvs, (mix0, mix1, other_ref, half_ref, vec_ref) = refs[0:2], refs[2:4], refs[4:9]
    refs = refs[9:]
    outs, halves, dwo_ref, sems = refs[:4], refs[4:6], refs[6], refs[7]
    core = my_core()
    half = half_ref[...].reshape(2, 2, BAND, 384)
    own = [half[:, m].reshape(2 * BAND, 384) for m in range(2)]
    dwo = dot_nn(mix0[...], own[0]) + dot_nn(mix1[...], own[1])
    dwo_ref[pl.ds(pl.multiple_of(core * 384, 384), 384)] = dwo.astype(BF16)
    other = [jnp.concatenate([half[1, m], half[0, m]], axis=0) for m in range(2)]
    dwo = dot_nn(other_ref[0], other[0]) + dot_nn(other_ref[1], other[1])
    dwo_ref[pl.ds(pl.multiple_of((1 - core) * 384, 384), 384)] = dwo.astype(BF16)

    def step(j, _):
        cols = pl.ds(pl.multiple_of(j * 384, 384), 384)
        x = [x_ref[:, m, :, cols].reshape(8 * BAND, 384) for m in range(2)]

        def total(refs, count):
            terms = [dot_tn(x[m][: count * BAND], refs[m][...].reshape(count * BAND, -1)) for m in range(2)]
            return (terms[0] + terms[1]).astype(BF16)

        dwq, dwkv = total(dqs, 2), total(dkvs, 8)
        for i in range(8):
            rows = slice(48 * i, 48 * i + 48)
            dwo = dwo_ref[pl.ds(pl.multiple_of(j * 384 + 48 * i, 16), 48)]
            place_rows(
                halves,
                j * 8 + i,
                jnp.concatenate([dwq[rows], dwkv[rows, :384]], axis=1),
                jnp.concatenate([dwkv[rows, 384:], dwo], axis=1),
            )
        return 0

    lax.fori_loop(0, 2, step, 0)
    copies = flush(halves, outs, sems)
    for i, out in enumerate(outs):
        copies.append(pltpu.make_async_copy(vec_ref.at[i], out.at[pl.ds(384, 64)], sems.at[4 + i]))
    finish(copies)


def add(*terms):
    total = terms[0].astype(F32)
    for t in terms[1:]:
        total = total + t.astype(F32)
    return total


def first_hop(terms):
    return (terms[0], send(terms[1], Y), terms[2], send(terms[3], X))


def halves_of(g, near, rows):
    return jnp.concatenate(
        [g[192 * near : 192 * near + 192]] + ([g[384 + 32 * near : 416 + 32 * near]] if rows > 48 else [])
    )


def near_terms(hop, rows):
    return tuple(
        add(halves_of(hop[i], 1, rows), halves_of(hop[i + 1], 1, rows)).astype(BF16) for i in (0, 2)
    )


def hop_terms(low):
    return (send(low[0], X), send(low[1], Y))


def far_terms(hop, got, rows):
    return tuple(
        add(halves_of(hop[i], 0, rows), halves_of(hop[i + 1], 0, rows), got[i // 2]).astype(BF16) for i in (0, 2)
    )


def along_line(blocks):
    return (blocks[0], send(blocks[1], Z1), send(blocks[2], Z2), send(blocks[3], Z3))


def line_parts(halves, rows):
    return along_line(
        [
            jnp.concatenate(
                [
                    jnp.concatenate(
                        [h[48 * z : 48 * z + 48]] + ([h[192 + 8 * z : 200 + 8 * z]] if rows > 48 else []), axis=0
                    )
                    for h in halves
                ],
                axis=1,
            )
            for z in range(4)
        ]
    )


def block_parts(block):
    return along_line([block[48 * z : 48 * z + 48] for z in range(4)])


def flip(values, axis, index, bits):
    for bit in range(bits):
        shape = values.shape
        n = shape[axis]
        split = shape[:axis] + (n >> (bit + 1), 2, 1 << bit) + shape[axis + 1 :]
        swapped = jnp.flip(values.reshape(split), axis + 1).reshape(shape)
        values = jnp.where((index >> bit) & 1 == 1, swapped, values)
    return values


def per_device_paired(
    inputs, segments, w_query, b_query, w_key, w_value, b_value, w_output, b_output, gain_first,
    shift_first, w_inner, b_inner, w_outer, b_outer, gain_second, shift_second, cotangent,
):
    seq = lax.axis_index("seq")
    me, core = my_chip(), my_core()
    even = core == 0

    def in_order(mine, got, axis):
        return jnp.where(even, jnp.concatenate([mine, got], axis), jnp.concatenate([got, mine], axis))

    lanes = [b_query, b_value, b_output, gain_first, shift_first, b_outer, gain_second, shift_second, b_inner]
    mine, theirs, outer_rows = call(
        prepare_kernel, [((32, 1536), BF16), ((32, 1536), BF16), ((48, 1536), BF16)], 14
    )(w_query, w_key, w_value, w_output, *(v.reshape(1, -1) for v in lanes), w_outer)
    (square,) = call(chip_rows_kernel, [((56, 1536), BF16)], 2)(mine, send(theirs, CORE))
    wide = after(w_inner, mine).astype(BF16).reshape(24, CHIPS, 2, 96)
    mine, theirs = (
        jnp.where(even, wide[:, :, 0], wide[:, :, 1]).reshape(24, 1536),
        jnp.where(even, wide[:, :, 1], wide[:, :, 0]).reshape(24, 1536),
    )
    inner_rows = in_order(mine, send(theirs, CORE), 0)
    tokens, cot = inputs[:, 0], cotangent[:, 0]
    segs = segments[:, 0]
    segs = flip(segs.reshape(2, 8, BAND), 1, seq, 3)
    kseg = segs.reshape(2, 8 * BAND, 1)
    qseg = segs[:, :2].reshape(2, 1, 2 * BAND)

    other_tokens = send(tokens, CORE)
    hidden_rows = jnp.concatenate([inner_rows, outer_rows], axis=1)
    square, hidden_rows, other_tokens = after_both((square, hidden_rows, other_tokens), ())
    square = line(square)
    square = jnp.concatenate([p[:48] for p in square] + [p[48:] for p in square], axis=0)
    square, hidden_rows = after_both((square, hidden_rows), ())
    square = lines(square)
    hidden = line(hidden_rows)
    hidden, tokens = after_both((hidden, tokens), (kseg, qseg))
    hidden = [jnp.concatenate([h[:, c : c + 1536] for h in hidden], axis=0) for c in (0, 1536)]
    places = jnp.arange(CHIPS)
    order = ((places[:, None] ^ me) == places[None, :]).astype(BF16)
    line_order = ((places[:, None] ^ (me % 4)) == places[None, :]).astype(BF16)
    vecs = square.reshape(4, 224, 1536)[:, 192:].reshape(CHIPS, 8, 1536)[:, :2].reshape(CHIPS, 2 * 1536)
    vecs = dot_nn(line_order, vecs).reshape(CHIPS, 2, 12, 128)
    vec8 = vecs[:, :, :8, :24].transpose(2, 0, 1, 3).reshape(8, 768)
    b1 = jnp.where(even, vecs[:, 0, 8, :96], vecs[:, 1, 8, :96]).reshape(1, 1536)
    bq = jnp.where(even, vec8[0:1, :384], vec8[0:1, 384:])
    bv = jnp.where(even, vec8[1:2, :384], vec8[1:2, 384:])

    wo_rows = square[:, 1152:]
    wo_got = send(jnp.where(even, wo_rows[448:], wo_rows[:448]), CORE)

    near = x_then_y(*hidden)
    beside, second, opposite = send(tokens, Z1), send(tokens, Z2), send(tokens, MIDDLE)
    theirs = send(jnp.stack(after_both((beside, second, opposite, cot), (near, vec8, b1, bq, bv, wo_got))), CORE)
    slots = [tokens, other_tokens, beside, second, opposite, theirs]
    far = y_then_x(*hidden)

    slot_shape, head_shape = (2, BAND, 768), (2, BAND, 384)
    q, k, v, w_abs, x_all = call(
        project_kernel,
        [((2, *head_shape), BF16), ((8, *head_shape), BF16), ((8, *head_shape), BF16), ((768, 1536), BF16), ((8, *slot_shape), BF16)],
        9,
        in_specs=[IN_PLACE] * 7 + [IN_VMEM] * 2,
        out_specs=[IN_VMEM] + [IN_PLACE] * 4,
        scratch=[
            pltpu.VMEM((8, *head_shape), BF16),
            pltpu.VMEM((8, *head_shape), BF16),
            pltpu.VMEM((768, 1536), BF16),
            pltpu.VMEM((8, *slot_shape), BF16),
            pltpu.SemaphoreType.DMA((46,)),
        ],
        cost=(2_800_000_000, 16_000_000),
    )(*slots, square, bq, bv)
    def attention_specs(m=None):
        micro = (lambda i: i) if m is None else (lambda i: m)
        q_spec = pl.BlockSpec((2, 1, BAND, 384), lambda i: (0, micro(i), 0, 0))
        k_spec = pl.BlockSpec((8, 1, BAND, 384), lambda i: (0, micro(i), 0, 0))
        t_spec = pl.BlockSpec((1, 384, 2 * BAND), lambda i: (micro(i), 0, 0))
        lse_spec = pl.BlockSpec((1, 8, 2 * BAND), lambda i: (micro(i), 0, 0))
        segs = [
            pl.BlockSpec((1, 8 * BAND, 1), lambda i: (micro(i), 0, 0)),
            pl.BlockSpec((1, 1, 2 * BAND), lambda i: (micro(i), 0, 0)),
        ]
        return ([q_spec, k_spec, k_spec], [t_spec, t_spec, lse_spec], segs)

    qkv_specs, mix_specs, seg_specs = attention_specs()
    near, (q, k, v) = after_both((near, (q, k, v)), far)
    both = y_then_x(*near)
    mix, mix_low, lse, branch, wo = call(
        attend_kernel,
        [((2, 384, 256), F32), ((2, 384, 256), BF16), ((2, 8, 256), F32), ((2, *slot_shape), BF16), ((384, 768), BF16)],
        7,
        grid=(2,),
        in_specs=qkv_specs + seg_specs + [IN_PLACE] * 2,
        out_specs=[
            *mix_specs,
            pl.BlockSpec((2, 1, BAND, 768), lambda i: (0, i, 0, 0)),
            pl.BlockSpec((384, 768), lambda i: (0, 0)),
        ],
        scratch=[
            pltpu.VMEM((1024, 256), F32),
            pltpu.VMEM((2, 1024, 256), F32),
            pltpu.VMEM((2, 1024, 256), BF16),
            pltpu.SemaphoreType.DMA((16,)),
        ],
        cost=(1_900_000_000, 10_000_000),
    )(q, k, v, kseg, qseg, square, wo_got)
    branch, both = after_both((branch, both), ())
    hidden = [g[i] for i in range(2) for g in (hidden, near, far, both)]
    branch_other = send(branch, CORE)
    n1, r1, hid_low, act, slope, f_own, w1, w2 = call(
        forward_kernel,
        [((512, 768), F32), ((512, 1), F32), ((512, 768), BF16), ((512, 1536), BF16), ((512, 1536), BF16), ((512, 768), BF16), ((768, 1536), BF16), ((1536, 768), BF16)],
        13,
        in_specs=[IN_PLACE] * 3 + [IN_VMEM] * 2 + [IN_PLACE] * 8,
        out_specs=[IN_PLACE, IN_VMEM, IN_PLACE, IN_PLACE, IN_PLACE, IN_VMEM, IN_PLACE, IN_PLACE],
        scratch=[
            pltpu.VMEM((512, 768), F32),
            pltpu.VMEM((512, 768), BF16),
            pltpu.VMEM((512, 1536), BF16),
            pltpu.VMEM((512, 1536), BF16),
            pltpu.VMEM((768, 1536), BF16),
            pltpu.VMEM((1536, 768), BF16),
            *([pltpu.VMEM((2, *slot_shape), BF16)] * 3),
            pltpu.SemaphoreType.DMA((57,)),
        ],
        cost=(2_500_000_000, 16_000_000),
    )(x_all, branch, branch_other, vec8, b1, *hidden)
    mix_other = send(after(mix_low, n1), CORE)
    result, df, dz2, sums2 = call(
        middle_kernel,
        [((256, 768), BF16), ((512, 768), BF16), ((512, 768), F32), ((8, 768), F32)],
        6,
        in_specs=[IN_VMEM] * 4 + [IN_PLACE, IN_VMEM],
        scratch=[pltpu.VMEM(slot_shape, BF16), pltpu.SemaphoreType.DMA],
        cost=(50_000_000, 8_000_000),
    )(n1, f_own, send(f_own, CORE), cot, theirs, vec8)

    piece = [pltpu.VMEM((2, 384, 768), BF16)] * 2
    outer_terms = call(
        outer_grad_kernel,
        [((384, 768), BF16)] * 4,
        2,
        out_specs=[IN_PLACE] * 4,
        scratch=piece + [pltpu.SemaphoreType.DMA((4,))],
        cost=(1_200_000_000, 6_000_000),
    )(act, df)
    outer_hop = first_hop(outer_terms)
    du, dh_own, db1 = call(
        hidden_kernel,
        [((512, 1536), BF16), ((512, 768), BF16), ((1, 1536), F32)],
        4,
        in_specs=[IN_VMEM, IN_VMEM, IN_PLACE, IN_VMEM],
        out_specs=[IN_PLACE, IN_VMEM, IN_VMEM],
        scratch=[pltpu.VMEM((768, 1536), BF16), pltpu.VMEM((512, 1536), BF16), pltpu.SemaphoreType.DMA((2,))],
        cost=(2_400_000_000, 9_000_000),
    )(after(df, *outer_terms), slope, w1, w2)
    dh_other = send(dh_own, CORE)
    (inner_terms,) = call(inner_grad_kernel, [((768, 1536), BF16)], 2, cost=(1_200_000_000, 6_000_000))(hid_low, du)
    inner_block = lax.psum_scatter(inner_terms, "dp", scatter_dimension=0, tiled=True)
    outer_hop = after_both(outer_hop, (inner_terms,))
    outer_low = near_terms(outer_hop, 48)
    dh_own = after(dh_own, inner_terms, *outer_low)
    outer_sent = hop_terms(outer_low)
    dz1, do, do_half, da, sums1 = call(
        first_kernel,
        [((256, 768), F32), ((512, 768), BF16), ((512, 384), BF16), ((2, 384, 256), BF16), ((8, 768), F32)],
        7,
        cost=(300_000_000, 10_000_000),
    )(dz2, dh_own, dh_other, n1, r1, vec8, wo)

    def back(m, events):
        specs = attention_specs(m)
        shapes = [(2, BAND, 384), (8, BAND, 768), (4, BAND, 768), (4, BAND, 768)]
        return call(
            attend_back_kernel,
            [(shape, BF16) for shape in shapes] + [((8, 384), F32)],
            9,
            grid=(1,),
            in_specs=specs[0] + specs[1] + specs[2] + [IN_PLACE],
            out_specs=[pl.BlockSpec(shape, lambda i: (0, 0, 0)) for shape in shapes] + [pl.BlockSpec((8, 384), lambda i: (0, 0))],
            scratch=[pltpu.VMEM((1024, 256), F32), pltpu.VMEM((768, 1536), BF16), pltpu.SemaphoreType.DMA],
            cost=(3_400_000_000, 10_000_000),
        )(q, k, v, mix, after(da, *events), lse, kseg, qseg, w_abs)

    def core_sums(own, got):
        return [add(own[z], got[z]) if z == 0 else add(own[z], got[z]).astype(BF16) for z in range(4)]

    def line_sums(sums):
        return (sums[0], send(sums[1], Z1), send(sums[2], Z2), send(sums[3], MIDDLE))

    outer_hop, outer_sent = after_both((outer_hop, outer_sent), (da,))
    outer_half = far_terms(outer_hop, outer_sent, 48)
    *grads0, dx0, dx_send, sums_q0 = back(0, ())
    got0 = send(dx_send, CORE)
    outer_half = after_both(outer_half, grads0[:1])
    outer_parts = line_parts(outer_half, 48)
    *grads1, dx1, dx_send, sums_q1 = back(1, (dx0, *outer_half))
    outer_parts, got0, dx0 = after_both((outer_parts, got0, dx0), grads1[:1])
    got1 = send(dx_send, CORE)
    low0 = core_sums(dx0, got0)
    grads1, _ = lax.optimization_barrier((grads1, (outer_parts, low0, inner_block)))
    inner_parts = block_parts(inner_block)
    sent0 = line_sums(low0)

    def widen(value):
        zero = jnp.zeros_like(value)
        return in_order(value, zero, 1)

    sums_q = sums_q0 + sums_q1
    eight = jnp.concatenate(
        [widen(sums_q[0:1]), widen(sums_q[1:2]), sums1[2:3], sums1[0:1], sums1[1:2], sums2[2:3], sums2[0:1], sums2[1:2]], 0
    )
    eight = jnp.pad(eight.reshape(8, CHIPS, 2, 24), ((0, 0), (0, 0), (0, 0), (0, 104))).transpose(1, 2, 0, 3)
    db1 = jnp.where(jnp.arange(2)[None, :, None] == core, db1.reshape(CHIPS, 1, 96), 0.0)
    db1 = jnp.pad(db1, ((0, 0), (0, 0), (0, 416)))
    vec_grads = jnp.concatenate([eight.reshape(CHIPS, 2, 1024), db1], axis=2).reshape(CHIPS, 3072)
    vec_grads = dot_nn(order, vec_grads.astype(BF16)).astype(BF16).reshape(2, 2, 4, 2, 1536)
    vec_grads = jnp.pad(vec_grads, ((0, 0), (0, 0), (0, 0), (0, 6), (0, 0)))
    vec_first = vec_grads[..., :768].reshape(2, 64, 768)
    vec_second = vec_grads[..., 768:].transpose(1, 0, 2, 3, 4).reshape(2, 64, 768)
    square_terms = call(
        projection_grad_kernel,
        [((448, 768), BF16)] * 4,
        10,
        out_specs=[IN_PLACE] * 4,
        scratch=piece + [pltpu.VMEM((768, 384), BF16), pltpu.SemaphoreType.DMA((8,))],
        cost=(3_300_000_000, 12_000_000),
    )(x_all, grads0[0], grads1[0], grads0[1], grads1[1], mix_low[0], mix_low[1], mix_other, do_half, jnp.concatenate([vec_first, vec_second]))
    square_hop = first_hop(square_terms)
    inner_parts, got1 = after_both((inner_parts, got1), square_terms)
    sent1 = line_sums(core_sums(dx1, got1))
    square_hop, sent0 = after_both((square_hop, sent0), ())
    square_sent = hop_terms(near_terms(square_hop, 56))
    square_half = far_terms(square_hop, square_sent, 56)
    square_parts = line_parts(square_half, 56)

    outer_total = add(*outer_parts)
    inner_total = add(*inner_parts)
    grad_outer = jnp.concatenate([outer_total[:, :768], outer_total[:, 768:]], axis=0)
    keep = jnp.where(even, inner_total[:24], inner_total[24:])
    got = send(jnp.where(even, inner_total[24:], inner_total[:24]).astype(BF16), CORE).astype(F32)
    grad_inner = in_order(keep.reshape(24, CHIPS, 1, 96), got.reshape(24, CHIPS, 1, 96), 2).reshape(24, 3072)
    keep, other = call(owner_kernel, [((32, 1536), F32), ((32, 1536), BF16)], 5)(*square_half, *square_parts[1:])
    grads = call(
        result_kernel,
        [((24, 768), F32)] * 4 + [((1, 24), F32)] * 8 + [((1, 96), F32)],
        2,
    )(keep, send(other, CORE))
    squares, small = grads[:4], [g.reshape(-1) for g in grads[4:]]
    dz1 = dz1.reshape(slot_shape)
    dz1 = dz1.reshape(2, BAND, 768)
    grad_tokens = jnp.stack([add(dz1[m], *sent).astype(BF16) for m, sent in enumerate((sent0, sent1))])
    return (
        result.reshape(2, 1, BAND, 768), grad_tokens[:, None],
        squares[0], small[0], squares[1], squares[2], small[1], squares[3], small[2],
        small[3], small[4], grad_inner, small[8], grad_outer, small[5], small[6], small[7],
    )


def solution(mesh):
    in_specs = (
        P(None, "dp", "seq", None),
        P(None, "dp", None),
        P(("dp", "seq"), None),
        P(("dp", "seq")),
        P(("dp", "seq"), None),
        P(("dp", "seq"), None),
        P(("dp", "seq")),
        P(("dp", "seq"), None),
        P(("dp", "seq")),
        P(("dp", "seq")),
        P(("dp", "seq")),
        P(("dp", "seq"), None),
        P(("dp", "seq")),
        P(("dp", "seq"), None),
        P(("dp", "seq")),
        P(("dp", "seq")),
        P(("dp", "seq")),
        P(None, "dp", "seq", None),
    )
    out_specs = (
        P(None, "dp", "seq", None),
        P(None, "dp", "seq", None),
        P(("dp", "seq"), None),
        P(("dp", "seq")),
        P(("dp", "seq"), None),
        P(("dp", "seq"), None),
        P(("dp", "seq")),
        P(("dp", "seq"), None),
        P(("dp", "seq")),
        P(("dp", "seq")),
        P(("dp", "seq")),
        P(("dp", "seq"), None),
        P(("dp", "seq")),
        P(("dp", "seq"), None),
        P(("dp", "seq")),
        P(("dp", "seq")),
        P(("dp", "seq")),
    )
    paired = (mesh.shape["dp"], mesh.shape["seq"]) == (4, 8)
    return jax.shard_map(
        per_device_paired if paired else per_device, mesh=mesh, in_specs=in_specs, out_specs=out_specs, check_vma=False
    )
```

```python
import math

import jax
import jax.numpy as jnp
from jax import lax
from jax.experimental import pallas as pl
from jax.experimental.pallas import tpu as pltpu
from jax.sharding import PartitionSpec as P

HEADS = 12
HEAD_DIM = 64


def narrow(masters):
    return tuple((item.astype(jnp.bfloat16) for item in masters))


def fetch_forward(masters):
    lowered = narrow(masters)
    return (
        lax.all_gather(lowered[0], ("dp", "seq"), axis=0, tiled=True),
        lax.all_gather(lowered[1], ("dp", "seq"), axis=0, tiled=True),
        lax.all_gather(lowered[2], ("dp", "seq"), axis=0, tiled=True),
        lax.all_gather(lowered[3], ("dp", "seq"), axis=0, tiled=True),
        lax.all_gather(lowered[4], ("dp", "seq"), axis=0, tiled=True),
        lax.all_gather(lowered[5], ("dp", "seq"), axis=0, tiled=True),
        lax.all_gather(lowered[6], ("dp", "seq"), axis=0, tiled=True),
        lax.all_gather(lowered[7], ("dp", "seq"), axis=0, tiled=True),
        lax.all_gather(lowered[8], ("dp", "seq"), axis=0, tiled=True),
        lax.all_gather(lowered[9], ("dp", "seq"), axis=0, tiled=True),
        lax.all_gather(lowered[10], ("dp", "seq"), axis=0, tiled=True),
        lax.all_gather(lowered[11], ("dp", "seq"), axis=0, tiled=True),
        lax.all_gather(lowered[12], ("dp", "seq"), axis=0, tiled=True),
        lax.all_gather(lowered[13], ("dp", "seq"), axis=0, tiled=True),
        lax.all_gather(lowered[14], ("dp", "seq"), axis=0, tiled=True),
    )


def fetch_backward(masters):
    lowered = narrow(masters)
    return (
        lax.all_gather(lowered[0], ("dp", "seq"), axis=0, tiled=True),
        lax.all_gather(lowered[1], ("dp", "seq"), axis=0, tiled=True),
        lax.all_gather(lowered[2], ("dp", "seq"), axis=0, tiled=True),
        lax.all_gather(lowered[3], ("dp", "seq"), axis=0, tiled=True),
        lax.all_gather(lowered[4], ("dp", "seq"), axis=0, tiled=True),
        lax.all_gather(lowered[5], ("dp", "seq"), axis=0, tiled=True),
        lax.all_gather(lowered[6], ("dp", "seq"), axis=0, tiled=True),
        lax.all_gather(lowered[7], ("dp", "seq"), axis=0, tiled=True),
        lax.all_gather(lowered[8], ("dp", "seq"), axis=0, tiled=True),
        lax.all_gather(lowered[9], ("dp", "seq"), axis=0, tiled=True),
        lax.all_gather(lowered[10], ("dp", "seq"), axis=0, tiled=True),
        lax.all_gather(lowered[11], ("dp", "seq"), axis=0, tiled=True),
        lax.all_gather(lowered[12], ("dp", "seq"), axis=0, tiled=True),
        lax.all_gather(lowered[13], ("dp", "seq"), axis=0, tiled=True),
        lax.all_gather(lowered[14], ("dp", "seq"), axis=0, tiled=True),
    )


def sum_owners(terms):
    return (
        lax.psum_scatter(terms[0], ("dp", "seq"), scatter_dimension=0, tiled=True),
        lax.psum_scatter(terms[1], ("dp", "seq"), scatter_dimension=0, tiled=True),
        lax.psum_scatter(terms[2], ("dp", "seq"), scatter_dimension=0, tiled=True),
        lax.psum_scatter(terms[3], ("dp", "seq"), scatter_dimension=0, tiled=True),
        lax.psum_scatter(terms[4], ("dp", "seq"), scatter_dimension=0, tiled=True),
        lax.psum_scatter(terms[5], ("dp", "seq"), scatter_dimension=0, tiled=True),
        lax.psum_scatter(terms[6], ("dp", "seq"), scatter_dimension=0, tiled=True),
        lax.psum_scatter(terms[7], ("dp", "seq"), scatter_dimension=0, tiled=True),
        lax.psum_scatter(terms[8], ("dp", "seq"), scatter_dimension=0, tiled=True),
        lax.psum_scatter(terms[9], ("dp", "seq"), scatter_dimension=0, tiled=True),
        lax.psum_scatter(terms[10], ("dp", "seq"), scatter_dimension=0, tiled=True),
        lax.psum_scatter(terms[11], ("dp", "seq"), scatter_dimension=0, tiled=True),
        lax.psum_scatter(terms[12], ("dp", "seq"), scatter_dimension=0, tiled=True),
        lax.psum_scatter(terms[13], ("dp", "seq"), scatter_dimension=0, tiled=True),
        lax.psum_scatter(terms[14], ("dp", "seq"), scatter_dimension=0, tiled=True),
    )


def layer_norm(z, gain, shift):
    mean = jnp.mean(z, axis=-1, keepdims=True)
    centered = z - mean
    rstd = lax.rsqrt(jnp.mean(centered * centered, axis=-1, keepdims=True) + 1e-05)
    normed = centered * rstd
    return (normed * gain + shift, normed, rstd)


def norm_back(grad, normed, rstd, gain):
    scaled = grad * gain
    inner = (
        scaled
        - jnp.mean(scaled, axis=-1, keepdims=True)
        - normed * jnp.mean(scaled * normed, axis=-1, keepdims=True)
    )
    return (rstd * inner, jnp.sum(grad * normed, axis=0), jnp.sum(grad, axis=0))


def gelu_exact(value):
    return jax.nn.gelu(value, approximate=False)


def key_blocks(keys_all, values_all, seg_row):
    length = keys_all.shape[0]
    width = math.gcd(length, 1024)
    count = length // width
    keys_split = keys_all.reshape(count, width, HEADS, HEAD_DIM)
    values_split = values_all.reshape(count, width, HEADS, HEAD_DIM)
    return (keys_split, values_split, seg_row.reshape(count, width))


def block_scores(queries, keys, query_seg, key_seg):
    scores = jnp.einsum("qhd,khd->hqk", queries, keys, preferred_element_type=jnp.float32) * 0.125
    same = (query_seg[:, None] == key_seg[None, :])[None]
    return jnp.where(same, scores, -1e30)


def attend(queries, keys_all, values_all, seg_row, query_seg):
    rows = queries.shape[0]
    query_h = queries.reshape(rows, HEADS, HEAD_DIM)
    keys_split, values_split, seg_split = key_blocks(keys_all, values_all, seg_row)

    def first_pass(carry, block):
        top, total = carry
        keys, key_seg = block
        scores = block_scores(query_h, keys, query_seg, key_seg)
        new_top = jnp.maximum(top, jnp.max(scores, axis=-1))
        total = total * jnp.exp(top - new_top) + jnp.sum(
            jnp.exp(scores - new_top[..., None]), axis=-1
        )
        return ((new_top, total), None)

    start = (jnp.full((HEADS, rows), -1e30, jnp.float32), jnp.zeros((HEADS, rows), jnp.float32))
    (top, total), _ = lax.scan(first_pass, start, (keys_split, seg_split))
    lse = top + jnp.log(total)

    def second_pass(acc, block):
        keys, values, key_seg = block
        scores = block_scores(query_h, keys, query_seg, key_seg)
        probs = jnp.exp(scores - lse[..., None]).astype(jnp.bfloat16)
        return (
            acc + jnp.einsum("hqk,khd->qhd", probs, values, preferred_element_type=jnp.float32),
            None,
        )

    mixed, _ = lax.scan(
        second_pass,
        jnp.zeros((rows, HEADS, HEAD_DIM), jnp.float32),
        (keys_split, values_split, seg_split),
    )
    return (lse, mixed.reshape(rows, HEADS * HEAD_DIM))


def attend_back(queries, grad_mixed, lse, delta, keys_all, values_all, seg_row, query_seg):
    rows = queries.shape[0]
    query_h = queries.reshape(rows, HEADS, HEAD_DIM)
    grad_h = grad_mixed.reshape(rows, HEADS, HEAD_DIM)
    keys_split, values_split, seg_split = key_blocks(keys_all, values_all, seg_row)

    def step(grad_query, block):
        keys, values, key_seg = block
        scores = block_scores(query_h, keys, query_seg, key_seg)
        probs = jnp.exp(scores - lse[..., None])
        grad_probs = jnp.einsum("qhd,khd->hqk", grad_h, values, preferred_element_type=jnp.float32)
        grad_scores = (probs * (grad_probs - delta[..., None])).astype(jnp.bfloat16)
        grad_query = grad_query + jnp.einsum(
            "hqk,khd->qhd", grad_scores, keys, preferred_element_type=jnp.float32
        )
        grad_keys = (
            jnp.einsum("hqk,qhd->khd", grad_scores, query_h, preferred_element_type=jnp.float32)
            * 0.125
        )
        grad_values = jnp.einsum(
            "hqk,qhd->khd", probs.astype(jnp.bfloat16), grad_h, preferred_element_type=jnp.float32
        )
        width = keys.shape[0]
        joined = jnp.concatenate(
            [
                grad_keys.reshape(width, HEADS * HEAD_DIM),
                grad_values.reshape(width, HEADS * HEAD_DIM),
            ],
            axis=-1,
        )
        return (grad_query, joined)

    grad_query, joined = lax.scan(
        step, jnp.zeros((rows, HEADS, HEAD_DIM), jnp.float32), (keys_split, values_split, seg_split)
    )
    grad_query = (grad_query * 0.125).reshape(rows, HEADS * HEAD_DIM)
    return (grad_query, joined.reshape(keys_all.shape[0], 2 * HEADS * HEAD_DIM))


def outer_sum(left, right):
    return jnp.einsum("tf,tg->fg", left, right, preferred_element_type=jnp.float32)


def times_transposed(left, weight):
    return jnp.einsum("tg,fg->tf", left, weight, preferred_element_type=jnp.float32)


def column_sum(value):
    return jnp.sum(value.astype(jnp.float32), axis=0)


def per_device(
    inputs,
    segments,
    w_query,
    b_query,
    w_key,
    w_value,
    b_value,
    w_output,
    b_output,
    gain_first,
    shift_first,
    w_inner,
    b_inner,
    w_outer,
    b_outer,
    gain_second,
    shift_second,
    cotangent,
):
    masters = (
        w_query,
        b_query,
        w_key,
        w_value,
        b_value,
        w_output,
        b_output,
        gain_first,
        shift_first,
        w_inner,
        b_inner,
        w_outer,
        b_outer,
        gain_second,
        shift_second,
    )
    rows = inputs.shape[2]
    offset = lax.axis_index("seq") * rows
    results = []
    grad_rows = []
    totals = None
    for micro in range(inputs.shape[0]):
        tokens = inputs[micro, 0]
        seg_row = segments[micro, 0]
        query_seg = lax.dynamic_slice_in_dim(seg_row, offset, rows)
        full = fetch_forward(masters)
        wq, bq, wk, wv, bv, wo, bo, g1, s1, w1, b1, w2, b2, g2, s2 = full
        g1f, s1f, g2f, s2f = (
            g1.astype(jnp.float32),
            s1.astype(jnp.float32),
            g2.astype(jnp.float32),
            s2.astype(jnp.float32),
        )
        queries = (
            jnp.dot(tokens, wq, preferred_element_type=jnp.float32) + bq.astype(jnp.float32)
        ).astype(jnp.bfloat16)
        keys = jnp.dot(tokens, wk, preferred_element_type=jnp.float32).astype(jnp.bfloat16)
        values = (
            jnp.dot(tokens, wv, preferred_element_type=jnp.float32) + bv.astype(jnp.float32)
        ).astype(jnp.bfloat16)
        keys_all, values_all = (
            lax.all_gather(keys, "seq", axis=0, tiled=True),
            lax.all_gather(values, "seq", axis=0, tiled=True),
        )
        lse, mixed = attend(queries, keys_all, values_all, seg_row, query_seg)
        mixed_low = mixed.astype(jnp.bfloat16)
        branch = jnp.dot(mixed_low, wo, preferred_element_type=jnp.float32) + bo.astype(jnp.float32)
        hidden, normed_first, rstd_first = layer_norm(tokens.astype(jnp.float32) + branch, g1f, s1f)
        hidden_low = hidden.astype(jnp.bfloat16)
        inner = jnp.dot(hidden_low, w1, preferred_element_type=jnp.float32) + b1.astype(jnp.float32)
        active, gelu_pull = jax.vjp(gelu_exact, inner)
        active_low = active.astype(jnp.bfloat16)
        outer = jnp.dot(active_low, w2, preferred_element_type=jnp.float32) + b2.astype(jnp.float32)
        result, normed_second, rstd_second = layer_norm(hidden + outer, g2f, s2f)
        results.append(result.astype(jnp.bfloat16))
        wq, bq, wk, wv, bv, wo, bo, g1, s1, w1, b1, w2, b2, g2, s2 = fetch_backward(masters)
        keys_all, values_all = (
            lax.all_gather(keys, "seq", axis=0, tiled=True),
            lax.all_gather(values, "seq", axis=0, tiled=True),
        )
        grad_out = cotangent[micro, 0].astype(jnp.float32)
        grad_z2, grad_g2, grad_s2 = norm_back(grad_out, normed_second, rstd_second, g2f)
        grad_outer = grad_z2.astype(jnp.bfloat16)
        grad_w2 = outer_sum(active_low, grad_outer)
        grad_b2 = column_sum(grad_outer)
        grad_active = times_transposed(grad_outer, w2)
        grad_inner = gelu_pull(grad_active)[0].astype(jnp.bfloat16)
        grad_w1 = outer_sum(hidden_low, grad_inner)
        grad_b1 = column_sum(grad_inner)
        grad_hidden = times_transposed(grad_inner, w1) + grad_z2
        grad_z1, grad_g1, grad_s1 = norm_back(grad_hidden, normed_first, rstd_first, g1f)
        grad_branch = grad_z1.astype(jnp.bfloat16)
        grad_wo = outer_sum(mixed_low, grad_branch)
        grad_bo = column_sum(grad_branch)
        grad_mixed = times_transposed(grad_branch, wo).astype(jnp.bfloat16)
        delta = jnp.sum(
            (grad_mixed.astype(jnp.float32) * mixed).reshape(rows, HEADS, HEAD_DIM), axis=-1
        ).T
        grad_query, joined = attend_back(
            queries, grad_mixed, lse, delta, keys_all, values_all, seg_row, query_seg
        )
        summed = lax.psum_scatter(
            joined.astype(jnp.bfloat16), "seq", scatter_dimension=0, tiled=True
        ).astype(jnp.float32)
        width = summed.shape[1] // 2
        grad_keys = summed[:, :width].astype(jnp.bfloat16)
        grad_values = summed[:, width:].astype(jnp.bfloat16)
        grad_query = grad_query.astype(jnp.bfloat16)
        grad_wq = outer_sum(tokens, grad_query)
        grad_wk = outer_sum(tokens, grad_keys)
        grad_wv = outer_sum(tokens, grad_values)
        grad_bq = column_sum(grad_query)
        grad_bv = column_sum(grad_values)
        grad_tokens = (
            times_transposed(grad_query, wq)
            + times_transposed(grad_keys, wk)
            + times_transposed(grad_values, wv)
            + grad_z1
        )
        grad_rows.append(grad_tokens.astype(jnp.bfloat16))
        terms = (
            grad_wq,
            grad_bq,
            grad_wk,
            grad_wv,
            grad_bv,
            grad_wo,
            grad_bo,
            grad_g1,
            grad_s1,
            grad_w1,
            grad_b1,
            grad_w2,
            grad_b2,
            grad_g2,
            grad_s2,
        )
        totals = terms if totals is None else tuple((old + new for old, new in zip(totals, terms)))
    owned = sum_owners(totals)
    outputs = jnp.stack(results)[:, None]
    grad_inputs = jnp.stack(grad_rows)[:, None]
    return (
        outputs,
        grad_inputs,
        owned[0],
        owned[1],
        owned[2],
        owned[3],
        owned[4],
        owned[5],
        owned[6],
        owned[7],
        owned[8],
        owned[9],
        owned[10],
        owned[11],
        owned[12],
        owned[13],
        owned[14],
    )


BOTH = ("dp", "seq")
CHIPS = 16
BAND = 128
F32 = jnp.float32
BF16 = jnp.bfloat16
IN_VMEM = pl.BlockSpec(memory_space=pltpu.VMEM)
IN_PLACE = pl.BlockSpec(memory_space=pl.ANY)


def pairs(dp_bits, seq_bits, keep=lambda dp, seq: True):
    return [
        (dp * 8 + seq, (dp ^ dp_bits) * 8 + (seq ^ seq_bits))
        for dp in range(4)
        for seq in range(8)
        if keep(dp, seq)
    ]


CORE, Z1, Z2, Z3 = pairs(0, 1), pairs(0, 2), pairs(0, 4), pairs(0, 6)
X, Y = pairs(1, 0), pairs(2, 0)
MIDDLE = pairs(0, 6, lambda dp, seq: seq // 2 in (1, 2))


def send(value, route):
    return lax.ppermute(value, BOTH, route)


def after(value, *events):
    return lax.optimization_barrier((value, *events))[0]


def after_both(values, events):
    return lax.optimization_barrier((tuple(values), tuple(events)))[0]


def my_chip():
    return lax.axis_index("dp") * 4 + lax.axis_index("seq") // 2


def my_core():
    return lax.axis_index("seq") % 2


def dot_nn(a, b):
    return lax.dot_general(a, b, (((1,), (0,)), ((), ())), preferred_element_type=F32)


def dot_nt(a, b):
    return lax.dot_general(a, b, (((1,), (1,)), ((), ())), preferred_element_type=F32)


def dot_tn(a, b):
    return lax.dot_general(a, b, (((0,), (0,)), ((), ())), preferred_element_type=F32)


def call(body, outs, n_in, in_specs=None, out_specs=None, scratch=(), grid=None, cost=None):
    kwargs = {} if grid is None else {"grid": grid}
    return pl.pallas_call(
        body,
        out_shape=[jax.ShapeDtypeStruct(s, d) for s, d in outs],
        in_specs=in_specs or [IN_VMEM] * n_in,
        out_specs=out_specs or [IN_VMEM] * len(outs),
        scratch_shapes=list(scratch),
        cost_estimate=pl.CostEstimate(flops=cost[0], bytes_accessed=cost[1], transcendentals=0)
        if cost
        else None,
        **kwargs,
    )


def line(block):
    return [block, send(block, Z1), send(block, Z2), send(block, Z3)]


def lines(block):
    return lax.all_gather(block, "dp", axis=0, tiled=True)


def placed(rows, target, sems, base):
    me = my_chip() % 4
    copies = []
    for i in range(CHIPS):
        at = pl.multiple_of(((i // 4) * 4 + ((i % 4) ^ me)) * 48, 16)
        copies.append(
            pltpu.make_async_copy(
                rows.at[pl.ds((i // 4) * 224 + (i % 4) * 48, 48)], target.at[pl.ds(at, 48)], sems.at[base + i]
            )
        )
    return copies


def x_then_y(first, second):
    return (send(first, X), send(second, Y))


def y_then_x(first, second):
    return (send(first, Y), send(second, X))


def placed_hidden(groups, targets, sems):
    me = my_chip()
    copies = ([], [])
    for i, group in enumerate(groups):
        which, far, near = i // 4, (i // 2) % 2, i % 2
        for z in range(4):
            b = (far * (8, 4)[which] + near * (4, 8)[which] + z) ^ me
            for part in range(1 + which):
                cols = pl.ds(768 * part, 768) if which else pl.ds(0, 1536)
                at = pl.multiple_of(b * (48, 96)[which] + 48 * part, 16)
                sem = sems.at[16 * which + len(copies[which])]
                rows = group.at[pl.ds(z * 48, 48), cols]
                copies[which].append(pltpu.make_async_copy(rows, targets[which].at[pl.ds(at, 48)], sem))
    return copies


def prepare_kernel(*refs):
    weights, vecs, outer_ref = refs[0:4], refs[4:13], refs[13]
    mine_ref, theirs_ref, rows_ref = refs[14:]
    even = my_core() == 0
    theirs_ref[24:32] = jnp.zeros((8, 1536), BF16)
    for i, ref in enumerate(weights):
        w, cols = ref[...].astype(BF16), slice(384 * i, 384 * i + 384)
        mine_ref[0:24, cols] = jnp.where(even, w[:, :384], w[:, 384:])
        theirs_ref[0:24, cols] = jnp.where(even, w[:, 384:], w[:, :384])
    pieces = []
    for ref in vecs:
        pieces += [ref[...], jnp.zeros((1, 128 - ref.shape[1]), F32)]
    row = jnp.concatenate(pieces + [jnp.zeros((1, 384), F32)], axis=1)
    row = jnp.where(lax.broadcasted_iota(jnp.int32, (8, 1536), 0) == 0, row, 0.0).astype(BF16)
    mine_ref[24:32] = row
    theirs_ref[24:32] = row
    rows_ref[:, 0:768] = outer_ref[0:48].astype(BF16)
    rows_ref[:, 768:1536] = outer_ref[48:96].astype(BF16)


def chip_rows_kernel(mine_ref, got_ref, out_ref):
    even = my_core() == 0
    mine, got = mine_ref[...].astype(F32), got_ref[...].astype(F32)
    out_ref[0:24] = jnp.where(even, mine[:24], got[:24]).astype(BF16)
    out_ref[24:48] = jnp.where(even, got[:24], mine[:24]).astype(BF16)
    first = jnp.where(even, mine[24:32], got[24:32])
    second = jnp.where(even, got[24:32], mine[24:32])
    row = lax.broadcasted_iota(jnp.int32, (8, 1536), 0)
    out_ref[48:56] = jnp.where(row == 1, second[0:1], jnp.where(row == 0, first[0:1], 0.0)).astype(BF16)


def owner_kernel(first_ref, second_ref, *refs):
    parts, (keep_ref, other_ref) = refs[:3], refs[3:]
    even = my_core() == 0
    for c, ref in ((0, first_ref), (768, second_ref)):
        cols = slice(c, c + 768)
        a, b, d = (p[:, cols].astype(F32) for p in parts)
        rows = ref[0:48].astype(F32) + a[:48] + b[:48] + d[:48]
        keep_ref[0:24, cols] = jnp.where(even, rows[:24], rows[24:])
        other_ref[0:24, cols] = jnp.where(even, rows[24:], rows[:24]).astype(BF16)
        vec = ref[192:200].astype(F32) + a[48:56] + b[48:56] + d[48:56]
        zero = jnp.zeros((7, 768), F32)
        keep_ref[24:32, cols] = jnp.concatenate([jnp.where(even, vec[0:1], vec[1:2]), zero], axis=0)
        other_ref[24:32, cols] = jnp.concatenate([jnp.where(even, vec[1:2], vec[0:1]), zero], axis=0).astype(BF16)


def result_kernel(keep_ref, got_ref, *refs):
    outs, vecs = refs[:4], refs[4:]
    even = my_core() == 0
    for i, ref in enumerate(outs):
        cols = slice(384 * i, 384 * i + 384)
        keep, got = keep_ref[0:24, cols], got_ref[0:24, cols].astype(F32)
        ref[:, 0:384] = jnp.where(even, keep, got)
        ref[:, 384:768] = jnp.where(even, got, keep)
    vec = keep_ref[24:25] + got_ref[24:32].astype(F32)[0:1]
    for i, ref in enumerate(vecs):
        ref[...] = vec[:, 128 * i : 128 * i + ref.shape[1]]


def project_kernel(*refs):
    xs, theirs, rows = refs[0:5], refs[5], refs[6]
    bq_ref, bv_ref = refs[7:9]
    q_ref, k_out, v_out, w_out, x_out, k_ref, v_ref, w_ref, x_ref, sems = refs[9:]
    stores = [pltpu.make_async_copy(w_ref, w_out, sems.at[40]), pltpu.make_async_copy(x_ref, x_out, sems.at[41])]
    slots = [*zip((0, 1, 2, 4, 6), xs), *((2 * z + 3, theirs.at[z]) for z in range(3))]
    loads = [pltpu.make_async_copy(ref, x_ref.at[s], sems.at[32 + s]) for s, ref in slots]
    loads += placed(rows, w_ref, sems, 0)
    for c in loads:
        c.start()
    for c in loads:
        c.wait()
    for c in stores:
        c.start()
    bq, bv = bq_ref[...], bv_ref[...]

    q = (dot_nn(x_ref[0:2].reshape(4 * BAND, 768), w_ref[:, 0:384]) + bq).astype(BF16) * jnp.asarray(0.125, BF16)
    q_ref[...] = q.reshape(2, 2, BAND, 384)

    def slots4(i, _):
        four = pl.ds(4 * i, 4)
        both = dot_nn(x_ref[four].reshape(8 * BAND, 768), w_ref[:, 384:1152])
        k_ref[four] = both[:, :384].astype(BF16).reshape(4, 2, BAND, 384)
        v_ref[four] = (both[:, 384:] + bv).astype(BF16).reshape(4, 2, BAND, 384)
        for n, (src, dst) in enumerate(((k_ref, k_out), (v_ref, v_out))):
            pltpu.make_async_copy(src.at[four], dst.at[four], sems.at[42 + 2 * i + n]).start()
        return 0

    lax.fori_loop(0, 2, slots4, 0)
    for i in range(2):
        for n, (src, dst) in enumerate(((k_ref, k_out), (v_ref, v_out))):
            four = pl.ds(4 * i, 4)
            stores.append(pltpu.make_async_copy(src.at[four], dst.at[four], sems.at[42 + 2 * i + n]))
    for c in stores:
        c.wait()


def fill_mask(mask_ref, kseg_ref, qseg_ref):
    for c in range(4):
        rows = slice(256 * c, 256 * c + 256)
        mask_ref[rows] = jnp.where(kseg_ref[0, rows] == qseg_ref[0], 0.0, -1e30)


def attend_kernel(
    q_ref, k_ref, v_ref, kseg_ref, qseg_ref, rows_ref, got_ref,
    mix_ref, low_ref, lse_ref, out_ref, wo_ref, mask_ref, score_ref, weight_ref, sems,
):
    core, me = my_core(), my_chip() % 4
    first = pl.program_id(0) == 0
    loads = []
    for i in range(8):
        at = pl.ds(pl.multiple_of((i // 4) * 192 + ((i % 4) ^ me) * 48, 16), 48)
        row = (i // 4) * 224 + (i % 4) * 48
        mine = rows_ref.at[pl.ds(pl.multiple_of(core * 448 + row, 16), 48), pl.ds(1152, 384)]
        for j, src in enumerate((mine, got_ref.at[pl.ds(row, 48)])):
            cols = pl.ds(pl.multiple_of((core if j == 0 else 1 - core) * 384, 128), 384)
            loads.append(pltpu.make_async_copy(src, wo_ref.at[at, cols], sems.at[2 * i + j]))

    @pl.when(first)
    def _():
        for c in loads:
            c.start()

    fill_mask(mask_ref, kseg_ref, qseg_ref)

    def pair(j, _):
        both = pl.ds(pl.multiple_of(128 * j, 128), 128)
        q2 = q_ref[:, 0, :, both].reshape(2 * BAND, 128)

        def score(c, tops):
            rows = pl.ds(pl.multiple_of(256 * c, 256), 256)
            k2 = k_ref[pl.ds(2 * c, 2), 0, :, both].reshape(256, 128)
            new = []
            for h in range(2):
                cols = slice(64 * h, 64 * h + 64)
                s = dot_nt(k2[:, cols], q2[:, cols]) + mask_ref[rows]
                score_ref[h, rows] = s
                new.append(jnp.maximum(tops[h], jnp.max(s, axis=0, keepdims=True)))
            return tuple(new)

        tops = lax.fori_loop(0, 4, score, (jnp.full((1, 256), -1e30, F32),) * 2, unroll=True)

        def weigh(c, totals):
            rows = pl.ds(pl.multiple_of(256 * c, 256), 256)
            new = []
            for h in range(2):
                e = jnp.exp(score_ref[h, rows] - tops[h])
                weight_ref[h, rows] = e.astype(BF16)
                new.append(totals[h] + jnp.sum(e, axis=0, keepdims=True))
            return tuple(new)

        totals = lax.fori_loop(0, 4, weigh, (jnp.zeros((1, 256), F32),) * 2, unroll=True)
        v2 = v_ref[:, 0, :, both].reshape(8 * BAND, 128)
        for h in range(2):
            mixed = dot_tn(v2[:, 64 * h : 64 * h + 64], weight_ref[h]) * (1.0 / totals[h])
            rows = pl.ds(pl.multiple_of(128 * j + 64 * h, 64), 64)
            mix_ref[0, rows] = mixed
            low_ref[0, rows] = mixed.astype(BF16)
            lse_ref[0, pl.ds(2 * j + h, 1)] = tops[h] + jnp.log(totals[h])
        return 0

    lax.fori_loop(0, 3, pair, 0)

    @pl.when(first)
    def _():
        for c in loads:
            c.wait()

    out_ref[:, 0] = dot_tn(low_ref[0], wo_ref[...]).astype(BF16).reshape(2, BAND, 768)


def norm(z):
    mean = jnp.mean(z, axis=-1, keepdims=True)
    centered = z - mean
    rstd = lax.rsqrt(jnp.mean(centered * centered, axis=-1, keepdims=True) + 1e-05)
    return (centered * rstd, rstd)


def norm_grad(grad, normed, rstd, gain):
    scaled = grad * gain
    return rstd * (
        scaled
        - jnp.mean(scaled, axis=-1, keepdims=True)
        - normed * jnp.mean(scaled * normed, axis=-1, keepdims=True)
    )


def forward_kernel(*refs):
    x_ref, own_ref, other_ref, vec_ref, b1_ref = refs[0:5]
    n1_out, r1_ref, low_out, act_out, slope_out, f_ref, w1_out, w2_out = refs[13:21]
    n1_ref, low_ref, act_ref, slope_ref, w1_ref, w2_ref, tok_buf, own_buf, other_buf, sems = refs[21:]
    results = ((n1_ref, n1_out), (low_ref, low_out), (w1_ref, w1_out), (act_ref, act_out), (slope_ref, slope_out), (w2_ref, w2_out))
    stores = [pltpu.make_async_copy(src, dst, sems.at[51 + i]) for i, (src, dst) in enumerate(results)]
    loads1, loads2 = placed_hidden(refs[5:13], (w1_ref, w2_ref), sems)
    early = [
        pltpu.make_async_copy(src, dst, sems.at[48 + i])
        for i, (src, dst) in enumerate(
            ((x_ref.at[pl.ds(0, 2)], tok_buf), (own_ref, own_buf), (other_ref, other_buf))
        )
    ]
    for c in early + loads1 + loads2:
        c.start()
    for c in early:
        c.wait()
    bo, g1, s1 = vec_ref[2:3], vec_ref[3:4], vec_ref[4:5]

    def rows(i, _):
        r = pl.ds(i * 128, 128)
        c, m = i // 2, i % 2
        z = tok_buf[c, m].astype(F32) + (own_buf[c, m].astype(F32) + other_buf[1 - c, m].astype(F32)) + bo
        n, rstd = norm(z)
        n1_ref[r] = n
        r1_ref[r] = rstd
        low_ref[r] = (n * g1 + s1).astype(BF16)
        return 0

    lax.fori_loop(0, 4, rows, 0)
    for c in loads1:
        c.wait()
    for c in stores[:3]:
        c.start()

    def inner(j, _):
        cols = pl.ds(pl.multiple_of(j * 256, 256), 256)
        u = dot_nn(low_ref[...], w1_ref[:, cols]) + b1_ref[:, cols]
        cdf = 0.5 * (1.0 + lax.erf(u * (1.0 / math.sqrt(2.0))))
        act_ref[:, cols] = (u * cdf).astype(BF16)
        slope = cdf + u * (jnp.exp(-0.5 * u * u) * (1.0 / math.sqrt(2.0 * math.pi)))
        slope_ref[:, cols] = slope.astype(BF16)
        return 0

    lax.fori_loop(0, 6, inner, 0)
    for c in loads2:
        c.wait()
    for c in stores[3:]:
        c.start()

    def outer(j, _):
        cols = pl.ds(pl.multiple_of(j * 256, 256), 256)
        f_ref[:, cols] = dot_nn(act_ref[...], w2_ref[:, cols]).astype(BF16)
        return 0

    lax.fori_loop(0, 3, outer, 0)
    for c in stores:
        c.wait()


def middle_kernel(
    n1_ref, own_ref, other_ref, cot_ref, theirs_ref, vec_ref, out_ref, df_ref, dz_ref, sums_ref, pcot_ref, sem,
):
    load = pltpu.make_async_copy(theirs_ref.at[3], pcot_ref, sem)
    load.start()
    g1, s1, b2, g2, s2 = (vec_ref[i : i + 1] for i in (3, 4, 5, 6, 7))

    def rows(i, which):
        ref, base = which
        r, o = pl.ds(base + i * 128, 128), pl.ds(256 - base + i * 128, 128)
        z = n1_ref[r] * g1 + s1 + (own_ref[r].astype(F32) + other_ref[o].astype(F32)) + b2
        n, rstd = norm(z)
        grad = ref[i].astype(F32)
        dz = norm_grad(grad, n, rstd, g2)
        dz_ref[r] = dz
        df_ref[r] = dz.astype(BF16)
        return (r, n, grad, dz)

    sums_ref[...] = jnp.zeros_like(sums_ref)

    def own_rows(i, _):
        r, n, grad, dz = rows(i, (cot_ref, 0))
        out_ref[r] = (n * g2 + s2).astype(BF16)
        sums_ref[0:1] += jnp.sum(grad * n, axis=0, keepdims=True)
        sums_ref[1:2] += jnp.sum(grad, axis=0, keepdims=True)
        sums_ref[2:3] += jnp.sum(dz.astype(BF16).astype(F32), axis=0, keepdims=True)
        return 0

    def other_rows(i, _):
        rows(i, (pcot_ref, 256))
        return 0

    lax.fori_loop(0, 2, own_rows, 0)
    load.wait()
    lax.fori_loop(0, 2, other_rows, 0)


def hidden_kernel(df_ref, slope_ref, w1_in, w2_ref, du_out, dh_ref, db1_ref, w1_ref, du_ref, sems):
    load = pltpu.make_async_copy(w1_in, w1_ref, sems.at[0])
    store = pltpu.make_async_copy(du_ref, du_out, sems.at[1])
    load.start()

    def hidden(j, _):
        cols = pl.ds(pl.multiple_of(j * 256, 256), 256)
        du = (dot_nt(df_ref[...], w2_ref[cols, :]) * slope_ref[:, cols].astype(F32)).astype(BF16)
        du_ref[:, cols] = du
        db1_ref[:, cols] = jnp.sum(du.astype(F32), axis=0, keepdims=True)
        return 0

    lax.fori_loop(0, 6, hidden, 0)
    store.start()
    load.wait()

    def back(j, _):
        cols = pl.ds(pl.multiple_of(j * 256, 256), 256)
        dh_ref[:, cols] = dot_nt(du_ref[...], w1_ref[cols, :]).astype(BF16)
        return 0

    lax.fori_loop(0, 3, back, 0)
    store.wait()


def first_kernel(
    dz_ref, own_ref, other_ref, n1_ref, r1_ref, vec_ref, wo_ref, dz1_ref, do_ref, half_ref, da_ref, sums_ref,
):
    g1 = vec_ref[3:4]
    core = my_core()
    sums_ref[...] = jnp.zeros_like(sums_ref)

    def rows(i):
        r, o = pl.ds(i * 128, 128), pl.ds((i ^ 2) * 128, 128)
        grad = dz_ref[r] + (own_ref[r].astype(F32) + other_ref[o].astype(F32))
        n = n1_ref[r]
        dz = norm_grad(grad, n, r1_ref[r], g1)
        low = dz.astype(BF16)
        do_ref[r] = low
        half_ref[r] = jnp.where(core == 0, low[:, :384], low[:, 384:])
        return (r, n, grad, dz, low)

    def own_rows(i, _):
        r, n, grad, dz, low = rows(i)
        dz1_ref[r] = dz
        sums_ref[0:1] += jnp.sum(grad * n, axis=0, keepdims=True)
        sums_ref[1:2] += jnp.sum(grad, axis=0, keepdims=True)
        sums_ref[2:3] += jnp.sum(low.astype(F32), axis=0, keepdims=True)
        return 0

    def other_rows(i, _):
        rows(i)
        return 0

    lax.fori_loop(0, 2, own_rows, 0)
    lax.fori_loop(2, 4, other_rows, 0)
    for m in range(2):
        for c in range(2):
            part = do_ref[pl.ds((c * 2 + m) * BAND, BAND), :]
            da_ref[m, :, c * BAND : (c + 1) * BAND] = dot_nt(wo_ref[...], part).astype(BF16)


def attend_back_kernel(
    q_ref, k_ref, v_ref, mix_ref, da_ref, lse_ref, kseg_ref, qseg_ref, w_in, dq_ref, dkv_ref, own_ref, send_ref, sums_ref,
    mask_ref, w_ref, sem,
):
    load = pltpu.make_async_copy(w_in, w_ref, sem)
    load.start()
    fill_mask(mask_ref, kseg_ref, qseg_ref)

    def pair(j, _):
        both = pl.ds(pl.multiple_of(128 * j, 128), 128)
        q2 = q_ref[:, 0, :, both].reshape(2 * BAND, 128)
        das, deltas, lses = [], [], []
        for h in range(2):
            rows = pl.ds(pl.multiple_of(128 * j + 64 * h, 64), 64)
            das.append(da_ref[0, rows])
            deltas.append(jnp.sum(das[h].astype(F32) * mix_ref[0, rows], axis=0, keepdims=True))
            lses.append(lse_ref[0, pl.ds(2 * j + h, 1)])
        k2 = k_ref[:, 0, :, both].reshape(8 * BAND, 128)
        v2 = v_ref[:, 0, :, both].reshape(8 * BAND, 128)
        dks, dvs, dqs = [], [], []
        for h in range(2):
            cols = slice(64 * h, 64 * h + 64)
            k, v, qh, da = k2[:, cols], v2[:, cols], q2[:, cols], das[h]
            p = jnp.exp(dot_nt(k, qh) + mask_ref[...] - lses[h])
            ds = (p * (dot_nn(v, da) - deltas[h])).astype(BF16)
            dvs.append(dot_nt(p.astype(BF16), da))
            dks.append(dot_nn(ds, qh))
            dqs.append(dot_tn(k, ds))
        later = pl.ds(pl.multiple_of(384 + 128 * j, 128), 128)
        dkv_ref[:, :, both] = jnp.concatenate(dks, axis=1).astype(BF16).reshape(8, BAND, 128)
        dkv_ref[:, :, later] = jnp.concatenate(dvs, axis=1).astype(BF16).reshape(8, BAND, 128)
        dq = jnp.transpose(jnp.concatenate(dqs, axis=0) * 0.125)
        dq_ref[:, :, both] = dq.astype(BF16).reshape(2, BAND, 128)
        return 0

    lax.fori_loop(0, 3, pair, 0)

    load.wait()
    sums_ref[0:1] = jnp.sum(dq_ref[...].reshape(2 * BAND, 384).astype(F32), axis=0, keepdims=True)
    sums_ref[1:2] = jnp.sum(dkv_ref[:, :, 384:].reshape(8 * BAND, 384).astype(F32), axis=0, keepdims=True)

    def step(i, _):
        dx = dot_nt(dkv_ref[pl.ds(4 * i, 4)].reshape(4 * BAND, 768), w_ref[:, 384:1152])
        for z in range(2):
            own_ref[2 * i + z] = dx[2 * z * BAND : (2 * z + 1) * BAND].astype(BF16)
            send_ref[2 * i + z] = dx[(2 * z + 1) * BAND : (2 * z + 2) * BAND].astype(BF16)
        return 0

    lax.fori_loop(0, 2, step, 0)
    dx = dot_nt(dq_ref[...].reshape(2 * BAND, 384), w_ref[:, 0:384])
    own_ref[0] = (own_ref[0].astype(F32) + dx[:BAND]).astype(BF16)
    send_ref[0] = (send_ref[0].astype(F32) + dx[BAND:]).astype(BF16)


def inner_grad_kernel(low_ref, du_ref, out_ref):
    me = my_chip() % 4

    def step(j, _):
        cols = pl.ds(pl.multiple_of(j * 384, 384), 384)
        value = dot_tn(low_ref[:, cols], du_ref[...]).astype(BF16)
        for i in range(8):
            rows = pl.ds(pl.multiple_of((j * 8 + (i ^ me)) * 48, 16), 48)
            out_ref[rows, :] = value[48 * i : 48 * i + 48]
        return 0

    lax.fori_loop(0, 2, step, 0)


def stored_at(block):
    p = block ^ my_chip()
    y, x, z = p // 8, (p // 4) % 2, p % 4
    return ((y, x * 4 + z), (x, y * 4 + z))


def place_rows(halves, block, first, second):
    for ref, (away, row), value in zip(halves, stored_at(block), (first, second)):
        ref[away, pl.ds(pl.multiple_of(row * 48, 16), 48)] = value


def flush(halves, outs, sems):
    copies = [
        pltpu.make_async_copy(halves[i // 2].at[i % 2], out.at[pl.ds(0, 384)], sems.at[i])
        for i, out in enumerate(outs)
    ]
    return copies


def finish(copies):
    for c in copies:
        c.start()
    for c in copies:
        c.wait()


def outer_grad_kernel(act_ref, df_ref, *refs):
    outs, halves, sems = refs[:4], refs[4:6], refs[6]

    def step(j, _):
        cols = pl.ds(pl.multiple_of(j * 384, 384), 384)
        value = dot_tn(act_ref[:, cols], df_ref[...]).astype(BF16)
        for i in range(4):
            place_rows(halves, j * 4 + i, value[96 * i : 96 * i + 48], value[96 * i + 48 : 96 * i + 96])
        return 0

    lax.fori_loop(0, 4, step, 0)
    finish(flush(halves, outs, sems))


def projection_grad_kernel(x_ref, *refs):
    dqs, dkvs, (mix0, mix1, other_ref, half_ref, vec_ref) = refs[0:2], refs[2:4], refs[4:9]
    refs = refs[9:]
    outs, halves, dwo_ref, sems = refs[:4], refs[4:6], refs[6], refs[7]
    core = my_core()
    half = half_ref[...].reshape(2, 2, BAND, 384)
    own = [half[:, m].reshape(2 * BAND, 384) for m in range(2)]
    dwo = dot_nn(mix0[...], own[0]) + dot_nn(mix1[...], own[1])
    dwo_ref[pl.ds(pl.multiple_of(core * 384, 384), 384)] = dwo.astype(BF16)
    other = [jnp.concatenate([half[1, m], half[0, m]], axis=0) for m in range(2)]
    dwo = dot_nn(other_ref[0], other[0]) + dot_nn(other_ref[1], other[1])
    dwo_ref[pl.ds(pl.multiple_of((1 - core) * 384, 384), 384)] = dwo.astype(BF16)

    def step(j, _):
        cols = pl.ds(pl.multiple_of(j * 384, 384), 384)
        x = [x_ref[:, m, :, cols].reshape(8 * BAND, 384) for m in range(2)]

        def total(refs, count):
            terms = [dot_tn(x[m][: count * BAND], refs[m][...].reshape(count * BAND, -1)) for m in range(2)]
            return (terms[0] + terms[1]).astype(BF16)

        dwq, dwkv = total(dqs, 2), total(dkvs, 8)
        for i in range(8):
            rows = slice(48 * i, 48 * i + 48)
            dwo = dwo_ref[pl.ds(pl.multiple_of(j * 384 + 48 * i, 16), 48)]
            place_rows(
                halves,
                j * 8 + i,
                jnp.concatenate([dwq[rows], dwkv[rows, :384]], axis=1),
                jnp.concatenate([dwkv[rows, 384:], dwo], axis=1),
            )
        return 0

    lax.fori_loop(0, 2, step, 0)
    copies = flush(halves, outs, sems)
    for i, out in enumerate(outs):
        copies.append(pltpu.make_async_copy(vec_ref.at[i], out.at[pl.ds(384, 64)], sems.at[4 + i]))
    finish(copies)


def add(*terms):
    total = terms[0].astype(F32)
    for t in terms[1:]:
        total = total + t.astype(F32)
    return total


def first_hop(terms):
    return (terms[0], send(terms[1], Y), terms[2], send(terms[3], X))


def halves_of(g, near, rows):
    return jnp.concatenate(
        [g[192 * near : 192 * near + 192]] + ([g[384 + 32 * near : 416 + 32 * near]] if rows > 48 else [])
    )


def near_terms(hop, rows):
    return tuple(
        add(halves_of(hop[i], 1, rows), halves_of(hop[i + 1], 1, rows)).astype(BF16) for i in (0, 2)
    )


def hop_terms(low):
    return (send(low[0], X), send(low[1], Y))


def far_terms(hop, got, rows):
    return tuple(
        add(halves_of(hop[i], 0, rows), halves_of(hop[i + 1], 0, rows), got[i // 2]).astype(BF16) for i in (0, 2)
    )


def along_line(blocks):
    return (blocks[0], send(blocks[1], Z1), send(blocks[2], Z2), send(blocks[3], Z3))


def line_parts(halves, rows):
    return along_line(
        [
            jnp.concatenate(
                [
                    jnp.concatenate(
                        [h[48 * z : 48 * z + 48]] + ([h[192 + 8 * z : 200 + 8 * z]] if rows > 48 else []), axis=0
                    )
                    for h in halves
                ],
                axis=1,
            )
            for z in range(4)
        ]
    )


def block_parts(block):
    return along_line([block[48 * z : 48 * z + 48] for z in range(4)])


def flip(values, axis, index, bits):
    for bit in range(bits):
        shape = values.shape
        n = shape[axis]
        split = shape[:axis] + (n >> (bit + 1), 2, 1 << bit) + shape[axis + 1 :]
        swapped = jnp.flip(values.reshape(split), axis + 1).reshape(shape)
        values = jnp.where((index >> bit) & 1 == 1, swapped, values)
    return values


def per_device_paired(
    inputs, segments, w_query, b_query, w_key, w_value, b_value, w_output, b_output, gain_first,
    shift_first, w_inner, b_inner, w_outer, b_outer, gain_second, shift_second, cotangent,
):
    seq = lax.axis_index("seq")
    me, core = my_chip(), my_core()
    even = core == 0

    def in_order(mine, got, axis):
        return jnp.where(even, jnp.concatenate([mine, got], axis), jnp.concatenate([got, mine], axis))

    lanes = [b_query, b_value, b_output, gain_first, shift_first, b_outer, gain_second, shift_second, b_inner]
    mine, theirs, outer_rows = call(
        prepare_kernel, [((32, 1536), BF16), ((32, 1536), BF16), ((48, 1536), BF16)], 14
    )(w_query, w_key, w_value, w_output, *(v.reshape(1, -1) for v in lanes), w_outer)
    (square,) = call(chip_rows_kernel, [((56, 1536), BF16)], 2)(mine, send(theirs, CORE))
    wide = after(w_inner, mine).astype(BF16).reshape(24, CHIPS, 2, 96)
    mine, theirs = (
        jnp.where(even, wide[:, :, 0], wide[:, :, 1]).reshape(24, 1536),
        jnp.where(even, wide[:, :, 1], wide[:, :, 0]).reshape(24, 1536),
    )
    inner_rows = in_order(mine, send(theirs, CORE), 0)
    tokens, cot = inputs[:, 0], cotangent[:, 0]
    segs = segments[:, 0]
    segs = flip(segs.reshape(2, 8, BAND), 1, seq, 3)
    kseg = segs.reshape(2, 8 * BAND, 1)
    qseg = segs[:, :2].reshape(2, 1, 2 * BAND)

    other_tokens = send(tokens, CORE)
    hidden_rows = jnp.concatenate([inner_rows, outer_rows], axis=1)
    square, hidden_rows, other_tokens = after_both((square, hidden_rows, other_tokens), ())
    square = line(square)
    square = jnp.concatenate([p[:48] for p in square] + [p[48:] for p in square], axis=0)
    square, hidden_rows = after_both((square, hidden_rows), ())
    square = lines(square)
    hidden = line(hidden_rows)
    hidden, tokens = after_both((hidden, tokens), (kseg, qseg))
    hidden = [jnp.concatenate([h[:, c : c + 1536] for h in hidden], axis=0) for c in (0, 1536)]
    places = jnp.arange(CHIPS)
    order = ((places[:, None] ^ me) == places[None, :]).astype(BF16)
    line_order = ((places[:, None] ^ (me % 4)) == places[None, :]).astype(BF16)
    vecs = square.reshape(4, 224, 1536)[:, 192:].reshape(CHIPS, 8, 1536)[:, :2].reshape(CHIPS, 2 * 1536)
    vecs = dot_nn(line_order, vecs).reshape(CHIPS, 2, 12, 128)
    vec8 = vecs[:, :, :8, :24].transpose(2, 0, 1, 3).reshape(8, 768)
    b1 = jnp.where(even, vecs[:, 0, 8, :96], vecs[:, 1, 8, :96]).reshape(1, 1536)
    bq = jnp.where(even, vec8[0:1, :384], vec8[0:1, 384:])
    bv = jnp.where(even, vec8[1:2, :384], vec8[1:2, 384:])

    wo_rows = square[:, 1152:]
    wo_got = send(jnp.where(even, wo_rows[448:], wo_rows[:448]), CORE)

    near = x_then_y(*hidden)
    beside, second, opposite = send(tokens, Z1), send(tokens, Z2), send(tokens, MIDDLE)
    theirs = send(jnp.stack(after_both((beside, second, opposite, cot), (near, vec8, b1, bq, bv, wo_got))), CORE)
    slots = [tokens, other_tokens, beside, second, opposite, theirs]
    far = y_then_x(*hidden)

    slot_shape, head_shape = (2, BAND, 768), (2, BAND, 384)
    q, k, v, w_abs, x_all = call(
        project_kernel,
        [((2, *head_shape), BF16), ((8, *head_shape), BF16), ((8, *head_shape), BF16), ((768, 1536), BF16), ((8, *slot_shape), BF16)],
        9,
        in_specs=[IN_PLACE] * 7 + [IN_VMEM] * 2,
        out_specs=[IN_VMEM] + [IN_PLACE] * 4,
        scratch=[
            pltpu.VMEM((8, *head_shape), BF16),
            pltpu.VMEM((8, *head_shape), BF16),
            pltpu.VMEM((768, 1536), BF16),
            pltpu.VMEM((8, *slot_shape), BF16),
            pltpu.SemaphoreType.DMA((46,)),
        ],
        cost=(2_800_000_000, 16_000_000),
    )(*slots, square, bq, bv)
    def attention_specs(m=None):
        micro = (lambda i: i) if m is None else (lambda i: m)
        q_spec = pl.BlockSpec((2, 1, BAND, 384), lambda i: (0, micro(i), 0, 0))
        k_spec = pl.BlockSpec((8, 1, BAND, 384), lambda i: (0, micro(i), 0, 0))
        t_spec = pl.BlockSpec((1, 384, 2 * BAND), lambda i: (micro(i), 0, 0))
        lse_spec = pl.BlockSpec((1, 8, 2 * BAND), lambda i: (micro(i), 0, 0))
        segs = [
            pl.BlockSpec((1, 8 * BAND, 1), lambda i: (micro(i), 0, 0)),
            pl.BlockSpec((1, 1, 2 * BAND), lambda i: (micro(i), 0, 0)),
        ]
        return ([q_spec, k_spec, k_spec], [t_spec, t_spec, lse_spec], segs)

    qkv_specs, mix_specs, seg_specs = attention_specs()
    near, (q, k, v) = after_both((near, (q, k, v)), far)
    both = y_then_x(*near)
    mix, mix_low, lse, branch, wo = call(
        attend_kernel,
        [((2, 384, 256), F32), ((2, 384, 256), BF16), ((2, 8, 256), F32), ((2, *slot_shape), BF16), ((384, 768), BF16)],
        7,
        grid=(2,),
        in_specs=qkv_specs + seg_specs + [IN_PLACE] * 2,
        out_specs=[
            *mix_specs,
            pl.BlockSpec((2, 1, BAND, 768), lambda i: (0, i, 0, 0)),
            pl.BlockSpec((384, 768), lambda i: (0, 0)),
        ],
        scratch=[
            pltpu.VMEM((1024, 256), F32),
            pltpu.VMEM((2, 1024, 256), F32),
            pltpu.VMEM((2, 1024, 256), BF16),
            pltpu.SemaphoreType.DMA((16,)),
        ],
        cost=(1_900_000_000, 10_000_000),
    )(q, k, v, kseg, qseg, square, wo_got)
    branch, both = after_both((branch, both), ())
    hidden = [g[i] for i in range(2) for g in (hidden, near, far, both)]
    branch_other = send(branch, CORE)
    n1, r1, hid_low, act, slope, f_own, w1, w2 = call(
        forward_kernel,
        [((512, 768), F32), ((512, 1), F32), ((512, 768), BF16), ((512, 1536), BF16), ((512, 1536), BF16), ((512, 768), BF16), ((768, 1536), BF16), ((1536, 768), BF16)],
        13,
        in_specs=[IN_PLACE] * 3 + [IN_VMEM] * 2 + [IN_PLACE] * 8,
        out_specs=[IN_PLACE, IN_VMEM, IN_PLACE, IN_PLACE, IN_PLACE, IN_VMEM, IN_PLACE, IN_PLACE],
        scratch=[
            pltpu.VMEM((512, 768), F32),
            pltpu.VMEM((512, 768), BF16),
            pltpu.VMEM((512, 1536), BF16),
            pltpu.VMEM((512, 1536), BF16),
            pltpu.VMEM((768, 1536), BF16),
            pltpu.VMEM((1536, 768), BF16),
            *([pltpu.VMEM((2, *slot_shape), BF16)] * 3),
            pltpu.SemaphoreType.DMA((57,)),
        ],
        cost=(2_500_000_000, 16_000_000),
    )(x_all, branch, branch_other, vec8, b1, *hidden)
    mix_other = send(after(mix_low, n1), CORE)
    result, df, dz2, sums2 = call(
        middle_kernel,
        [((256, 768), BF16), ((512, 768), BF16), ((512, 768), F32), ((8, 768), F32)],
        6,
        in_specs=[IN_VMEM] * 4 + [IN_PLACE, IN_VMEM],
        scratch=[pltpu.VMEM(slot_shape, BF16), pltpu.SemaphoreType.DMA],
        cost=(50_000_000, 8_000_000),
    )(n1, f_own, send(f_own, CORE), cot, theirs, vec8)

    piece = [pltpu.VMEM((2, 384, 768), BF16)] * 2
    outer_terms = call(
        outer_grad_kernel,
        [((384, 768), BF16)] * 4,
        2,
        out_specs=[IN_PLACE] * 4,
        scratch=piece + [pltpu.SemaphoreType.DMA((4,))],
        cost=(1_200_000_000, 6_000_000),
    )(act, df)
    outer_hop = first_hop(outer_terms)
    du, dh_own, db1 = call(
        hidden_kernel,
        [((512, 1536), BF16), ((512, 768), BF16), ((1, 1536), F32)],
        4,
        in_specs=[IN_VMEM, IN_VMEM, IN_PLACE, IN_VMEM],
        out_specs=[IN_PLACE, IN_VMEM, IN_VMEM],
        scratch=[pltpu.VMEM((768, 1536), BF16), pltpu.VMEM((512, 1536), BF16), pltpu.SemaphoreType.DMA((2,))],
        cost=(2_400_000_000, 9_000_000),
    )(after(df, *outer_terms), slope, w1, w2)
    dh_other = send(dh_own, CORE)
    (inner_terms,) = call(inner_grad_kernel, [((768, 1536), BF16)], 2, cost=(1_200_000_000, 6_000_000))(hid_low, du)
    inner_block = lax.psum_scatter(inner_terms, "dp", scatter_dimension=0, tiled=True)
    outer_hop = after_both(outer_hop, (inner_terms,))
    outer_low = near_terms(outer_hop, 48)
    dh_own = after(dh_own, inner_terms)
    outer_sent = hop_terms(outer_low)
    dz1, do, do_half, da, sums1 = call(
        first_kernel,
        [((256, 768), F32), ((512, 768), BF16), ((512, 384), BF16), ((2, 384, 256), BF16), ((8, 768), F32)],
        7,
        cost=(300_000_000, 10_000_000),
    )(dz2, dh_own, dh_other, n1, r1, vec8, wo)

    def back(m, events):
        specs = attention_specs(m)
        shapes = [(2, BAND, 384), (8, BAND, 768), (4, BAND, 768), (4, BAND, 768)]
        return call(
            attend_back_kernel,
            [(shape, BF16) for shape in shapes] + [((8, 384), F32)],
            9,
            grid=(1,),
            in_specs=specs[0] + specs[1] + specs[2] + [IN_PLACE],
            out_specs=[pl.BlockSpec(shape, lambda i: (0, 0, 0)) for shape in shapes] + [pl.BlockSpec((8, 384), lambda i: (0, 0))],
            scratch=[pltpu.VMEM((1024, 256), F32), pltpu.VMEM((768, 1536), BF16), pltpu.SemaphoreType.DMA],
            cost=(3_400_000_000, 10_000_000),
        )(q, k, v, mix, after(da, *events), lse, kseg, qseg, w_abs)

    def core_sums(own, got):
        return [add(own[z], got[z]) if z == 0 else add(own[z], got[z]).astype(BF16) for z in range(4)]

    def line_sums(sums):
        return (sums[0], send(sums[1], Z1), send(sums[2], Z2), send(sums[3], MIDDLE))

    outer_hop, outer_sent = after_both((outer_hop, outer_sent), (da,))
    outer_half = far_terms(outer_hop, outer_sent, 48)
    *grads0, dx0, dx_send, sums_q0 = back(0, ())
    got0 = send(dx_send, CORE)
    outer_half = after_both(outer_half, grads0[:1])
    outer_parts = line_parts(outer_half, 48)
    *grads1, dx1, dx_send, sums_q1 = back(1, (dx0, *outer_half))
    outer_parts = after_both(outer_parts, grads1[:1])
    got1 = send(dx_send, CORE)
    grads1, _ = lax.optimization_barrier((grads1, (outer_parts, inner_block)))
    inner_parts = block_parts(inner_block)

    def widen(value):
        zero = jnp.zeros_like(value)
        return in_order(value, zero, 1)

    sums_q = sums_q0 + sums_q1
    eight = jnp.concatenate(
        [widen(sums_q[0:1]), widen(sums_q[1:2]), sums1[2:3], sums1[0:1], sums1[1:2], sums2[2:3], sums2[0:1], sums2[1:2]], 0
    )
    eight = jnp.pad(eight.reshape(8, CHIPS, 2, 24), ((0, 0), (0, 0), (0, 0), (0, 104))).transpose(1, 2, 0, 3)
    db1 = jnp.where(jnp.arange(2)[None, :, None] == core, db1.reshape(CHIPS, 1, 96), 0.0)
    db1 = jnp.pad(db1, ((0, 0), (0, 0), (0, 416)))
    vec_grads = jnp.concatenate([eight.reshape(CHIPS, 2, 1024), db1], axis=2).reshape(CHIPS, 3072)
    vec_grads = dot_nn(order, vec_grads.astype(BF16)).astype(BF16).reshape(2, 2, 4, 2, 1536)
    vec_grads = jnp.pad(vec_grads, ((0, 0), (0, 0), (0, 0), (0, 6), (0, 0)))
    vec_first = vec_grads[..., :768].reshape(2, 64, 768)
    vec_second = vec_grads[..., 768:].transpose(1, 0, 2, 3, 4).reshape(2, 64, 768)
    square_terms = call(
        projection_grad_kernel,
        [((448, 768), BF16)] * 4,
        10,
        out_specs=[IN_PLACE] * 4,
        scratch=piece + [pltpu.VMEM((768, 384), BF16), pltpu.SemaphoreType.DMA((8,))],
        cost=(3_300_000_000, 12_000_000),
    )(x_all, grads0[0], grads1[0], grads0[1], grads1[1], mix_low[0], mix_low[1], mix_other, do_half, jnp.concatenate([vec_first, vec_second]))
    square_hop = first_hop(square_terms)
    inner_parts, got0, got1 = after_both((inner_parts, got0, got1), square_terms)
    sent0 = line_sums(core_sums(dx0, got0))
    sent1 = line_sums(core_sums(dx1, got1))
    square_hop, sent0 = after_both((square_hop, sent0), ())
    square_sent = hop_terms(near_terms(square_hop, 56))
    square_half = far_terms(square_hop, square_sent, 56)
    square_parts = line_parts(square_half, 56)

    outer_total = add(*outer_parts)
    inner_total = add(*inner_parts)
    grad_outer = jnp.concatenate([outer_total[:, :768], outer_total[:, 768:]], axis=0)
    keep = jnp.where(even, inner_total[:24], inner_total[24:])
    got = send(jnp.where(even, inner_total[24:], inner_total[:24]).astype(BF16), CORE).astype(F32)
    grad_inner = in_order(keep.reshape(24, CHIPS, 1, 96), got.reshape(24, CHIPS, 1, 96), 2).reshape(24, 3072)
    keep, other = call(owner_kernel, [((32, 1536), F32), ((32, 1536), BF16)], 5)(*square_half, *square_parts[1:])
    grads = call(
        result_kernel,
        [((24, 768), F32)] * 4 + [((1, 24), F32)] * 8 + [((1, 96), F32)],
        2,
    )(keep, send(other, CORE))
    squares, small = grads[:4], [g.reshape(-1) for g in grads[4:]]
    dz1 = dz1.reshape(slot_shape)
    dz1 = dz1.reshape(2, BAND, 768)
    grad_tokens = jnp.stack([add(dz1[m], *sent).astype(BF16) for m, sent in enumerate((sent0, sent1))])
    return (
        result.reshape(2, 1, BAND, 768), grad_tokens[:, None],
        squares[0], small[0], squares[1], squares[2], small[1], squares[3], small[2],
        small[3], small[4], grad_inner, small[8], grad_outer, small[5], small[6], small[7],
    )


def solution(mesh):
    in_specs = (
        P(None, "dp", "seq", None),
        P(None, "dp", None),
        P(("dp", "seq"), None),
        P(("dp", "seq")),
        P(("dp", "seq"), None),
        P(("dp", "seq"), None),
        P(("dp", "seq")),
        P(("dp", "seq"), None),
        P(("dp", "seq")),
        P(("dp", "seq")),
        P(("dp", "seq")),
        P(("dp", "seq"), None),
        P(("dp", "seq")),
        P(("dp", "seq"), None),
        P(("dp", "seq")),
        P(("dp", "seq")),
        P(("dp", "seq")),
        P(None, "dp", "seq", None),
    )
    out_specs = (
        P(None, "dp", "seq", None),
        P(None, "dp", "seq", None),
        P(("dp", "seq"), None),
        P(("dp", "seq")),
        P(("dp", "seq"), None),
        P(("dp", "seq"), None),
        P(("dp", "seq")),
        P(("dp", "seq"), None),
        P(("dp", "seq")),
        P(("dp", "seq")),
        P(("dp", "seq")),
        P(("dp", "seq"), None),
        P(("dp", "seq")),
        P(("dp", "seq"), None),
        P(("dp", "seq")),
        P(("dp", "seq")),
        P(("dp", "seq")),
    )
    paired = (mesh.shape["dp"], mesh.shape["seq"]) == (4, 8)
    return jax.shard_map(
        per_device_paired if paired else per_device, mesh=mesh, in_specs=in_specs, out_specs=out_specs, check_vma=False
    )
```
